512 devices in a mesh: head: 16 (over z_lo, x), seq: 32 (over y, z_hi, core).
Axes of the slice: x: 4, y: 8, z: 8 (z_hi: 2, z_lo: 4; z = z_hi * 4 + z_lo), core: 2. Of those that a mesh axis runs over, the one named last changes fastest.
Arguments:
- queries: bfloat16 [32, 2048, 4096], P('seq', 'head'), may hold values from -13 to 13
- keys: bfloat16 [32, 2048, 1024], P('seq', 'head'), may hold values from -8 to 8
- values: bfloat16 [32, 2048, 1024], P('seq', 'head'), may hold values from -6 to 6
- output_gradient: bfloat16 [32, 2048, 4096], P('seq', 'head'), may hold values from -6 to 6
- windows: int32 [32], replicated, may hold values from 1 to 4, as said below
- sinks: int32 [32], replicated, may hold values from 0 to 2, as said below
Outputs:
- grad_queries: bfloat16 [32, 2048, 4096], P('seq', 'head')
- key_gradient: bfloat16 [32, 2048, 1024], P('seq', 'head')
- value_gradient: bfloat16 [32, 2048, 1024], P('seq', 'head')
The draws below stay inside these ranges and needn't reach their ends.
Inputs may be any that keep to these rules, and one draw needn't show every extreme that they name: `windows`: some head has a window of exactly 4 blocks. `sinks`: some head has exactly 2 sink blocks.
All inputs are finite; a program needn't handle non-finite values.
Results may differ from the reference program's by a relative error of at most 0.009.
Values may be sent and summed in bfloat16 or wider, within the bound.
No kernel may reach another device: no remote copies, remote signals or barrier semaphores. Data moves between devices by JAX's collectives and lax.ppermute only.
A program may use at most 64 MiB of HBM per device.

```python
import math
import jax
import jax.numpy as jnp
from jax import lax

QUERY_HEADS = 32
KEY_VALUE_HEADS = 8
HEAD_DIMENSION = 128
BLOCK_TOKENS = 128
WMAX = 4
SMAX = 2
SPAN_COUNT = 32
SPAN_LENGTH = 2048


def build_keys(key):
    full_rows = SPAN_COUNT * SPAN_LENGTH
    starting_rows = jnp.clip(jax.random.normal(jax.random.fold_in(key, 11), (full_rows, KEY_VALUE_HEADS * HEAD_DIMENSION), jnp.float32), -6.0, 6.0)
    return starting_rows


def draw_keys(key, part):
    return build_keys(key).reshape(SPAN_COUNT, SPAN_LENGTH, KEY_VALUE_HEADS * HEAD_DIMENSION).astype(jnp.bfloat16)


def draw_queries(key, part):
    full_rows = SPAN_COUNT * SPAN_LENGTH
    drawn_rows = jnp.clip(jax.random.normal(jax.random.fold_in(key, 13), (full_rows, QUERY_HEADS * HEAD_DIMENSION), jnp.float32), -6.0, 6.0)
    return drawn_rows.reshape(SPAN_COUNT, SPAN_LENGTH, QUERY_HEADS * HEAD_DIMENSION).astype(jnp.bfloat16)


def draw_windows(key, part):
    raw_counts = jax.random.randint(jax.random.fold_in(key, 21), (QUERY_HEADS,), 1, WMAX + 1)
    picked = jax.random.randint(jax.random.fold_in(key, 22), (), 0, QUERY_HEADS)
    return jnp.where(jnp.arange(QUERY_HEADS) == picked, WMAX, raw_counts).astype(jnp.int32)


def draw_sinks(key, part):
    raw_counts = jax.random.randint(jax.random.fold_in(key, 31), (QUERY_HEADS,), 0, SMAX + 1)
    picked = jax.random.randint(jax.random.fold_in(key, 32), (), 0, QUERY_HEADS)
    return jnp.where(jnp.arange(QUERY_HEADS) == picked, SMAX, raw_counts).astype(jnp.int32)


def shard_levels(stream_key, shape, shards, smallest, largest):
    def one(dim, parts):
        draws = jax.random.uniform(jax.random.fold_in(jax.random.fold_in(stream_key, 6), dim), (parts,), jnp.float32, smallest / len(shards), largest / len(shards))
        return jnp.repeat(jnp.exp(draws), shape[dim] // parts).reshape((-1,) + (1,) * (len(shape) - dim - 1))

    factor_of = one(*shards[0])
    for cut in shards[1:]:
        factor_of = factor_of * one(*cut)
    return factor_of


def centred(rng, dims, width, reach, split=(), kind=jnp.bfloat16):
    values = jax.random.normal(rng, dims, jnp.float32) * width
    if len(split) > 0:
        values = shard_levels(rng, dims, split, -0.22, 0.18) * values
    return jnp.clip(values, min=-reach, max=reach).astype(kind)


def setup_inputs(seed: int = 0) -> dict:
    seeds = jax.random.split(jax.random.key(seed), 7)
    return {
        "queries": draw_queries(jax.random.fold_in(seeds[6], 71), 0),
        "keys": draw_keys(jax.random.fold_in(seeds[6], 71), 0),
        "values": centred(seeds[2], (SPAN_COUNT, SPAN_LENGTH, KEY_VALUE_HEADS * HEAD_DIMENSION), 1.0, 6.0, ((0, 32), (1, 16))),
        "output_gradient": centred(seeds[3], (SPAN_COUNT, SPAN_LENGTH, QUERY_HEADS * HEAD_DIMENSION), 1.0, 6.0, ((0, 32), (1, 16))),
        "windows": draw_windows(jax.random.fold_in(seeds[6], 71), 0),
        "sinks": draw_sinks(jax.random.fold_in(seeds[6], 71), 0),
    }


NEG_FILL = -1e+30

def mask_for(query_blocks, window, sink_count, block, wmax, smax):
    columns = jnp.arange((wmax + smax) * block, dtype=jnp.int32)
    slot_id = columns // block
    col_tok = columns % block
    row_tok = jnp.arange(block, dtype=jnp.int32)
    query_block = query_blocks.reshape((-1,) + (1,) * (window.ndim + 2))
    win_w = window[None, ..., None, None]
    sink_s = sink_count[None, ..., None, None]
    in_window = slot_id < wmax
    causal = (slot_id > 0) | (col_tok[None, :] <= row_tok[:, None])
    window_ok = in_window & (query_block - slot_id >= 0) & (slot_id < win_w) & causal
    sink_ok = jnp.logical_not(in_window) & (slot_id - wmax < sink_s) & (slot_id - wmax <= query_block - win_w)
    return window_ok | sink_ok

def slot_keys(padded, whole, block_count):
    windowed = jnp.stack([padded[WMAX - 1 - offset:WMAX - 1 - offset + block_count] for offset in range(WMAX)], 1)
    sunk = jnp.broadcast_to(whole[:SMAX][None], (block_count, SMAX, BLOCK_TOKENS, HEAD_DIMENSION))
    joined = jnp.concatenate([windowed, sunk], 1)
    return joined.reshape(block_count, (WMAX + SMAX) * BLOCK_TOKENS, HEAD_DIMENSION).astype(jnp.float32)

def fold_slots(slot_grads, block_count):
    parts_all = slot_grads.reshape(block_count, WMAX + SMAX, BLOCK_TOKENS, HEAD_DIMENSION)
    total = jnp.zeros((block_count + WMAX - 1, BLOCK_TOKENS, HEAD_DIMENSION), jnp.float32)
    for offset in range(WMAX):
        total = total.at[WMAX - 1 - offset:WMAX - 1 - offset + block_count].add(parts_all[:, offset])
    total = total[WMAX - 1:]
    return total.at[:SMAX].add(lax.optimization_barrier(jnp.sum(parts_all[:, WMAX:], 0)))

def head_grads(q_head, go_head, k_head, v_head, window, sink_count):
    block_count = q_head.shape[0]
    scale_factor = 1.0 / math.sqrt(HEAD_DIMENSION)
    zero_pad = jnp.zeros((WMAX - 1, BLOCK_TOKENS, HEAD_DIMENSION), k_head.dtype)
    key_collection = slot_keys(jnp.concatenate([zero_pad, k_head], 0), k_head, block_count)
    value_collection = slot_keys(jnp.concatenate([zero_pad, v_head], 0), v_head, block_count)
    allowed = mask_for(jnp.arange(block_count, dtype=jnp.int32), window, sink_count, BLOCK_TOKENS, WMAX, SMAX)
    query_wide = q_head.astype(jnp.float32)
    output_grad_wide = go_head.astype(jnp.float32)
    score_matrix = jnp.einsum('frx,fpx->frp', query_wide, key_collection) * scale_factor
    score_matrix = jnp.where(allowed, score_matrix, NEG_FILL)
    row_max = lax.optimization_barrier(jnp.max(score_matrix, -1, keepdims=True))
    exp_scores = jnp.exp(score_matrix - row_max)
    weights = exp_scores / lax.optimization_barrier(jnp.sum(exp_scores, -1, keepdims=True))
    block_weights = lax.optimization_barrier(weights.astype(jnp.bfloat16)).astype(jnp.float32)
    attention_output = jnp.einsum('eng,egv->env', block_weights, value_collection)
    row_dot = lax.optimization_barrier(jnp.sum(output_grad_wide * attention_output, -1, keepdims=True))
    weight_gradient = jnp.einsum('frx,fpx->frp', output_grad_wide, value_collection)
    score_block_grad = (weights * (weight_gradient - row_dot)).astype(jnp.bfloat16)
    score_block_grad = lax.optimization_barrier(score_block_grad).astype(jnp.float32)
    query_grad_result = jnp.einsum('eng,egv->env', score_block_grad, key_collection) * scale_factor
    key_grad_result = jnp.einsum('nze,nzp->nep', score_block_grad, query_wide) * scale_factor
    value_grad_result = jnp.einsum('nze,nzp->nep', block_weights, output_grad_wide)
    return (query_grad_result, fold_slots(key_grad_result, block_count), fold_slots(value_grad_result, block_count))

def reference(queries, keys, values, output_gradient, windows, sinks):
    block_count = SPAN_COUNT * SPAN_LENGTH // BLOCK_TOKENS
    group_width = QUERY_HEADS // KEY_VALUE_HEADS
    query_full = queries.reshape(block_count, BLOCK_TOKENS, KEY_VALUE_HEADS, group_width, HEAD_DIMENSION).transpose(2, 3, 0, 1, 4)
    output_grad_full = output_gradient.reshape(block_count, BLOCK_TOKENS, KEY_VALUE_HEADS, group_width, HEAD_DIMENSION).transpose(2, 3, 0, 1, 4)
    key_full = keys.reshape(block_count, BLOCK_TOKENS, KEY_VALUE_HEADS, HEAD_DIMENSION).transpose(2, 0, 1, 3)
    value_full = values.reshape(block_count, BLOCK_TOKENS, KEY_VALUE_HEADS, HEAD_DIMENSION).transpose(2, 0, 1, 3)
    window_lookup = windows.reshape(KEY_VALUE_HEADS, group_width)
    sink_lookup = sinks.reshape(KEY_VALUE_HEADS, group_width)

    def per_kv_head(head_items):
        q_grp, g_grp, k_head, v_head, win_grp, sink_grp = head_items

        def per_q_head(running, inner_items):
            q_head, go_head, window, sink_count = inner_items
            query_grad_result, key_grad_result, value_grad_result = head_grads(q_head, go_head, k_head, v_head, window, sink_count)
            return ((running[0] + key_grad_result, running[1] + value_grad_result), query_grad_result)
        zero_grads = jnp.zeros((block_count, BLOCK_TOKENS, HEAD_DIMENSION), jnp.float32)
        (key_grad_result, value_grad_result), query_grad_result = lax.scan(per_q_head, (zero_grads, zero_grads), (q_grp, g_grp, win_grp, sink_grp))
        return (query_grad_result, key_grad_result, value_grad_result)
    query_grad_result, key_grad_result, value_grad_result = lax.map(per_kv_head, (query_full, output_grad_full, key_full, value_full, window_lookup, sink_lookup))
    grad_queries = query_grad_result.transpose(2, 3, 0, 1, 4).reshape(SPAN_COUNT, SPAN_LENGTH, QUERY_HEADS * HEAD_DIMENSION).astype(jnp.bfloat16)
    key_gradient = key_grad_result.transpose(1, 2, 0, 3).reshape(SPAN_COUNT, SPAN_LENGTH, KEY_VALUE_HEADS * HEAD_DIMENSION).astype(jnp.bfloat16)
    value_gradient = value_grad_result.transpose(1, 2, 0, 3).reshape(SPAN_COUNT, SPAN_LENGTH, KEY_VALUE_HEADS * HEAD_DIMENSION).astype(jnp.bfloat16)
    return (grad_queries, key_gradient, value_gradient)
```

```python
import math

import jax
import jax.numpy as jnp
from jax import lax
from jax.experimental import pallas as pl
from jax.experimental.pallas import tpu as pltpu
from jax.sharding import Mesh, PartitionSpec as P

QUERY_HEADS = 32
KEY_VALUE_HEADS = 8
HEAD_DIMENSION = 128
BLOCK_TOKENS = 128
WMAX = 4
SMAX = 2
NEG_FILL = -1e30

AXES = ("zl", "x", "y", "zh", "core")
SIZES = (4, 4, 8, 2, 2)
LINE = ("zl", "y", "zh", "core")
RUNS = 128
ROW = 4
KV_LOCAL = KEY_VALUE_HEADS // ROW
GROUP = QUERY_HEADS // KEY_VALUE_HEADS
Q_LOCAL = KV_LOCAL * GROUP
TAIL = WMAX - 1
D = HEAD_DIMENSION
B = BLOCK_TOKENS
SCALE = 1.0 / math.sqrt(HEAD_DIMENSION)
EXP2_SCALE = SCALE * math.log2(math.e)
F32 = jnp.float32
BF16 = jnp.bfloat16


def split_columns(tokens):
    width = tokens.shape[1] // ROW

    def body(src, dst):
        dst[0] = src[...]

    return pl.pallas_call(
        body,
        grid=(ROW,),
        in_specs=[pl.BlockSpec((B, width), lambda i: (0, i))],
        out_specs=pl.BlockSpec((1, B, width), lambda i: (i, 0, 0)),
        out_shape=jax.ShapeDtypeStruct((ROW, B, width), tokens.dtype),
    )(tokens)


def split_pair(keys, values):
    width = keys.shape[1] // ROW

    def body(k, v, dst):
        dst[0, :, :width] = k[...]
        dst[0, :, width:] = v[...]

    return pl.pallas_call(
        body,
        grid=(ROW,),
        in_specs=[pl.BlockSpec((B, width), lambda i: (0, i))] * 2,
        out_specs=pl.BlockSpec((1, B, 2 * width), lambda i: (i, 0, 0)),
        out_shape=jax.ShapeDtypeStruct((ROW, B, 2 * width), keys.dtype),
    )(keys, values)


def join_columns(parts):
    width = parts.shape[2]

    def body(src, dst):
        dst[...] = src[0]

    return pl.pallas_call(
        body,
        grid=(ROW,),
        in_specs=[pl.BlockSpec((1, B, width), lambda i: (i, 0, 0))],
        out_specs=pl.BlockSpec((B, width), lambda i: (0, i)),
        out_shape=jax.ShapeDtypeStruct((B, ROW * width), parts.dtype),
    )(parts)


def join_pair(parts):
    def body(src, dk, dv):
        for g in range(KV_LOCAL):
            dk[:, g * D : (g + 1) * D] = src[0, g, 0]
            dv[:, g * D : (g + 1) * D] = src[0, g, 1]

    out = jax.ShapeDtypeStruct((B, KEY_VALUE_HEADS * D), parts.dtype)
    return pl.pallas_call(
        body,
        grid=(ROW,),
        in_specs=[pl.BlockSpec((1, KV_LOCAL, 2, B, D), lambda i: (i, 0, 0, 0, 0))],
        out_specs=[pl.BlockSpec((B, KV_LOCAL * D), lambda i: (0, i))] * 2,
        out_shape=[out, out],
    )(parts)


def dot(a, b, ca, cb):
    return lax.dot_general(a, b, (((ca,), (cb,)), ((), ())), preferred_element_type=F32)


def attention_body(
    meta, q_ref, go_ref, k_ref, v_ref, tk_ref, tv_ref, sk_ref, sv_ref,
    dq_ref, own_ref, tail_ref, sink_ref, ks, vs, acc, sacc,
):
    g = pl.program_id(0)
    i = pl.program_id(1)

    @pl.when(i == 0)
    def _():
        ks[: TAIL * B] = tk_ref[...].reshape(TAIL * B, D)
        ks[TAIL * B :] = k_ref[...].reshape(ROW * B, D)
        vs[: TAIL * B] = tv_ref[...].reshape(TAIL * B, D)
        vs[TAIL * B :] = v_ref[...].reshape(ROW * B, D)
        acc[...] = jnp.zeros_like(acc)
        sacc[...] = jnp.zeros_like(sacc)

    block = meta[0] + i
    rows = pl.ds(pl.multiple_of(i * B, B), WMAX * B)
    kw = ks[rows, :]
    vw = vs[rows, :]
    ksink = sk_ref[...].reshape(SMAX * B, D)
    vsink = sv_ref[...].reshape(SMAX * B, D)
    q4 = jnp.concatenate([q_ref[0, :, h * D : (h + 1) * D] for h in range(GROUP)], 0)
    go4 = jnp.concatenate([go_ref[0, :, h * D : (h + 1) * D] for h in range(GROUP)], 0)

    sw = dot(kw, q4, 1, 1)
    ss = dot(ksink, q4, 1, 1)
    pw = dot(vw, go4, 1, 1)
    ps = dot(vsink, go4, 1, 1)
    window = [meta[1 + g * GROUP + h] for h in range(GROUP)]
    sink = [meta[1 + Q_LOCAL + g * GROUP + h] for h in range(GROUP)]

    def bias(allowed):
        return jnp.concatenate(
            [jnp.full((1, B), jnp.where(ok, 0.0, NEG_FILL), F32) for ok in allowed], 1
        )

    scores = []
    grads = []
    for j in range(WMAX):
        slot = TAIL - j
        s = sw[j * B : (j + 1) * B] * EXP2_SCALE
        if slot == 0:
            key = lax.broadcasted_iota(jnp.int32, (B, GROUP * B), 0)
            query = lax.broadcasted_iota(jnp.int32, (B, GROUP * B), 1) % B
            s = jnp.where(key <= query, s, NEG_FILL)
        else:
            s = s + bias([(block >= slot) & (slot < w) for w in window])
        scores.append(s)
        grads.append(pw[j * B : (j + 1) * B])
    for t in range(SMAX):
        s = ss[t * B : (t + 1) * B] * EXP2_SCALE
        s = s + bias([(t < c) & (t <= block - w) for w, c in zip(window, sink)])
        scores.append(s)
        grads.append(ps[t * B : (t + 1) * B])
    top = scores[0]
    for s in scores[1:]:
        top = jnp.maximum(top, s)
    top = jnp.max(top, 0, keepdims=True)
    exps = [jnp.exp2(s - top) for s in scores]
    total = exps[0]
    for e in exps[1:]:
        total = total + e
    inverse = 1.0 / jnp.sum(total, 0, keepdims=True)
    weights = [e * inverse for e in exps]
    rounded = [w.astype(BF16) for w in weights]
    row_dot = rounded[0].astype(F32) * grads[0]
    for w, p in zip(rounded[1:], grads[1:]):
        row_dot = row_dot + w.astype(F32) * p
    row_dot = jnp.sum(row_dot, 0, keepdims=True)
    dscores = [(w * (p - row_dot)).astype(BF16) for w, p in zip(weights, grads)]

    wb_window = jnp.concatenate(rounded[:WMAX], 0)
    wb_sink = jnp.concatenate(rounded[WMAX:], 0)
    ds_window = jnp.concatenate(dscores[:WMAX], 0)
    ds_sink = jnp.concatenate(dscores[WMAX:], 0)
    acc[0, rows, :] += dot(ds_window, q4, 1, 0)
    acc[1, rows, :] += dot(wb_window, go4, 1, 0)
    sacc[0] += dot(ds_sink, q4, 1, 0)
    sacc[1] += dot(wb_sink, go4, 1, 0)
    dqt = (dot(kw, ds_window, 0, 0) + dot(ksink, ds_sink, 0, 0)) * SCALE
    for h in range(GROUP):
        dq_ref[0, :, h * D : (h + 1) * D] = dqt[:, h * B : (h + 1) * B].T.astype(BF16)

    @pl.when(i == ROW - 1)
    def _():
        own_ref[0, 0] = acc[0, TAIL * B :] * SCALE
        own_ref[0, 1] = acc[1, TAIL * B :]
        tail_ref[0, 0] = (acc[0, : TAIL * B] * SCALE).astype(BF16)
        tail_ref[0, 1] = acc[1, : TAIL * B].astype(BF16)
        sink_ref[0, 0] = (sacc[0] * SCALE).astype(BF16)
        sink_ref[0, 1] = sacc[1].astype(BF16)


def attention(meta, q, go, kv, tail, sink, interpret=False):
    wide = pl.BlockSpec((1, B, GROUP * D), lambda g, i, m: (i, 0, g))

    def pair(count):
        return [
            pl.BlockSpec((count, B, D), lambda g, i, m: (0, 0, g)),
            pl.BlockSpec((count, B, D), lambda g, i, m: (0, 0, KV_LOCAL + g)),
        ]

    def result(rows, dtype):
        return (
            pl.BlockSpec((1, 2, rows * B, D), lambda g, i, m: (g, 0, 0, 0)),
            jax.ShapeDtypeStruct((KV_LOCAL, 2, rows * B, D), dtype),
        )

    results = [
        (wide, jax.ShapeDtypeStruct((ROW, B, Q_LOCAL * D), BF16)),
        result(ROW, F32),
        result(TAIL, BF16),
        result(SMAX, BF16),
    ]
    return pl.pallas_call(
        attention_body,
        grid_spec=pltpu.PrefetchScalarGridSpec(
            num_scalar_prefetch=1,
            grid=(KV_LOCAL, ROW),
            in_specs=[wide, wide] + pair(ROW) + pair(TAIL) + pair(SMAX),
            out_specs=[r[0] for r in results],
            scratch_shapes=[
                pltpu.VMEM(((TAIL + ROW) * B, D), BF16),
                pltpu.VMEM(((TAIL + ROW) * B, D), BF16),
                pltpu.VMEM((2, (TAIL + ROW) * B, D), F32),
                pltpu.VMEM((2, SMAX * B, D), F32),
            ],
        ),
        out_shape=[r[1] for r in results],
        compiler_params=pltpu.CompilerParams(vmem_limit_bytes=48 * 1024 * 1024),
        interpret=interpret,
    )(meta, q, go, kv, kv, tail, tail, sink, sink)


def passed(value, pairs):
    def position(run):
        return run % 4 * 32 + run // 4

    return lax.ppermute(value, LINE, [(position(a), position(b)) for a, b in pairs])


def exchanged(value, axes):
    return lax.all_to_all(value, axes, split_axis=0, concat_axis=0, tiled=False)


def shards(queries, keys, values, output_gradient, windows, sinks):
    run = lax.axis_index(("y", "zh", "core")) * 4 + lax.axis_index("zl")
    x = lax.axis_index("x")
    meta = jnp.concatenate(
        [
            (run * ROW)[None].astype(jnp.int32),
            lax.dynamic_slice_in_dim(windows, x * Q_LOCAL, Q_LOCAL),
            lax.dynamic_slice_in_dim(sinks, x * Q_LOCAL, Q_LOCAL),
        ]
    )
    kv = exchanged(split_pair(keys[0], values[0]), "x")
    q = exchanged(split_columns(queries[0]), "x")
    go = exchanged(split_columns(output_gradient[0]), "x")
    tail = passed(kv[ROW - TAIL :], [(r, r + 1) for r in range(RUNS - 1)])
    sink = jnp.where(run == 0, kv[:SMAX], jnp.zeros_like(kv[:SMAX]))
    holders = [0]
    for step in (64, 32, 16, 8, 2, 1, 4):
        sink = sink + passed(sink, [(r, r + step) for r in holders])
        holders = holders + [r + step for r in holders]
    dq, own, tail_grad, sink_grad = attention(meta, q, go, kv, tail, sink)
    dq_tokens = join_columns(exchanged(dq, "x"))

    tail_back = passed(tail_grad, [(r + 1, r) for r in range(RUNS - 1)])
    chunks = exchanged(sink_grad.reshape(RUNS, 8, D), LINE)
    part = jnp.sum(chunks.astype(F32), 0).astype(BF16)
    sink_total = exchanged(jnp.broadcast_to(part[None], (RUNS, 8, D)), LINE)
    sink_total = sink_total.reshape(KV_LOCAL, 2, SMAX * B, D).astype(F32)
    sink_total = jnp.where(run == 0, sink_total, 0.0)
    own = own.reshape(KV_LOCAL, 2, ROW, B, D)
    own = own + jnp.pad(
        tail_back.astype(F32).reshape(KV_LOCAL, 2, TAIL, B, D),
        ((0, 0), (0, 0), (ROW - TAIL, 0), (0, 0), (0, 0)),
    )
    own = own + jnp.pad(
        sink_total.reshape(KV_LOCAL, 2, SMAX, B, D),
        ((0, 0), (0, 0), (0, ROW - SMAX), (0, 0), (0, 0)),
    )
    own = jnp.transpose(own.astype(BF16), (2, 0, 1, 3, 4))
    dk, dv = join_pair(exchanged(own, "x"))
    return dq_tokens[None], dk[None], dv[None]


def solution(mesh):
    split = Mesh(mesh.devices.reshape(SIZES), AXES)
    tokens = P(("y", "zh", "core"), ("zl", "x"), None)
    return jax.shard_map(
        shards,
        mesh=split,
        in_specs=(tokens, tokens, tokens, tokens, P(), P()),
        out_specs=(tokens, tokens, tokens),
        check_vma=False,
    )
```

```python
import math

import jax
import jax.numpy as jnp
from jax import lax
from jax.experimental import pallas as pl
from jax.experimental.pallas import tpu as pltpu
from jax.sharding import Mesh, PartitionSpec as P

QUERY_HEADS = 32
KEY_VALUE_HEADS = 8
HEAD_DIMENSION = 128
BLOCK_TOKENS = 128
WMAX = 4
SMAX = 2
NEG_FILL = -1e30

AXES = ("zl", "x", "y", "zh", "core")
SIZES = (4, 4, 8, 2, 2)
LINE = ("zl", "y", "zh", "core")
ROW = 4
KV_LOCAL = KEY_VALUE_HEADS // ROW
GROUP = QUERY_HEADS // KEY_VALUE_HEADS
Q_LOCAL = KV_LOCAL * GROUP
TAIL = WMAX - 1
PAIR = 2
D = HEAD_DIMENSION
B = BLOCK_TOKENS
SCALE = 1.0 / math.sqrt(HEAD_DIMENSION)
EXP2_SCALE = SCALE * math.log2(math.e)
META_CORE = 1 + 2 * Q_LOCAL
F32 = jnp.float32
BF16 = jnp.bfloat16


ANY = pl.BlockSpec(memory_space=pl.ANY)


def split_pair(first, second):
    width = first.shape[1] // ROW

    def body(a, b, out, held, sem_in, sem_out):
        reads = []
        for i in range(ROW):
            columns = slice(i * width, (i + 1) * width)
            reads.append(
                pltpu.make_async_copy(a.at[:, columns], held.at[i, :, :width], sem_in.at[2 * i])
            )
            reads.append(
                pltpu.make_async_copy(b.at[:, columns], held.at[i, :, width:], sem_in.at[2 * i + 1])
            )
        for copy in reads:
            copy.start()
        writes = []
        for i in range(ROW):
            reads[2 * i].wait()
            reads[2 * i + 1].wait()
            writes.append(pltpu.make_async_copy(held.at[i], out.at[i], sem_out.at[i]))
            writes[-1].start()
        for copy in writes:
            copy.wait()

    shape = (ROW, B, 2 * width)
    return pl.pallas_call(
        body,
        in_specs=[ANY, ANY],
        out_specs=ANY,
        out_shape=jax.ShapeDtypeStruct(shape, first.dtype),
        scratch_shapes=[
            pltpu.VMEM(shape, first.dtype),
            pltpu.SemaphoreType.DMA((2 * ROW,)),
            pltpu.SemaphoreType.DMA((ROW,)),
        ],
    )(first, second)


def join_columns(parts):
    width = parts.shape[2]

    def body(src, out, held, sem_in, sem_out):
        reads = [pltpu.make_async_copy(src.at[i], held.at[i], sem_in.at[i]) for i in range(ROW)]
        for copy in reads:
            copy.start()
        writes = []
        for i in range(ROW):
            reads[i].wait()
            columns = slice(i * width, (i + 1) * width)
            writes.append(pltpu.make_async_copy(held.at[i], out.at[:, columns], sem_out.at[i]))
            writes[-1].start()
        for copy in writes:
            copy.wait()

    return pl.pallas_call(
        body,
        in_specs=[ANY],
        out_specs=ANY,
        out_shape=jax.ShapeDtypeStruct((B, ROW * width), parts.dtype),
        scratch_shapes=[
            pltpu.VMEM(parts.shape, parts.dtype),
            pltpu.SemaphoreType.DMA((ROW,)),
            pltpu.SemaphoreType.DMA((ROW,)),
        ],
    )(parts)


def join_pair(parts, pieces):
    def body(src, *refs):
        extra = refs[:ROW]
        for i in range(ROW):
            for g in range(KV_LOCAL):
                columns = slice((i * KV_LOCAL + g) * D, (i * KV_LOCAL + g + 1) * D)
                for which, out in enumerate(refs[ROW:]):
                    total = src[i, g, which].astype(F32) + extra[i][g, which].astype(F32)
                    out[:, columns] = total.astype(out.dtype)

    out = jax.ShapeDtypeStruct((B, KEY_VALUE_HEADS * D), parts.dtype)
    return pl.pallas_call(body, out_shape=[out, out])(parts, *pieces)


def dot(a, b, ca, cb):
    return lax.dot_general(a, b, (((ca,), (cb,)), ((), ())), preferred_element_type=F32)


def attention_body(
    meta, q_ref, go_ref, k_ref, v_ref, tk_ref, tv_ref, sk_ref, sv_ref, ok_ref, ov_ref,
    dq_ref, own_ref, tail_ref, sink_ref, ks, vs, ssk, ssv, kst, sst, acc, sacc,
):
    g = pl.program_id(0)
    i = pl.program_id(1)

    @pl.when(i == 0)
    def _():
        ks[: TAIL * B] = tk_ref[...].reshape(TAIL * B, D)
        ks[TAIL * B :] = k_ref[...].reshape(ROW * B, D)
        vs[: TAIL * B] = tv_ref[...].reshape(TAIL * B, D)
        vs[TAIL * B :] = v_ref[...].reshape(ROW * B, D)
        near = pl.ds(pl.multiple_of(meta[META_CORE] * B, B), B)
        far = pl.ds(pl.multiple_of((1 - meta[META_CORE]) * B, B), B)
        ssk[near, :] = sk_ref[...]
        ssv[near, :] = sv_ref[...]
        ssk[far, :] = ok_ref[...]
        ssv[far, :] = ov_ref[...]
        kst[...] = ks[...].T
        sst[...] = ssk[...].T
        acc[...] = jnp.zeros_like(acc)
        sacc[...] = jnp.zeros_like(sacc)

    block = meta[0] + i
    rows = pl.ds(pl.multiple_of(i * B, B), WMAX * B)
    kw = ks[rows, :]
    vw = vs[rows, :]
    kwt = kst[:, rows]
    ksink = ssk[...]
    vsink = ssv[...]
    ksinkt = sst[...]
    key = lax.broadcasted_iota(jnp.int32, (B, PAIR * B), 0)
    query = lax.broadcasted_iota(jnp.int32, (B, PAIR * B), 1) % B
    causal = key <= query
    sums = []
    for first in range(0, GROUP, PAIR):
        heads = range(first, first + PAIR)
        q2 = jnp.concatenate([q_ref[0, :, h * D : (h + 1) * D] for h in heads], 0)
        go2 = jnp.concatenate([go_ref[0, :, h * D : (h + 1) * D] for h in heads], 0)
        window = [meta[1 + g * GROUP + h] for h in heads]
        sink = [meta[1 + Q_LOCAL + g * GROUP + h] for h in heads]

        def bias(allowed):
            return jnp.concatenate(
                [jnp.full((1, B), jnp.where(ok, 0.0, NEG_FILL), F32) for ok in allowed], 1
            )

        sw = dot(kw, q2, 1, 1)
        ss = dot(ksink, q2, 1, 1)
        pw = dot(vw, go2, 1, 1)
        ps = dot(vsink, go2, 1, 1)
        scores = [sw[j * B : (j + 1) * B] for j in range(WMAX)]
        scores[TAIL] = jnp.where(causal, scores[TAIL], NEG_FILL)
        scores += [ss[t * B : (t + 1) * B] for t in range(SMAX)]
        grads = [pw[j * B : (j + 1) * B] for j in range(WMAX)]
        grads += [ps[t * B : (t + 1) * B] for t in range(SMAX)]
        biases = [
            bias([(block >= TAIL - j) & (TAIL - j < w) for w in window]) for j in range(TAIL)
        ]
        biases += [jnp.zeros((1, PAIR * B), F32)]
        biases += [
            bias([(t < c) & (t <= block - w) for w, c in zip(window, sink)]) for t in range(SMAX)
        ]
        tops = [
            jnp.max(s, 0, keepdims=True) * EXP2_SCALE + extra for s, extra in zip(scores, biases)
        ]
        top = tops[0]
        for t in tops[1:]:
            top = jnp.maximum(top, t)
        exps = [
            jnp.exp2(s * EXP2_SCALE - (top - extra)) for s, extra in zip(scores, biases)
        ]
        total = exps[0]
        product = exps[0] * grads[0]
        for e, p in zip(exps[1:], grads[1:]):
            total = total + e
            product = product + e * p
        inverse = 1.0 / jnp.sum(total, 0, keepdims=True)
        row_dot = jnp.sum(product, 0, keepdims=True) * inverse
        weights = [e * inverse for e in exps]
        rounded = [w.astype(BF16) for w in weights]
        dscores = [(w * (p - row_dot)).astype(BF16) for w, p in zip(weights, grads)]
        wb_window = jnp.concatenate(rounded[:WMAX], 0)
        wb_sink = jnp.concatenate(rounded[WMAX:], 0)
        ds_window = jnp.concatenate(dscores[:WMAX], 0)
        ds_sink = jnp.concatenate(dscores[WMAX:], 0)
        sums.append(
            [
                dot(ds_window, q2, 1, 0),
                dot(wb_window, go2, 1, 0),
                dot(ds_sink, q2, 1, 0),
                dot(wb_sink, go2, 1, 0),
            ]
        )
        dqt = (dot(kwt, ds_window, 1, 0) + dot(ksinkt, ds_sink, 1, 0)) * SCALE
        for n, h in enumerate(heads):
            dq_ref[0, :, h * D : (h + 1) * D] = dqt[:, n * B : (n + 1) * B].T.astype(BF16)
    acc[0, rows, :] += sum(s[0] for s in sums[1:]) + sums[0][0]
    acc[1, rows, :] += sum(s[1] for s in sums[1:]) + sums[0][1]
    sacc[0] += sum(s[2] for s in sums[1:]) + sums[0][2]
    sacc[1] += sum(s[3] for s in sums[1:]) + sums[0][3]

    @pl.when(i == ROW - 1)
    def _():
        own_ref[0, 0] = acc[0, TAIL * B :] * SCALE
        own_ref[0, 1] = acc[1, TAIL * B :]
        tail_ref[0, 0] = (acc[0, : TAIL * B] * SCALE).astype(BF16)
        tail_ref[0, 1] = acc[1, : TAIL * B].astype(BF16)
        for t in range(SMAX):
            sink_ref[t, 0, 0] = sacc[0, t * B : (t + 1) * B] * SCALE
            sink_ref[t, 0, 1] = sacc[1, t * B : (t + 1) * B]


def attention(meta, qgo, kv, tail, sink, other, interpret=False):
    wide = pl.BlockSpec((1, B, GROUP * D), lambda g, i, m: (i, 0, g))
    wide_go = pl.BlockSpec((1, B, GROUP * D), lambda g, i, m: (i, 0, KV_LOCAL + g))

    def pair(count):
        return [
            pl.BlockSpec((count, B, D), lambda g, i, m: (0, 0, g)),
            pl.BlockSpec((count, B, D), lambda g, i, m: (0, 0, KV_LOCAL + g)),
        ]

    one = [
        pl.BlockSpec((B, D), lambda g, i, m: (0, g)),
        pl.BlockSpec((B, D), lambda g, i, m: (0, KV_LOCAL + g)),
    ]

    def result(rows, dtype):
        return (
            pl.BlockSpec((1, 2, rows * B, D), lambda g, i, m: (g, 0, 0, 0)),
            jax.ShapeDtypeStruct((KV_LOCAL, 2, rows * B, D), dtype),
        )

    results = [
        (wide, jax.ShapeDtypeStruct((ROW, B, Q_LOCAL * D), BF16)),
        result(ROW, F32),
        result(TAIL, BF16),
        (
            pl.BlockSpec((SMAX, 1, 2, B, D), lambda g, i, m: (0, g, 0, 0, 0)),
            jax.ShapeDtypeStruct((SMAX, KV_LOCAL, 2, B, D), F32),
        ),
    ]
    return pl.pallas_call(
        attention_body,
        grid_spec=pltpu.PrefetchScalarGridSpec(
            num_scalar_prefetch=1,
            grid=(KV_LOCAL, ROW),
            in_specs=[wide, wide_go] + pair(ROW) + pair(TAIL) + one + one,
            out_specs=[r[0] for r in results],
            scratch_shapes=[
                pltpu.VMEM(((TAIL + ROW) * B, D), BF16),
                pltpu.VMEM(((TAIL + ROW) * B, D), BF16),
                pltpu.VMEM((SMAX * B, D), BF16),
                pltpu.VMEM((SMAX * B, D), BF16),
                pltpu.VMEM((D, (TAIL + ROW) * B), BF16),
                pltpu.VMEM((D, SMAX * B), BF16),
                pltpu.VMEM((2, (TAIL + ROW) * B, D), F32),
                pltpu.VMEM((2, SMAX * B, D), F32),
            ],
        ),
        out_shape=[r[1] for r in results],
        compiler_params=pltpu.CompilerParams(vmem_limit_bytes=48 * 1024 * 1024),
        interpret=interpret,
    )(meta, qgo, qgo, kv, kv, tail, tail, sink, sink, other, other)


def line(y, z, core):
    return ((z % 4 * 8 + y) * 2 + z // 4) * 2 + core


def tree():
    rounds = []
    holders = [[(0, 0)], [(0, 0)]]
    for step in range(6):
        pairs = []
        for core in range(2):
            along_y = (step < 3) == (core == 0)
            stride = 4 >> step % 3
            moves = [
                ((y, z), (y + stride, z) if along_y else (y, z + stride)) for y, z in holders[core]
            ]
            pairs += [(line(*a, core), line(*b, core)) for a, b in moves]
            holders[core] = holders[core] + [b for _, b in moves]
        rounds.append(pairs)
    return rounds


def exchanged(value, axes):
    return lax.all_to_all(value, axes, split_axis=0, concat_axis=0, tiled=False)


def after(value, *others):
    return lax.optimization_barrier((value, others))[0]


def shards(queries, keys, values, output_gradient, windows, sinks):
    core = lax.axis_index("core")
    run = lax.axis_index(("y", "zh", "core")) * 4 + lax.axis_index("zl")
    x = lax.axis_index("x")
    meta = jnp.concatenate(
        [
            (run * ROW)[None].astype(jnp.int32),
            lax.dynamic_slice_in_dim(windows, x * Q_LOCAL, Q_LOCAL),
            lax.dynamic_slice_in_dim(sinks, x * Q_LOCAL, Q_LOCAL),
            core[None].astype(jnp.int32),
        ]
    )
    runs = [(run // 4 // 4, run // 4 // 2 % 2 * 4 + run % 4, run // 4 % 2) for run in range(128)]
    to_next = [(line(*a), line(*b)) for a, b in zip(runs[:-1], runs[1:])]
    swap = [(0, 1), (1, 0)]

    kv_split = split_pair(keys[0], values[0])
    kv = exchanged(kv_split, "x")
    qgo_split = split_pair(after(queries[0], kv_split), output_gradient[0])
    qgo = exchanged(qgo_split, "x")
    tail = lax.ppermute(kv[ROW - TAIL :], LINE, to_next)
    sink = lax.ppermute(kv[1], LINE, [(line(0, 0, 0), line(0, 0, 1))])
    sink = jnp.where(run == 0, kv[0], sink)
    for pairs in tree():
        sink = sink + lax.ppermute(sink, LINE, pairs)
    other = lax.ppermute(sink, "core", swap)
    dq, own, tail_grad, sink_grad = attention(meta, qgo, kv, tail, sink, other)

    dq_tokens = join_columns(exchanged(dq, "x"))
    tail_back = lax.ppermute(tail_grad, LINE, [(b, a) for a, b in to_next])
    own = own.reshape(KV_LOCAL, 2, ROW, B, D)
    own = own + jnp.pad(
        tail_back.astype(F32).reshape(KV_LOCAL, 2, TAIL, B, D),
        ((0, 0), (0, 0), (ROW - TAIL, 0), (0, 0), (0, 0)),
    )
    own = jnp.transpose(own.astype(BF16), (2, 0, 1, 3, 4))
    parts = exchanged(own, "x")

    total = lax.dynamic_index_in_dim(sink_grad, core, 0, False)
    away = lax.dynamic_index_in_dim(sink_grad, 1 - core, 0, False).astype(BF16)
    total = total + lax.ppermute(away, "core", swap).astype(F32)
    for pairs in reversed(tree()):
        back = [(b, a) for a, b in pairs]
        total = total + lax.ppermute(total.astype(BF16), LINE, back).astype(F32)
    total = total.astype(BF16)

    def at(x, core):
        return x * 32 + core

    pieces = [
        lax.ppermute(total, AXES, [(at(j, c), at(c, 0)) for c in range(SMAX)]) for j in range(ROW)
    ]
    dk, dv = join_pair(parts, pieces)
    return dq_tokens[None], dk[None], dv[None]


def solution(mesh):
    split = Mesh(mesh.devices.reshape(SIZES), AXES)
    tokens = P(("y", "zh", "core"), ("zl", "x"), None)
    return jax.shard_map(
        shards,
        mesh=split,
        in_specs=(tokens, tokens, tokens, tokens, P(), P()),
        out_specs=(tokens, tokens, tokens),
        check_vma=False,
    )
```

```python
import math

import jax
import jax.numpy as jnp
from jax import lax
from jax.experimental import pallas as pl
from jax.experimental.pallas import tpu as pltpu
from jax.sharding import Mesh, PartitionSpec as P

QUERY_HEADS = 32
KEY_VALUE_HEADS = 8
HEAD_DIMENSION = 128
BLOCK_TOKENS = 128
WMAX = 4
SMAX = 2
NEG_FILL = -1e30

AXES = ("zl", "x", "y", "zh", "core")
SIZES = (4, 4, 8, 2, 2)
LINE = ("zl", "y", "zh", "core")
ROW = 4
KV_LOCAL = KEY_VALUE_HEADS // ROW
GROUP = QUERY_HEADS // KEY_VALUE_HEADS
Q_LOCAL = KV_LOCAL * GROUP
TAIL = WMAX - 1
PAIR = 2
D = HEAD_DIMENSION
B = BLOCK_TOKENS
SCALE = 1.0 / math.sqrt(HEAD_DIMENSION)
EXP2_SCALE = SCALE * math.log2(math.e)
META_CORE = 1 + 2 * Q_LOCAL
F32 = jnp.float32
BF16 = jnp.bfloat16


ANY = pl.BlockSpec(memory_space=pl.ANY)


def split_pair(first, second):
    width = first.shape[1] // ROW

    def body(a, b, out, held, sem_in, sem_out):
        reads = []
        for i in range(ROW):
            columns = slice(i * width, (i + 1) * width)
            reads.append(
                pltpu.make_async_copy(a.at[:, columns], held.at[i, :, :width], sem_in.at[2 * i])
            )
            reads.append(
                pltpu.make_async_copy(b.at[:, columns], held.at[i, :, width:], sem_in.at[2 * i + 1])
            )
        for copy in reads:
            copy.start()
        writes = []
        for i in range(ROW):
            reads[2 * i].wait()
            reads[2 * i + 1].wait()
            writes.append(pltpu.make_async_copy(held.at[i], out.at[i], sem_out.at[i]))
            writes[-1].start()
        for copy in writes:
            copy.wait()

    shape = (ROW, B, 2 * width)
    return pl.pallas_call(
        body,
        in_specs=[ANY, ANY],
        out_specs=ANY,
        out_shape=jax.ShapeDtypeStruct(shape, first.dtype),
        scratch_shapes=[
            pltpu.VMEM(shape, first.dtype),
            pltpu.SemaphoreType.DMA((2 * ROW,)),
            pltpu.SemaphoreType.DMA((ROW,)),
        ],
    )(first, second)


def join_columns(parts):
    width = parts.shape[2]

    def body(src, out, held, sem_in, sem_out):
        reads = [pltpu.make_async_copy(src.at[i], held.at[i], sem_in.at[i]) for i in range(ROW)]
        for copy in reads:
            copy.start()
        writes = []
        for i in range(ROW):
            reads[i].wait()
            columns = slice(i * width, (i + 1) * width)
            writes.append(pltpu.make_async_copy(held.at[i], out.at[:, columns], sem_out.at[i]))
            writes[-1].start()
        for copy in writes:
            copy.wait()

    return pl.pallas_call(
        body,
        in_specs=[ANY],
        out_specs=ANY,
        out_shape=jax.ShapeDtypeStruct((B, ROW * width), parts.dtype),
        scratch_shapes=[
            pltpu.VMEM(parts.shape, parts.dtype),
            pltpu.SemaphoreType.DMA((ROW,)),
            pltpu.SemaphoreType.DMA((ROW,)),
        ],
    )(parts)


def join_pair(parts, pieces):
    def body(src, *refs):
        extra = refs[:ROW]
        for i in range(ROW):
            for g in range(KV_LOCAL):
                columns = slice((i * KV_LOCAL + g) * D, (i * KV_LOCAL + g + 1) * D)
                for which, out in enumerate(refs[ROW:]):
                    total = src[i, g, which].astype(F32) + extra[i][g, which].astype(F32)
                    out[:, columns] = total.astype(out.dtype)

    out = jax.ShapeDtypeStruct((B, KEY_VALUE_HEADS * D), parts.dtype)
    return pl.pallas_call(body, out_shape=[out, out])(parts, *pieces)


def dot(a, b, ca, cb):
    return lax.dot_general(a, b, (((ca,), (cb,)), ((), ())), preferred_element_type=F32)


def attention_body(
    meta, q_ref, go_ref, k_ref, v_ref, tk_ref, tv_ref, sk_ref, sv_ref, ok_ref, ov_ref,
    dq_ref, own_ref, tail_ref, sink_ref, ks, vs, ssk, ssv, kst, sst, acc, sacc,
):
    g = pl.program_id(0)
    i = pl.program_id(1)

    @pl.when(i == 0)
    def _():
        ks[: TAIL * B] = tk_ref[...].reshape(TAIL * B, D)
        ks[TAIL * B :] = k_ref[...].reshape(ROW * B, D)
        vs[: TAIL * B] = tv_ref[...].reshape(TAIL * B, D)
        vs[TAIL * B :] = v_ref[...].reshape(ROW * B, D)
        near = pl.ds(pl.multiple_of(meta[META_CORE] * B, B), B)
        far = pl.ds(pl.multiple_of((1 - meta[META_CORE]) * B, B), B)
        ssk[near, :] = sk_ref[...]
        ssv[near, :] = sv_ref[...]
        ssk[far, :] = ok_ref[...]
        ssv[far, :] = ov_ref[...]
        kst[...] = ks[...].T
        sst[...] = ssk[...].T
        acc[...] = jnp.zeros_like(acc)
        sacc[...] = jnp.zeros_like(sacc)

    block = meta[0] + i
    rows = pl.ds(pl.multiple_of(i * B, B), WMAX * B)
    kw = ks[rows, :]
    vw = vs[rows, :]
    kwt = kst[:, rows]
    ksink = ssk[...]
    vsink = ssv[...]
    ksinkt = sst[...]
    key = lax.broadcasted_iota(jnp.int32, (B, PAIR * B), 0)
    query = lax.broadcasted_iota(jnp.int32, (B, PAIR * B), 1) % B
    causal = key <= query
    sums = []
    for first in range(0, GROUP, PAIR):
        heads = range(first, first + PAIR)
        q2 = jnp.concatenate([q_ref[0, :, h * D : (h + 1) * D] for h in heads], 0)
        go2 = jnp.concatenate([go_ref[0, :, h * D : (h + 1) * D] for h in heads], 0)
        window = [meta[1 + g * GROUP + h] for h in heads]
        sink = [meta[1 + Q_LOCAL + g * GROUP + h] for h in heads]

        def bias(allowed):
            return jnp.concatenate(
                [jnp.full((1, B), jnp.where(ok, 0.0, NEG_FILL), F32) for ok in allowed], 1
            )

        sw = dot(kw, q2, 1, 1)
        ss = dot(ksink, q2, 1, 1)
        pw = dot(vw, go2, 1, 1)
        ps = dot(vsink, go2, 1, 1)
        scores = [sw[j * B : (j + 1) * B] for j in range(WMAX)]
        scores[TAIL] = jnp.where(causal, scores[TAIL], NEG_FILL)
        scores += [ss[t * B : (t + 1) * B] for t in range(SMAX)]
        grads = [pw[j * B : (j + 1) * B] for j in range(WMAX)]
        grads += [ps[t * B : (t + 1) * B] for t in range(SMAX)]
        biases = [
            bias([(block >= TAIL - j) & (TAIL - j < w) for w in window]) for j in range(TAIL)
        ]
        biases += [jnp.zeros((1, PAIR * B), F32)]
        biases += [
            bias([(t < c) & (t <= block - w) for w, c in zip(window, sink)]) for t in range(SMAX)
        ]
        tops = [
            jnp.max(s, 0, keepdims=True) * EXP2_SCALE + extra for s, extra in zip(scores, biases)
        ]
        top = tops[0]
        for t in tops[1:]:
            top = jnp.maximum(top, t)
        exps = [
            jnp.exp2(s * EXP2_SCALE - (top - extra)) for s, extra in zip(scores, biases)
        ]
        total = exps[0]
        product = exps[0] * grads[0]
        for e, p in zip(exps[1:], grads[1:]):
            total = total + e
            product = product + e * p
        inverse = 1.0 / jnp.sum(total, 0, keepdims=True)
        row_dot = jnp.sum(product, 0, keepdims=True) * inverse
        weights = [e * inverse for e in exps]
        rounded = [w.astype(BF16) for w in weights]
        dscores = [(w * (p - row_dot)).astype(BF16) for w, p in zip(weights, grads)]
        wb_window = jnp.concatenate(rounded[:WMAX], 0)
        wb_sink = jnp.concatenate(rounded[WMAX:], 0)
        ds_window = jnp.concatenate(dscores[:WMAX], 0)
        ds_sink = jnp.concatenate(dscores[WMAX:], 0)
        sums.append(
            [
                dot(ds_window, q2, 1, 0),
                dot(wb_window, go2, 1, 0),
                dot(ds_sink, q2, 1, 0),
                dot(wb_sink, go2, 1, 0),
            ]
        )
        dqt = (dot(kwt, ds_window, 1, 0) + dot(ksinkt, ds_sink, 1, 0)) * SCALE
        for n, h in enumerate(heads):
            dq_ref[0, :, h * D : (h + 1) * D] = dqt[:, n * B : (n + 1) * B].T.astype(BF16)
    acc[0, rows, :] += sum(s[0] for s in sums[1:]) + sums[0][0]
    acc[1, rows, :] += sum(s[1] for s in sums[1:]) + sums[0][1]
    sacc[0] += sum(s[2] for s in sums[1:]) + sums[0][2]
    sacc[1] += sum(s[3] for s in sums[1:]) + sums[0][3]

    @pl.when(i == ROW - 1)
    def _():
        own_ref[0, 0] = acc[0, TAIL * B :] * SCALE
        own_ref[0, 1] = acc[1, TAIL * B :]
        tail_ref[0, 0] = (acc[0, : TAIL * B] * SCALE).astype(BF16)
        tail_ref[0, 1] = acc[1, : TAIL * B].astype(BF16)
        for t in range(SMAX):
            sink_ref[t, 0, 0] = sacc[0, t * B : (t + 1) * B] * SCALE
            sink_ref[t, 0, 1] = sacc[1, t * B : (t + 1) * B]


def attention(meta, qgo, kv, tail, sink, other, interpret=False):
    wide = pl.BlockSpec((1, B, GROUP * D), lambda g, i, m: (i, 0, g))
    wide_go = pl.BlockSpec((1, B, GROUP * D), lambda g, i, m: (i, 0, KV_LOCAL + g))

    def pair(count):
        return [
            pl.BlockSpec((count, B, D), lambda g, i, m: (0, 0, g)),
            pl.BlockSpec((count, B, D), lambda g, i, m: (0, 0, KV_LOCAL + g)),
        ]

    one = [
        pl.BlockSpec((B, D), lambda g, i, m: (0, g)),
        pl.BlockSpec((B, D), lambda g, i, m: (0, KV_LOCAL + g)),
    ]

    def result(rows, dtype):
        return (
            pl.BlockSpec((1, 2, rows * B, D), lambda g, i, m: (g, 0, 0, 0)),
            jax.ShapeDtypeStruct((KV_LOCAL, 2, rows * B, D), dtype),
        )

    results = [
        (wide, jax.ShapeDtypeStruct((ROW, B, Q_LOCAL * D), BF16)),
        result(ROW, F32),
        result(TAIL, BF16),
        (
            pl.BlockSpec((SMAX, 1, 2, B, D), lambda g, i, m: (0, g, 0, 0, 0)),
            jax.ShapeDtypeStruct((SMAX, KV_LOCAL, 2, B, D), F32),
        ),
    ]
    return pl.pallas_call(
        attention_body,
        grid_spec=pltpu.PrefetchScalarGridSpec(
            num_scalar_prefetch=1,
            grid=(KV_LOCAL, ROW),
            in_specs=[wide, wide_go] + pair(ROW) + pair(TAIL) + one + one,
            out_specs=[r[0] for r in results],
            scratch_shapes=[
                pltpu.VMEM(((TAIL + ROW) * B, D), BF16),
                pltpu.VMEM(((TAIL + ROW) * B, D), BF16),
                pltpu.VMEM((SMAX * B, D), BF16),
                pltpu.VMEM((SMAX * B, D), BF16),
                pltpu.VMEM((D, (TAIL + ROW) * B), BF16),
                pltpu.VMEM((D, SMAX * B), BF16),
                pltpu.VMEM((2, (TAIL + ROW) * B, D), F32),
                pltpu.VMEM((2, SMAX * B, D), F32),
            ],
        ),
        out_shape=[r[1] for r in results],
        compiler_params=pltpu.CompilerParams(vmem_limit_bytes=48 * 1024 * 1024),
        interpret=interpret,
    )(meta, qgo, qgo, kv, kv, tail, tail, sink, sink, other, other)


def line(y, z, core):
    return ((z % 4 * 8 + y) * 2 + z // 4) * 2 + core


ROUNDS = (((2, 0), (4, 0), (6, 0)), ((1, 0), (0, 4), (1, 4)), ((0, 1), (0, 2), (0, 7)))


def tree():
    holders = [(0, 0)]
    rounds = []
    for offsets in ROUNDS:
        permutes = []
        added = []
        for da, db in offsets:
            moves = [((a, b), ((a + da) % 8, (b + db) % 8)) for a, b in holders]
            permutes.append(
                [(line(*p, 0), line(*q, 0)) for p, q in moves]
                + [(line(*p[::-1], 1), line(*q[::-1], 1)) for p, q in moves]
            )
            added += [q for _, q in moves]
        holders = holders + added
        rounds.append(permutes)
    return rounds


def exchanged(value, axes):
    return lax.all_to_all(value, axes, split_axis=0, concat_axis=0, tiled=False)


def after(value, *others):
    return lax.optimization_barrier((value, others))[0]


def shards(queries, keys, values, output_gradient, windows, sinks):
    core = lax.axis_index("core")
    run = lax.axis_index(("y", "zh", "core")) * 4 + lax.axis_index("zl")
    x = lax.axis_index("x")
    meta = jnp.concatenate(
        [
            (run * ROW)[None].astype(jnp.int32),
            lax.dynamic_slice_in_dim(windows, x * Q_LOCAL, Q_LOCAL),
            lax.dynamic_slice_in_dim(sinks, x * Q_LOCAL, Q_LOCAL),
            core[None].astype(jnp.int32),
        ]
    )
    runs = [(run // 4 // 4, run // 4 // 2 % 2 * 4 + run % 4, run // 4 % 2) for run in range(128)]
    to_next = [(line(*a), line(*b)) for a, b in zip(runs[:-1], runs[1:])]
    swap = [(0, 1), (1, 0)]

    kv_split = split_pair(keys[0], values[0])
    qgo_split = split_pair(after(queries[0], kv_split), output_gradient[0])
    kv = after(exchanged(kv_split, "x"), qgo_split)
    qgo = exchanged(qgo_split, "x")
    tail = lax.ppermute(kv[ROW - TAIL :], LINE, to_next)
    sink = lax.ppermute(kv[1], LINE, [(line(0, 0, 0), line(0, 0, 1))])
    sink = jnp.where(run == 0, kv[0], sink)
    for number, permutes in enumerate(tree()):
        if number == 2:
            sink = after(sink, tail)
        got = [lax.ppermute(sink, LINE, pairs) for pairs in permutes]
        sink = sink + got[0] + got[1] + got[2]
    other = lax.ppermute(sink, "core", swap)
    dq, own, tail_grad, sink_grad = attention(meta, qgo, kv, tail, sink, other)

    dq_parts = exchanged(dq, "x")
    dq_tokens = join_columns(dq_parts)
    tail_back = lax.ppermute(tail_grad, LINE, [(b, a) for a, b in to_next])
    own = own.reshape(KV_LOCAL, 2, ROW, B, D)
    own = own + jnp.pad(
        tail_back.astype(F32).reshape(KV_LOCAL, 2, TAIL, B, D),
        ((0, 0), (0, 0), (ROW - TAIL, 0), (0, 0), (0, 0)),
    )
    own = jnp.transpose(own.astype(BF16), (2, 0, 1, 3, 4))
    parts = exchanged(own, "x")

    total = lax.dynamic_index_in_dim(sink_grad, core, 0, False)
    away = lax.dynamic_index_in_dim(sink_grad, 1 - core, 0, False).astype(BF16)
    total = total + lax.ppermute(away, "core", swap).astype(F32)
    for number, permutes in enumerate(reversed(tree())):
        if number == 1:
            total = after(total, dq_parts)
        if number == 2:
            total = after(total, parts)
        send = total.astype(BF16)
        for pairs in permutes:
            got = lax.ppermute(send, LINE, [(b, a) for a, b in pairs])
            total = total + got.astype(F32)
    total = total.astype(BF16)

    def at(x, core):
        return x * 32 + core

    pieces = [
        lax.ppermute(total, AXES, [(at(j, c), at(c, 0)) for c in range(SMAX)]) for j in range(ROW)
    ]
    dk, dv = join_pair(parts, pieces)
    return dq_tokens[None], dk[None], dv[None]


def solution(mesh):
    split = Mesh(mesh.devices.reshape(SIZES), AXES)
    tokens = P(("y", "zh", "core"), ("zl", "x"), None)
    return jax.shard_map(
        shards,
        mesh=split,
        in_specs=(tokens, tokens, tokens, tokens, P(), P()),
        out_specs=(tokens, tokens, tokens),
        check_vma=False,
    )
```

```python
import math

import jax
import jax.numpy as jnp
from jax import lax
from jax.experimental import pallas as pl
from jax.experimental.pallas import tpu as pltpu
from jax.sharding import Mesh, PartitionSpec as P

QUERY_HEADS = 32
KEY_VALUE_HEADS = 8
HEAD_DIMENSION = 128
BLOCK_TOKENS = 128
WMAX = 4
SMAX = 2
NEG_FILL = -1e30

AXES = ("zl", "x", "y", "zh", "core")
SIZES = (4, 4, 8, 2, 2)
LINE = ("zl", "y", "zh", "core")
ROW = 4
KV_LOCAL = KEY_VALUE_HEADS // ROW
GROUP = QUERY_HEADS // KEY_VALUE_HEADS
Q_LOCAL = KV_LOCAL * GROUP
TAIL = WMAX - 1
KV_COLUMNS = 2 * KV_LOCAL * HEAD_DIMENSION
PAIR = 2
D = HEAD_DIMENSION
B = BLOCK_TOKENS
SCALE = 1.0 / math.sqrt(HEAD_DIMENSION)
EXP2_SCALE = SCALE * math.log2(math.e)
META_CORE = 1 + 2 * Q_LOCAL
MIB = 1024 * 1024
F32 = jnp.float32
BF16 = jnp.bfloat16


ANY = pl.BlockSpec(memory_space=pl.ANY)
SMALL = pltpu.CompilerParams(vmem_limit_bytes=6 * MIB)


def split_pair(first, second):
    width = first.shape[1] // ROW

    def body(a, b, out, held, sem_in, sem_out):
        reads = []
        for i in range(ROW):
            columns = slice(i * width, (i + 1) * width)
            reads.append(
                pltpu.make_async_copy(a.at[:, columns], held.at[i, :, :width], sem_in.at[2 * i])
            )
            reads.append(
                pltpu.make_async_copy(b.at[:, columns], held.at[i, :, width:], sem_in.at[2 * i + 1])
            )
        for copy in reads:
            copy.start()
        writes = []
        for i in range(ROW):
            reads[2 * i].wait()
            reads[2 * i + 1].wait()
            writes.append(pltpu.make_async_copy(held.at[i], out.at[i], sem_out.at[i]))
            writes[-1].start()
        for copy in writes:
            copy.wait()

    shape = (ROW, B, 2 * width)
    return pl.pallas_call(
        body,
        in_specs=[ANY, ANY],
        out_specs=ANY,
        out_shape=jax.ShapeDtypeStruct(shape, first.dtype),
        scratch_shapes=[
            pltpu.VMEM(shape, first.dtype),
            pltpu.SemaphoreType.DMA((2 * ROW,)),
            pltpu.SemaphoreType.DMA((ROW,)),
        ],
    )(first, second)


def join_columns(parts, width):
    def body(src, out, held, sem_in, sem_out):
        reads = [
            pltpu.make_async_copy(src.at[i, :, :width], held.at[i], sem_in.at[i])
            for i in range(ROW)
        ]
        for copy in reads:
            copy.start()
        writes = []
        for i in range(ROW):
            reads[i].wait()
            columns = slice(i * width, (i + 1) * width)
            writes.append(pltpu.make_async_copy(held.at[i], out.at[:, columns], sem_out.at[i]))
            writes[-1].start()
        for copy in writes:
            copy.wait()

    return pl.pallas_call(
        body,
        in_specs=[ANY],
        out_specs=ANY,
        out_shape=jax.ShapeDtypeStruct((B, ROW * width), parts.dtype),
        scratch_shapes=[
            pltpu.VMEM((ROW, B, width), parts.dtype),
            pltpu.SemaphoreType.DMA((ROW,)),
            pltpu.SemaphoreType.DMA((ROW,)),
        ],
        compiler_params=SMALL,
    )(parts)


def with_key_grads(dq, own, tail):
    def body(_, own_ref, tail_ref, out):
        for b in range(ROW):
            for n in range(2 * KV_LOCAL):
                g, which = divmod(n, 2)
                total = own_ref[g, which, b * B : (b + 1) * B]
                if b >= ROW - TAIL:
                    start = (b - (ROW - TAIL)) * B
                    total = total + tail_ref[g, which, start : start + B].astype(F32)
                out[b, :, n * D : (n + 1) * D] = total.astype(BF16)

    return pl.pallas_call(
        body,
        grid=(1,),
        in_specs=[
            ANY,
            pl.BlockSpec(own.shape, lambda i: (0, 0, 0, 0)),
            pl.BlockSpec(tail.shape, lambda i: (0, 0, 0, 0)),
        ],
        out_specs=pl.BlockSpec((ROW, B, KV_COLUMNS), lambda i: (0, 0, Q_LOCAL * D // KV_COLUMNS)),
        out_shape=jax.ShapeDtypeStruct(dq.shape, dq.dtype),
        input_output_aliases={0: 0},
        compiler_params=SMALL,
    )(dq, own, tail)


def join_pair(parts, pieces):
    def body(src, *refs):
        extra = refs[:ROW]
        for i in range(ROW):
            for n in range(2 * KV_LOCAL):
                g, which = divmod(n, 2)
                out = refs[ROW + which]
                total = src[i, :, n * D : (n + 1) * D].astype(F32) + extra[i][g, which].astype(F32)
                h = i * KV_LOCAL + g
                out[:, h * D : (h + 1) * D] = total.astype(out.dtype)

    piece = pl.BlockSpec(pieces[0].shape, lambda i: (0, 0, 0, 0))
    width = KEY_VALUE_HEADS * D
    out = jax.ShapeDtypeStruct((B, width), parts.dtype)
    return pl.pallas_call(
        body,
        grid=(1,),
        in_specs=[
            pl.BlockSpec((ROW, B, KV_COLUMNS), lambda i: (0, 0, Q_LOCAL * D // KV_COLUMNS))
        ]
        + [piece] * ROW,
        out_specs=[pl.BlockSpec((B, width), lambda i: (0, 0))] * 2,
        out_shape=[out, out],
        compiler_params=SMALL,
    )(parts, *pieces)


def dot(a, b, ca, cb):
    return lax.dot_general(a, b, (((ca,), (cb,)), ((), ())), preferred_element_type=F32)


def attention_body(
    meta, q_ref, go_ref, k_ref, v_ref, tk_ref, tv_ref, sk_ref, sv_ref, ok_ref, ov_ref,
    dq_ref, own_ref, tail_ref, sink_ref, ks, vs, ssk, ssv, kst, sst, acc, sacc,
):
    g = pl.program_id(0)
    i = pl.program_id(1)

    @pl.when(i == 0)
    def _():
        ks[: TAIL * B] = tk_ref[...].reshape(TAIL * B, D)
        ks[TAIL * B :] = k_ref[...].reshape(ROW * B, D)
        vs[: TAIL * B] = tv_ref[...].reshape(TAIL * B, D)
        vs[TAIL * B :] = v_ref[...].reshape(ROW * B, D)
        near = pl.ds(pl.multiple_of(meta[META_CORE] * B, B), B)
        far = pl.ds(pl.multiple_of((1 - meta[META_CORE]) * B, B), B)
        ssk[near, :] = sk_ref[...]
        ssv[near, :] = sv_ref[...]
        ssk[far, :] = ok_ref[...]
        ssv[far, :] = ov_ref[...]
        kst[...] = ks[...].T
        sst[...] = ssk[...].T
        acc[...] = jnp.zeros_like(acc)
        sacc[...] = jnp.zeros_like(sacc)

    block = meta[0] + i
    rows = pl.ds(pl.multiple_of(i * B, B), WMAX * B)
    kw = ks[rows, :]
    vw = vs[rows, :]
    kwt = kst[:, rows]
    ksink = ssk[...]
    vsink = ssv[...]
    ksinkt = sst[...]
    key = lax.broadcasted_iota(jnp.int32, (B, PAIR * B), 0)
    query = lax.broadcasted_iota(jnp.int32, (B, PAIR * B), 1) % B
    causal = key <= query
    sums = []
    for first in range(0, GROUP, PAIR):
        heads = range(first, first + PAIR)
        q2 = jnp.concatenate([q_ref[0, :, h * D : (h + 1) * D] for h in heads], 0)
        go2 = jnp.concatenate([go_ref[0, :, h * D : (h + 1) * D] for h in heads], 0)
        window = [meta[1 + g * GROUP + h] for h in heads]
        sink = [meta[1 + Q_LOCAL + g * GROUP + h] for h in heads]

        def bias(allowed):
            return jnp.concatenate(
                [jnp.full((1, B), jnp.where(ok, 0.0, NEG_FILL), F32) for ok in allowed], 1
            )

        sw = dot(kw, q2, 1, 1)
        ss = dot(ksink, q2, 1, 1)
        pw = dot(vw, go2, 1, 1)
        ps = dot(vsink, go2, 1, 1)
        scores = [sw[j * B : (j + 1) * B] for j in range(WMAX)]
        scores[TAIL] = jnp.where(causal, scores[TAIL], NEG_FILL)
        scores += [ss[t * B : (t + 1) * B] for t in range(SMAX)]
        grads = [pw[j * B : (j + 1) * B] for j in range(WMAX)]
        grads += [ps[t * B : (t + 1) * B] for t in range(SMAX)]
        biases = [
            bias([(block >= TAIL - j) & (TAIL - j < w) for w in window]) for j in range(TAIL)
        ]
        biases += [jnp.zeros((1, PAIR * B), F32)]
        biases += [
            bias([(t < c) & (t <= block - w) for w, c in zip(window, sink)]) for t in range(SMAX)
        ]
        tops = [
            jnp.max(s, 0, keepdims=True) * EXP2_SCALE + extra for s, extra in zip(scores, biases)
        ]
        top = tops[0]
        for t in tops[1:]:
            top = jnp.maximum(top, t)
        exps = [
            jnp.exp2(s * EXP2_SCALE - (top - extra)) for s, extra in zip(scores, biases)
        ]
        total = exps[0]
        product = exps[0] * grads[0]
        for e, p in zip(exps[1:], grads[1:]):
            total = total + e
            product = product + e * p
        inverse = 1.0 / jnp.sum(total, 0, keepdims=True)
        row_dot = jnp.sum(product, 0, keepdims=True) * inverse
        weights = [e * inverse for e in exps]
        rounded = [w.astype(BF16) for w in weights]
        dscores = [(w * (p - row_dot)).astype(BF16) for w, p in zip(weights, grads)]
        wb_window = jnp.concatenate(rounded[:WMAX], 0)
        wb_sink = jnp.concatenate(rounded[WMAX:], 0)
        ds_window = jnp.concatenate(dscores[:WMAX], 0)
        ds_sink = jnp.concatenate(dscores[WMAX:], 0)
        sums.append(
            [
                dot(ds_window, q2, 1, 0),
                dot(wb_window, go2, 1, 0),
                dot(ds_sink, q2, 1, 0),
                dot(wb_sink, go2, 1, 0),
            ]
        )
        dqt = (dot(kwt, ds_window, 1, 0) + dot(ksinkt, ds_sink, 1, 0)) * SCALE
        for n, h in enumerate(heads):
            dq_ref[0, :, h * D : (h + 1) * D] = dqt[:, n * B : (n + 1) * B].T.astype(BF16)
    acc[0, rows, :] += sum(s[0] for s in sums[1:]) + sums[0][0]
    acc[1, rows, :] += sum(s[1] for s in sums[1:]) + sums[0][1]
    sacc[0] += sum(s[2] for s in sums[1:]) + sums[0][2]
    sacc[1] += sum(s[3] for s in sums[1:]) + sums[0][3]

    @pl.when(i == ROW - 1)
    def _():
        own_ref[0, 0] = acc[0, TAIL * B :] * SCALE
        own_ref[0, 1] = acc[1, TAIL * B :]
        tail_ref[0, 0] = (acc[0, : TAIL * B] * SCALE).astype(BF16)
        tail_ref[0, 1] = acc[1, : TAIL * B].astype(BF16)
        for t in range(SMAX):
            sink_ref[t, 0, 0] = sacc[0, t * B : (t + 1) * B] * SCALE
            sink_ref[t, 0, 1] = sacc[1, t * B : (t + 1) * B]


def attention(meta, qgo, kv, tail, sink, other, interpret=False):
    wide = pl.BlockSpec((1, B, GROUP * D), lambda g, i, m: (i, 0, g))
    wide_go = pl.BlockSpec((1, B, GROUP * D), lambda g, i, m: (i, 0, KV_LOCAL + g))

    def pair(count):
        return [
            pl.BlockSpec((count, B, D), lambda g, i, m: (0, 0, g)),
            pl.BlockSpec((count, B, D), lambda g, i, m: (0, 0, KV_LOCAL + g)),
        ]

    one = [
        pl.BlockSpec((B, D), lambda g, i, m: (0, g)),
        pl.BlockSpec((B, D), lambda g, i, m: (0, KV_LOCAL + g)),
    ]

    def result(rows, dtype):
        return (
            pl.BlockSpec((1, 2, rows * B, D), lambda g, i, m: (g, 0, 0, 0)),
            jax.ShapeDtypeStruct((KV_LOCAL, 2, rows * B, D), dtype),
        )

    results = [
        (wide, jax.ShapeDtypeStruct((ROW, B, Q_LOCAL * D + KV_COLUMNS), BF16)),
        result(ROW, F32),
        result(TAIL, BF16),
        (
            pl.BlockSpec((SMAX, 1, 2, B, D), lambda g, i, m: (0, g, 0, 0, 0)),
            jax.ShapeDtypeStruct((SMAX, KV_LOCAL, 2, B, D), F32),
        ),
    ]
    return pl.pallas_call(
        attention_body,
        grid_spec=pltpu.PrefetchScalarGridSpec(
            num_scalar_prefetch=1,
            grid=(KV_LOCAL, ROW),
            in_specs=[wide, wide_go] + pair(ROW) + pair(TAIL) + one + one,
            out_specs=[r[0] for r in results],
            scratch_shapes=[
                pltpu.VMEM(((TAIL + ROW) * B, D), BF16),
                pltpu.VMEM(((TAIL + ROW) * B, D), BF16),
                pltpu.VMEM((SMAX * B, D), BF16),
                pltpu.VMEM((SMAX * B, D), BF16),
                pltpu.VMEM((D, (TAIL + ROW) * B), BF16),
                pltpu.VMEM((D, SMAX * B), BF16),
                pltpu.VMEM((2, (TAIL + ROW) * B, D), F32),
                pltpu.VMEM((2, SMAX * B, D), F32),
            ],
        ),
        out_shape=[r[1] for r in results],
        compiler_params=pltpu.CompilerParams(vmem_limit_bytes=48 * MIB),
        interpret=interpret,
    )(meta, qgo, qgo, kv, kv, tail, tail, sink, sink, other, other)


def line(y, z, core):
    return ((z % 4 * 8 + y) * 2 + z // 4) * 2 + core


def tree():
    rounds = []
    holders = [(0, 0)]
    for step in range(6):
        stride = 4 >> step % 3
        moves = [((a, b), (a + stride, b) if step < 3 else (a, b + stride)) for a, b in holders]
        rounds.append(
            [(line(*p, 0), line(*q, 0)) for p, q in moves]
            + [(line(*p[::-1], 1), line(*q[::-1], 1)) for p, q in moves]
        )
        holders = holders + [q for _, q in moves]
    return rounds


def exchanged(value, axes):
    return lax.all_to_all(value, axes, split_axis=0, concat_axis=0, tiled=False)


def after(value, *others):
    return lax.optimization_barrier((value, others))[0]


def shards(queries, keys, values, output_gradient, windows, sinks):
    core = lax.axis_index("core")
    run = lax.axis_index(("y", "zh", "core")) * 4 + lax.axis_index("zl")
    x = lax.axis_index("x")
    meta = jnp.concatenate(
        [
            (run * ROW)[None].astype(jnp.int32),
            lax.dynamic_slice_in_dim(windows, x * Q_LOCAL, Q_LOCAL),
            lax.dynamic_slice_in_dim(sinks, x * Q_LOCAL, Q_LOCAL),
            core[None].astype(jnp.int32),
        ]
    )
    runs = [(run // 4 // 4, run // 4 // 2 % 2 * 4 + run % 4, run // 4 % 2) for run in range(128)]
    to_next = [(line(*a), line(*b)) for a, b in zip(runs[:-1], runs[1:])]
    swap = [(0, 1), (1, 0)]

    kv_split = split_pair(keys[0], values[0])
    qgo_split = split_pair(after(queries[0], kv_split), output_gradient[0])
    kv = after(exchanged(kv_split, "x"), qgo_split)
    qgo = exchanged(qgo_split, "x")
    tail = lax.ppermute(kv[ROW - TAIL :], LINE, to_next)
    sink = lax.ppermute(kv[1], LINE, [(line(0, 0, 0), line(0, 0, 1))])
    sink = jnp.where(run == 0, kv[0], sink)
    for step, pairs in enumerate(tree()):
        if step == 3:
            sink = after(sink, tail)
        sink = sink + lax.ppermute(sink, LINE, pairs)
    other = lax.ppermute(sink, "core", swap)
    dq, own, tail_grad, sink_grad = attention(meta, qgo, kv, tail, sink, other)

    tail_back = lax.ppermute(tail_grad, LINE, [(b, a) for a, b in to_next])
    grads = with_key_grads(dq, own, tail_back)
    parts = exchanged(grads, "x")
    dq_tokens = join_columns(parts, Q_LOCAL * D)

    total = lax.dynamic_index_in_dim(sink_grad, core, 0, False)
    away = lax.dynamic_index_in_dim(sink_grad, 1 - core, 0, False).astype(BF16)
    total = total + lax.ppermute(away, "core", swap).astype(F32)
    for step, pairs in enumerate(reversed(tree())):
        if step == 2:
            total = after(total, grads)
        got = lax.ppermute(total.astype(BF16), LINE, [(b, a) for a, b in pairs])
        total = total + got.astype(F32)
    total = after(total, parts)
    total = total.astype(BF16)

    def at(x, core):
        return x * 32 + core

    pieces = [
        lax.ppermute(total, AXES, [(at(j, c), at(c, 0)) for c in range(SMAX)]) for j in range(ROW)
    ]
    dk, dv = join_pair(parts, pieces)
    return dq_tokens[None], dk[None], dv[None]


def solution(mesh):
    split = Mesh(mesh.devices.reshape(SIZES), AXES)
    tokens = P(("y", "zh", "core"), ("zl", "x"), None)
    return jax.shard_map(
        shards,
        mesh=split,
        in_specs=(tokens, tokens, tokens, tokens, P(), P()),
        out_specs=(tokens, tokens, tokens),
        check_vma=False,
    )
```

```python
import math

import jax
import jax.numpy as jnp
from jax import lax
from jax.experimental import pallas as pl
from jax.experimental.pallas import tpu as pltpu
from jax.sharding import Mesh, PartitionSpec as P

QUERY_HEADS = 32
KEY_VALUE_HEADS = 8
HEAD_DIMENSION = 128
BLOCK_TOKENS = 128
WMAX = 4
SMAX = 2
NEG_FILL = -1e30

AXES = ("zl", "x", "y", "zh", "core")
SIZES = (4, 4, 8, 2, 2)
LINE = ("zl", "y", "zh", "core")
ROW = 4
KV_LOCAL = KEY_VALUE_HEADS // ROW
GROUP = QUERY_HEADS // KEY_VALUE_HEADS
Q_LOCAL = KV_LOCAL * GROUP
TAIL = WMAX - 1
KV_COLUMNS = 2 * KV_LOCAL * HEAD_DIMENSION
PAIR = 2
D = HEAD_DIMENSION
B = BLOCK_TOKENS
SCALE = 1.0 / math.sqrt(HEAD_DIMENSION)
EXP2_SCALE = SCALE * math.log2(math.e)
META_CORE = 1 + 2 * Q_LOCAL
MIB = 1024 * 1024
F32 = jnp.float32
BF16 = jnp.bfloat16


ANY = pl.BlockSpec(memory_space=pl.ANY)
SMALL = pltpu.CompilerParams(vmem_limit_bytes=6 * MIB)


def split_pair(first, second):
    width = first.shape[1] // ROW

    def body(a, b, out, held, sem_in, sem_out):
        reads = []
        for i in range(ROW):
            columns = slice(i * width, (i + 1) * width)
            reads.append(
                pltpu.make_async_copy(a.at[:, columns], held.at[i, :, :width], sem_in.at[2 * i])
            )
            reads.append(
                pltpu.make_async_copy(b.at[:, columns], held.at[i, :, width:], sem_in.at[2 * i + 1])
            )
        for copy in reads:
            copy.start()
        writes = []
        for i in range(ROW):
            reads[2 * i].wait()
            reads[2 * i + 1].wait()
            writes.append(pltpu.make_async_copy(held.at[i], out.at[i], sem_out.at[i]))
            writes[-1].start()
        for copy in writes:
            copy.wait()

    shape = (ROW, B, 2 * width)
    return pl.pallas_call(
        body,
        in_specs=[ANY, ANY],
        out_specs=ANY,
        out_shape=jax.ShapeDtypeStruct(shape, first.dtype),
        scratch_shapes=[
            pltpu.VMEM(shape, first.dtype),
            pltpu.SemaphoreType.DMA((2 * ROW,)),
            pltpu.SemaphoreType.DMA((ROW,)),
        ],
    )(first, second)


def join_columns(parts, width):
    def body(src, out, held, sem_in, sem_out):
        reads = [
            pltpu.make_async_copy(src.at[i, :, :width], held.at[i], sem_in.at[i])
            for i in range(ROW)
        ]
        for copy in reads:
            copy.start()
        writes = []
        for i in range(ROW):
            reads[i].wait()
            columns = slice(i * width, (i + 1) * width)
            writes.append(pltpu.make_async_copy(held.at[i], out.at[:, columns], sem_out.at[i]))
            writes[-1].start()
        for copy in writes:
            copy.wait()

    return pl.pallas_call(
        body,
        in_specs=[ANY],
        out_specs=ANY,
        out_shape=jax.ShapeDtypeStruct((B, ROW * width), parts.dtype),
        scratch_shapes=[
            pltpu.VMEM((ROW, B, width), parts.dtype),
            pltpu.SemaphoreType.DMA((ROW,)),
            pltpu.SemaphoreType.DMA((ROW,)),
        ],
        compiler_params=SMALL,
    )(parts)


def with_key_grads(dq, own, tail):
    def body(_, own_ref, tail_ref, out):
        for b in range(ROW):
            for n in range(2 * KV_LOCAL):
                g, which = divmod(n, 2)
                total = own_ref[g, which, b * B : (b + 1) * B]
                if b >= ROW - TAIL:
                    start = (b - (ROW - TAIL)) * B
                    total = total + tail_ref[g, which, start : start + B].astype(F32)
                out[b, :, n * D : (n + 1) * D] = total.astype(BF16)

    return pl.pallas_call(
        body,
        grid=(1,),
        in_specs=[
            ANY,
            pl.BlockSpec(own.shape, lambda i: (0, 0, 0, 0)),
            pl.BlockSpec(tail.shape, lambda i: (0, 0, 0, 0)),
        ],
        out_specs=pl.BlockSpec((ROW, B, KV_COLUMNS), lambda i: (0, 0, Q_LOCAL * D // KV_COLUMNS)),
        out_shape=jax.ShapeDtypeStruct(dq.shape, dq.dtype),
        input_output_aliases={0: 0},
        compiler_params=SMALL,
    )(dq, own, tail)


def join_pair(parts, pieces):
    def body(src, *refs):
        extra = refs[:ROW]
        for i in range(ROW):
            for n in range(2 * KV_LOCAL):
                g, which = divmod(n, 2)
                out = refs[ROW + which]
                total = src[i, :, n * D : (n + 1) * D].astype(F32) + extra[i][g, which].astype(F32)
                h = i * KV_LOCAL + g
                out[:, h * D : (h + 1) * D] = total.astype(out.dtype)

    piece = pl.BlockSpec(pieces[0].shape, lambda i: (0, 0, 0, 0))
    width = KEY_VALUE_HEADS * D
    out = jax.ShapeDtypeStruct((B, width), parts.dtype)
    return pl.pallas_call(
        body,
        grid=(1,),
        in_specs=[
            pl.BlockSpec((ROW, B, KV_COLUMNS), lambda i: (0, 0, Q_LOCAL * D // KV_COLUMNS))
        ]
        + [piece] * ROW,
        out_specs=[pl.BlockSpec((B, width), lambda i: (0, 0))] * 2,
        out_shape=[out, out],
        compiler_params=SMALL,
    )(parts, *pieces)


def dot(a, b, ca, cb):
    return lax.dot_general(a, b, (((ca,), (cb,)), ((), ())), preferred_element_type=F32)


def attention_body(
    meta, q_ref, go_ref, k_ref, v_ref, tk_ref, tv_ref, sk_ref, sv_ref, ok_ref, ov_ref,
    dq_ref, own_ref, tail_ref, sink_ref, ks, vs, ssk, ssv, kst, sst, acc, sacc,
):
    g = pl.program_id(0)
    i = pl.program_id(1)

    @pl.when(i == 0)
    def _():
        ks[: TAIL * B] = tk_ref[...].reshape(TAIL * B, D)
        ks[TAIL * B :] = k_ref[...].reshape(ROW * B, D)
        vs[: TAIL * B] = tv_ref[...].reshape(TAIL * B, D)
        vs[TAIL * B :] = v_ref[...].reshape(ROW * B, D)
        near = pl.ds(pl.multiple_of(meta[META_CORE] * B, B), B)
        far = pl.ds(pl.multiple_of((1 - meta[META_CORE]) * B, B), B)
        ssk[near, :] = sk_ref[...]
        ssv[near, :] = sv_ref[...]
        ssk[far, :] = ok_ref[...]
        ssv[far, :] = ov_ref[...]
        kst[...] = ks[...].T
        sst[...] = ssk[...].T
        acc[...] = jnp.zeros_like(acc)
        sacc[...] = jnp.zeros_like(sacc)

    block = meta[0] + i
    rows = pl.ds(pl.multiple_of(i * B, B), WMAX * B)
    kw = ks[rows, :]
    vw = vs[rows, :]
    kwt = kst[:, rows]
    ksink = ssk[...]
    vsink = ssv[...]
    ksinkt = sst[...]
    key = lax.broadcasted_iota(jnp.int32, (B, PAIR * B), 0)
    query = lax.broadcasted_iota(jnp.int32, (B, PAIR * B), 1) % B
    causal = key <= query

    def bias(allowed):
        return jnp.concatenate(
            [jnp.full((1, B), jnp.where(ok, 0.0, NEG_FILL), F32) for ok in allowed], 1
        )

    pairs = [range(first, first + PAIR) for first in range(0, GROUP, PAIR)]
    first_products = []
    for heads in pairs:
        q2 = jnp.concatenate([q_ref[0, :, h * D : (h + 1) * D] for h in heads], 0)
        go2 = jnp.concatenate([go_ref[0, :, h * D : (h + 1) * D] for h in heads], 0)
        sw = dot(kw, q2, 1, 1)
        ss = dot(ksink, q2, 1, 1)
        pw = dot(vw, go2, 1, 1)
        ps = dot(vsink, go2, 1, 1)
        scores = [sw[j * B : (j + 1) * B] for j in range(WMAX)]
        scores[TAIL] = jnp.where(causal, scores[TAIL], NEG_FILL)
        scores += [ss[t * B : (t + 1) * B] for t in range(SMAX)]
        grads = [pw[j * B : (j + 1) * B] for j in range(WMAX)]
        grads += [ps[t * B : (t + 1) * B] for t in range(SMAX)]
        first_products.append((q2, go2, scores, grads))

    softmaxes = []
    for heads, (_, _, scores, grads) in zip(pairs, first_products):
        window = [meta[1 + g * GROUP + h] for h in heads]
        sink = [meta[1 + Q_LOCAL + g * GROUP + h] for h in heads]
        biases = [
            bias([(block >= TAIL - j) & (TAIL - j < w) for w in window]) for j in range(TAIL)
        ]
        biases += [jnp.zeros((1, PAIR * B), F32)]
        biases += [
            bias([(t < c) & (t <= block - w) for w, c in zip(window, sink)]) for t in range(SMAX)
        ]
        tops = [
            jnp.max(s, 0, keepdims=True) * EXP2_SCALE + extra for s, extra in zip(scores, biases)
        ]
        top = tops[0]
        for t in tops[1:]:
            top = jnp.maximum(top, t)
        exps = [jnp.exp2(s * EXP2_SCALE - (top - extra)) for s, extra in zip(scores, biases)]
        total = exps[0]
        product = exps[0] * grads[0]
        for e, p in zip(exps[1:], grads[1:]):
            total = total + e
            product = product + e * p
        inverse = 1.0 / jnp.sum(total, 0, keepdims=True)
        row_dot = jnp.sum(product, 0, keepdims=True) * inverse
        weights = [e * inverse for e in exps]
        rounded = [w.astype(BF16) for w in weights]
        dscores = [(w * (p - row_dot)).astype(BF16) for w, p in zip(weights, grads)]
        softmaxes.append(
            [
                jnp.concatenate(rows, 0)
                for rows in (rounded[:WMAX], rounded[WMAX:], dscores[:WMAX], dscores[WMAX:])
            ]
        )

    sums = []
    for heads, (q2, go2, _, _), (wb_window, wb_sink, ds_window, ds_sink) in zip(
        pairs, first_products, softmaxes
    ):
        sums.append(
            [
                dot(ds_window, q2, 1, 0),
                dot(wb_window, go2, 1, 0),
                dot(ds_sink, q2, 1, 0),
                dot(wb_sink, go2, 1, 0),
            ]
        )
        dqt = (dot(kwt, ds_window, 1, 0) + dot(ksinkt, ds_sink, 1, 0)) * SCALE
        for n, h in enumerate(heads):
            dq_ref[0, :, h * D : (h + 1) * D] = dqt[:, n * B : (n + 1) * B].T.astype(BF16)
    acc[0, rows, :] += sums[0][0] + sums[1][0]
    acc[1, rows, :] += sums[0][1] + sums[1][1]
    sacc[0] += sums[0][2] + sums[1][2]
    sacc[1] += sums[0][3] + sums[1][3]

    @pl.when(i == ROW - 1)
    def _():
        own_ref[0, 0] = acc[0, TAIL * B :] * SCALE
        own_ref[0, 1] = acc[1, TAIL * B :]
        tail_ref[0, 0] = (acc[0, : TAIL * B] * SCALE).astype(BF16)
        tail_ref[0, 1] = acc[1, : TAIL * B].astype(BF16)
        for t in range(SMAX):
            sink_ref[t, 0, 0] = sacc[0, t * B : (t + 1) * B] * SCALE
            sink_ref[t, 0, 1] = sacc[1, t * B : (t + 1) * B]


def attention(meta, qgo, kv, tail, sink, other, interpret=False):
    wide = pl.BlockSpec((1, B, GROUP * D), lambda g, i, m: (i, 0, g))
    wide_go = pl.BlockSpec((1, B, GROUP * D), lambda g, i, m: (i, 0, KV_LOCAL + g))

    def pair(count):
        return [
            pl.BlockSpec((count, B, D), lambda g, i, m: (0, 0, g)),
            pl.BlockSpec((count, B, D), lambda g, i, m: (0, 0, KV_LOCAL + g)),
        ]

    one = [
        pl.BlockSpec((B, D), lambda g, i, m: (0, g)),
        pl.BlockSpec((B, D), lambda g, i, m: (0, KV_LOCAL + g)),
    ]

    def result(rows, dtype):
        return (
            pl.BlockSpec((1, 2, rows * B, D), lambda g, i, m: (g, 0, 0, 0)),
            jax.ShapeDtypeStruct((KV_LOCAL, 2, rows * B, D), dtype),
        )

    results = [
        (wide, jax.ShapeDtypeStruct((ROW, B, Q_LOCAL * D + KV_COLUMNS), BF16)),
        result(ROW, F32),
        result(TAIL, BF16),
        (
            pl.BlockSpec((SMAX, 1, 2, B, D), lambda g, i, m: (0, g, 0, 0, 0)),
            jax.ShapeDtypeStruct((SMAX, KV_LOCAL, 2, B, D), F32),
        ),
    ]
    return pl.pallas_call(
        attention_body,
        grid_spec=pltpu.PrefetchScalarGridSpec(
            num_scalar_prefetch=1,
            grid=(KV_LOCAL, ROW),
            in_specs=[wide, wide_go] + pair(ROW) + pair(TAIL) + one + one,
            out_specs=[r[0] for r in results],
            scratch_shapes=[
                pltpu.VMEM(((TAIL + ROW) * B, D), BF16),
                pltpu.VMEM(((TAIL + ROW) * B, D), BF16),
                pltpu.VMEM((SMAX * B, D), BF16),
                pltpu.VMEM((SMAX * B, D), BF16),
                pltpu.VMEM((D, (TAIL + ROW) * B), BF16),
                pltpu.VMEM((D, SMAX * B), BF16),
                pltpu.VMEM((2, (TAIL + ROW) * B, D), F32),
                pltpu.VMEM((2, SMAX * B, D), F32),
            ],
        ),
        out_shape=[r[1] for r in results],
        compiler_params=pltpu.CompilerParams(vmem_limit_bytes=48 * MIB),
        interpret=interpret,
    )(meta, qgo, qgo, kv, kv, tail, tail, sink, sink, other, other)


def line(y, z, core):
    return ((z % 4 * 8 + y) * 2 + z // 4) * 2 + core


def moved(moves):
    return [(line(*p, 0), line(*q, 0)) for p, q in moves] + [
        (line(*p[::-1], 1), line(*q[::-1], 1)) for p, q in moves
    ]


ROUNDS = (((4, 0), (2, 0), (6, 0)), ((0, 4), (1, 4), (1, 0)), ((0, 2), (0, 1), (0, 7)))


def spread():
    holders = [(0, 0)]
    rounds = []
    for offsets in ROUNDS:
        moves = [
            [((a, b), ((a + da) % 8, (b + db) % 8)) for a, b in holders] for da, db in offsets
        ]
        rounds.append([moved(m) for m in moves])
        holders = holders + [q for m in moves for _, q in m]
    return rounds


def gather():
    order = (1, 2, 4, 3, 5, 6, 7)
    return [
        [moved([((a, o), (a, 0)) for a in range(8)]) for o in order],
        [moved([((o, 0), (0, 0))]) for o in order],
    ]


def exchanged(value, axes):
    return lax.all_to_all(value, axes, split_axis=0, concat_axis=0, tiled=False)


def summed(total, permutes):
    send = total.astype(BF16)
    for got in [lax.ppermute(send, LINE, pairs) for pairs in permutes]:
        total = total + got.astype(F32)
    return total


def after(value, *others):
    return lax.optimization_barrier((value, others))[0]


def shards(queries, keys, values, output_gradient, windows, sinks):
    core = lax.axis_index("core")
    run = lax.axis_index(("y", "zh", "core")) * 4 + lax.axis_index("zl")
    x = lax.axis_index("x")
    meta = jnp.concatenate(
        [
            (run * ROW)[None].astype(jnp.int32),
            lax.dynamic_slice_in_dim(windows, x * Q_LOCAL, Q_LOCAL),
            lax.dynamic_slice_in_dim(sinks, x * Q_LOCAL, Q_LOCAL),
            core[None].astype(jnp.int32),
        ]
    )
    runs = [(run // 4 // 4, run // 4 // 2 % 2 * 4 + run % 4, run // 4 % 2) for run in range(128)]
    to_next = [(line(*a), line(*b)) for a, b in zip(runs[:-1], runs[1:])]
    swap = [(0, 1), (1, 0)]

    kv_split = split_pair(keys[0], values[0])
    qgo_split = split_pair(after(queries[0], kv_split), output_gradient[0])
    kv = after(exchanged(kv_split, "x"), qgo_split)
    qgo = exchanged(qgo_split, "x")
    tail = lax.ppermute(kv[ROW - TAIL :], LINE, to_next)
    sink = lax.ppermute(kv[1], LINE, [(line(0, 0, 0), line(0, 0, 1))])
    sink = jnp.where(run == 0, kv[0], sink)
    for step, permutes in enumerate(spread()):
        if step == 2:
            sink = after(sink, tail)
        got = [lax.ppermute(sink, LINE, pairs) for pairs in permutes]
        sink = sink + got[0] + got[1] + got[2]
    other = lax.ppermute(sink, "core", swap)
    dq, own, tail_grad, sink_grad = attention(meta, qgo, kv, tail, sink, other)

    tail_back = lax.ppermute(tail_grad, LINE, [(b, a) for a, b in to_next])
    total = lax.dynamic_index_in_dim(sink_grad, core, 0, False)
    away = lax.dynamic_index_in_dim(sink_grad, 1 - core, 0, False).astype(BF16)
    total = total + lax.ppermute(away, "core", swap).astype(F32)
    along_second, along_first = gather()
    total = summed(total, along_second)
    grads = with_key_grads(dq, own, after(tail_back, total))
    parts = exchanged(grads, "x")
    dq_tokens = join_columns(parts, Q_LOCAL * D)
    total = summed(after(total, grads), along_first)
    total = after(total, parts)
    total = total.astype(BF16)

    def at(x, core):
        return x * 32 + core

    pieces = [
        lax.ppermute(total, AXES, [(at(j, c), at(c, 0)) for c in range(SMAX)]) for j in range(ROW)
    ]
    dk, dv = join_pair(parts, pieces)
    return dq_tokens[None], dk[None], dv[None]


def solution(mesh):
    split = Mesh(mesh.devices.reshape(SIZES), AXES)
    tokens = P(("y", "zh", "core"), ("zl", "x"), None)
    return jax.shard_map(
        shards,
        mesh=split,
        in_specs=(tokens, tokens, tokens, tokens, P(), P()),
        out_specs=(tokens, tokens, tokens),
        check_vma=False,
    )
```

```python
import math

import jax
import jax.numpy as jnp
from jax import lax
from jax.experimental import pallas as pl
from jax.experimental.pallas import tpu as pltpu
from jax.sharding import Mesh, PartitionSpec as P

QUERY_HEADS = 32
KEY_VALUE_HEADS = 8
HEAD_DIMENSION = 128
BLOCK_TOKENS = 128
WMAX = 4
SMAX = 2
NEG_FILL = -1e30

AXES = ("zl", "x", "y", "zh", "core")
SIZES = (4, 4, 8, 2, 2)
LINE = ("zl", "y", "zh", "core")
ROW = 4
KV_LOCAL = KEY_VALUE_HEADS // ROW
GROUP = QUERY_HEADS // KEY_VALUE_HEADS
Q_LOCAL = KV_LOCAL * GROUP
TAIL = WMAX - 1
KV_COLUMNS = 2 * KV_LOCAL * HEAD_DIMENSION
PAIR = 2
D = HEAD_DIMENSION
B = BLOCK_TOKENS
SCALE = 1.0 / math.sqrt(HEAD_DIMENSION)
EXP2_SCALE = SCALE * math.log2(math.e)
META_CORE = 1 + 2 * Q_LOCAL
MIB = 1024 * 1024
F32 = jnp.float32
BF16 = jnp.bfloat16


ANY = pl.BlockSpec(memory_space=pl.ANY)
SMALL = pltpu.CompilerParams(vmem_limit_bytes=6 * MIB)


def split_pair(first, second):
    width = first.shape[1] // ROW

    def body(a, b, out, held, sem_in, sem_out):
        reads = []
        for i in range(ROW):
            columns = slice(i * width, (i + 1) * width)
            reads.append(
                pltpu.make_async_copy(a.at[:, columns], held.at[i, :, :width], sem_in.at[2 * i])
            )
            reads.append(
                pltpu.make_async_copy(b.at[:, columns], held.at[i, :, width:], sem_in.at[2 * i + 1])
            )
        for copy in reads:
            copy.start()
        writes = []
        for i in range(ROW):
            reads[2 * i].wait()
            reads[2 * i + 1].wait()
            writes.append(pltpu.make_async_copy(held.at[i], out.at[i], sem_out.at[i]))
            writes[-1].start()
        for copy in writes:
            copy.wait()

    shape = (ROW, B, 2 * width)
    return pl.pallas_call(
        body,
        in_specs=[ANY, ANY],
        out_specs=ANY,
        out_shape=jax.ShapeDtypeStruct(shape, first.dtype),
        scratch_shapes=[
            pltpu.VMEM(shape, first.dtype),
            pltpu.SemaphoreType.DMA((2 * ROW,)),
            pltpu.SemaphoreType.DMA((ROW,)),
        ],
    )(first, second)


def join_columns(parts, width):
    def body(src, out, held, sem_in, sem_out):
        reads = [
            pltpu.make_async_copy(src.at[i, :, :width], held.at[i], sem_in.at[i])
            for i in range(ROW)
        ]
        for copy in reads:
            copy.start()
        writes = []
        for i in range(ROW):
            reads[i].wait()
            columns = slice(i * width, (i + 1) * width)
            writes.append(pltpu.make_async_copy(held.at[i], out.at[:, columns], sem_out.at[i]))
            writes[-1].start()
        for copy in writes:
            copy.wait()

    return pl.pallas_call(
        body,
        in_specs=[ANY],
        out_specs=ANY,
        out_shape=jax.ShapeDtypeStruct((B, ROW * width), parts.dtype),
        scratch_shapes=[
            pltpu.VMEM((ROW, B, width), parts.dtype),
            pltpu.SemaphoreType.DMA((ROW,)),
            pltpu.SemaphoreType.DMA((ROW,)),
        ],
        compiler_params=SMALL,
    )(parts)


def with_key_grads(dq, own, tail):
    def body(_, own_ref, tail_ref, out):
        for b in range(ROW):
            for n in range(2 * KV_LOCAL):
                g, which = divmod(n, 2)
                total = own_ref[g, which, b * B : (b + 1) * B]
                if b >= ROW - TAIL:
                    start = (b - (ROW - TAIL)) * B
                    total = total + tail_ref[g, which, start : start + B].astype(F32)
                out[b, :, n * D : (n + 1) * D] = total.astype(BF16)

    return pl.pallas_call(
        body,
        grid=(1,),
        in_specs=[
            ANY,
            pl.BlockSpec(own.shape, lambda i: (0, 0, 0, 0)),
            pl.BlockSpec(tail.shape, lambda i: (0, 0, 0, 0)),
        ],
        out_specs=pl.BlockSpec((ROW, B, KV_COLUMNS), lambda i: (0, 0, Q_LOCAL * D // KV_COLUMNS)),
        out_shape=jax.ShapeDtypeStruct(dq.shape, dq.dtype),
        input_output_aliases={0: 0},
        compiler_params=SMALL,
    )(dq, own, tail)


def join_pair(parts, pieces):
    def body(src, *refs):
        extra = refs[:ROW]
        for i in range(ROW):
            for n in range(2 * KV_LOCAL):
                g, which = divmod(n, 2)
                out = refs[ROW + which]
                total = src[i, :, n * D : (n + 1) * D].astype(F32) + extra[i][g, which].astype(F32)
                h = i * KV_LOCAL + g
                out[:, h * D : (h + 1) * D] = total.astype(out.dtype)

    piece = pl.BlockSpec(pieces[0].shape, lambda i: (0, 0, 0, 0))
    width = KEY_VALUE_HEADS * D
    out = jax.ShapeDtypeStruct((B, width), parts.dtype)
    return pl.pallas_call(
        body,
        grid=(1,),
        in_specs=[
            pl.BlockSpec((ROW, B, KV_COLUMNS), lambda i: (0, 0, Q_LOCAL * D // KV_COLUMNS))
        ]
        + [piece] * ROW,
        out_specs=[pl.BlockSpec((B, width), lambda i: (0, 0))] * 2,
        out_shape=[out, out],
        compiler_params=SMALL,
    )(parts, *pieces)


def dot(a, b, ca, cb):
    return lax.dot_general(a, b, (((ca,), (cb,)), ((), ())), preferred_element_type=F32)


def attention_body(
    meta, q_ref, go_ref, k_ref, v_ref, tk_ref, tv_ref, sk_ref, sv_ref, ok_ref, ov_ref,
    dq_ref, own_ref, tail_ref, sink_ref, ks, vs, ssk, ssv, kst, sst, acc, sacc,
):
    g = pl.program_id(0)
    i = pl.program_id(1)

    @pl.when(i == 0)
    def _():
        ks[: TAIL * B] = tk_ref[...].reshape(TAIL * B, D)
        ks[TAIL * B :] = k_ref[...].reshape(ROW * B, D)
        vs[: TAIL * B] = tv_ref[...].reshape(TAIL * B, D)
        vs[TAIL * B :] = v_ref[...].reshape(ROW * B, D)
        near = pl.ds(pl.multiple_of(meta[META_CORE] * B, B), B)
        far = pl.ds(pl.multiple_of((1 - meta[META_CORE]) * B, B), B)
        ssk[near, :] = sk_ref[...]
        ssv[near, :] = sv_ref[...]
        ssk[far, :] = ok_ref[...]
        ssv[far, :] = ov_ref[...]
        kst[...] = ks[...].T
        sst[...] = ssk[...].T
        acc[...] = jnp.zeros_like(acc)
        sacc[...] = jnp.zeros_like(sacc)

    block = meta[0] + i
    rows = pl.ds(pl.multiple_of(i * B, B), WMAX * B)
    kw = ks[rows, :]
    vw = vs[rows, :]
    kwt = kst[:, rows]
    ksink = ssk[...]
    vsink = ssv[...]
    ksinkt = sst[...]
    key = lax.broadcasted_iota(jnp.int32, (B, PAIR * B), 0)
    query = lax.broadcasted_iota(jnp.int32, (B, PAIR * B), 1) % B
    causal = key <= query

    def bias(allowed):
        return jnp.concatenate(
            [jnp.full((1, B), jnp.where(ok, 0.0, NEG_FILL), F32) for ok in allowed], 1
        )

    pairs = [range(first, first + PAIR) for first in range(0, GROUP, PAIR)]
    first_products = []
    for heads in pairs:
        q2 = jnp.concatenate([q_ref[0, :, h * D : (h + 1) * D] for h in heads], 0)
        go2 = jnp.concatenate([go_ref[0, :, h * D : (h + 1) * D] for h in heads], 0)
        sw = dot(kw, q2, 1, 1)
        ss = dot(ksink, q2, 1, 1)
        pw = dot(vw, go2, 1, 1)
        ps = dot(vsink, go2, 1, 1)
        scores = [sw[j * B : (j + 1) * B] for j in range(WMAX)]
        scores[TAIL] = jnp.where(causal, scores[TAIL], NEG_FILL)
        scores += [ss[t * B : (t + 1) * B] for t in range(SMAX)]
        grads = [pw[j * B : (j + 1) * B] for j in range(WMAX)]
        grads += [ps[t * B : (t + 1) * B] for t in range(SMAX)]
        first_products.append((q2, go2, scores, grads))

    softmaxes = []
    for heads, (_, _, scores, grads) in zip(pairs, first_products):
        window = [meta[1 + g * GROUP + h] for h in heads]
        sink = [meta[1 + Q_LOCAL + g * GROUP + h] for h in heads]
        biases = [
            bias([(block >= TAIL - j) & (TAIL - j < w) for w in window]) for j in range(TAIL)
        ]
        biases += [jnp.zeros((1, PAIR * B), F32)]
        biases += [
            bias([(t < c) & (t <= block - w) for w, c in zip(window, sink)]) for t in range(SMAX)
        ]
        tops = [
            jnp.max(s, 0, keepdims=True) * EXP2_SCALE + extra for s, extra in zip(scores, biases)
        ]
        top = tops[0]
        for t in tops[1:]:
            top = jnp.maximum(top, t)
        exps = [jnp.exp2(s * EXP2_SCALE - (top - extra)) for s, extra in zip(scores, biases)]
        total = exps[0]
        product = exps[0] * grads[0]
        for e, p in zip(exps[1:], grads[1:]):
            total = total + e
            product = product + e * p
        inverse = 1.0 / jnp.sum(total, 0, keepdims=True)
        row_dot = jnp.sum(product, 0, keepdims=True) * inverse
        weights = [e * inverse for e in exps]
        rounded = [w.astype(BF16) for w in weights]
        dscores = [(w * (p - row_dot)).astype(BF16) for w, p in zip(weights, grads)]
        softmaxes.append(
            [
                jnp.concatenate(rows, 0)
                for rows in (rounded[:WMAX], rounded[WMAX:], dscores[:WMAX], dscores[WMAX:])
            ]
        )

    sums = []
    for heads, (q2, go2, _, _), (wb_window, wb_sink, ds_window, ds_sink) in zip(
        pairs, first_products, softmaxes
    ):
        sums.append(
            [
                dot(ds_window, q2, 1, 0),
                dot(wb_window, go2, 1, 0),
                dot(ds_sink, q2, 1, 0),
                dot(wb_sink, go2, 1, 0),
            ]
        )
        dqt = (dot(kwt, ds_window, 1, 0) + dot(ksinkt, ds_sink, 1, 0)) * SCALE
        for n, h in enumerate(heads):
            dq_ref[0, :, h * D : (h + 1) * D] = dqt[:, n * B : (n + 1) * B].T.astype(BF16)
    acc[0, rows, :] += sums[0][0] + sums[1][0]
    acc[1, rows, :] += sums[0][1] + sums[1][1]
    sacc[0] += sums[0][2] + sums[1][2]
    sacc[1] += sums[0][3] + sums[1][3]

    @pl.when(i == ROW - 1)
    def _():
        own_ref[0, 0] = acc[0, TAIL * B :] * SCALE
        own_ref[0, 1] = acc[1, TAIL * B :]
        tail_ref[0, 0] = (acc[0, : TAIL * B] * SCALE).astype(BF16)
        tail_ref[0, 1] = acc[1, : TAIL * B].astype(BF16)
        for t in range(SMAX):
            sink_ref[t, 0, 0] = sacc[0, t * B : (t + 1) * B] * SCALE
            sink_ref[t, 0, 1] = sacc[1, t * B : (t + 1) * B]


def attention(meta, qgo, kv, tail, sink, other, interpret=False):
    wide = pl.BlockSpec((1, B, GROUP * D), lambda g, i, m: (i, 0, g))
    wide_go = pl.BlockSpec((1, B, GROUP * D), lambda g, i, m: (i, 0, KV_LOCAL + g))

    def pair(count):
        return [
            pl.BlockSpec((count, B, D), lambda g, i, m: (0, 0, g)),
            pl.BlockSpec((count, B, D), lambda g, i, m: (0, 0, KV_LOCAL + g)),
        ]

    one = [
        pl.BlockSpec((B, D), lambda g, i, m: (0, g)),
        pl.BlockSpec((B, D), lambda g, i, m: (0, KV_LOCAL + g)),
    ]

    def result(rows, dtype):
        return (
            pl.BlockSpec((1, 2, rows * B, D), lambda g, i, m: (g, 0, 0, 0)),
            jax.ShapeDtypeStruct((KV_LOCAL, 2, rows * B, D), dtype),
        )

    results = [
        (wide, jax.ShapeDtypeStruct((ROW, B, Q_LOCAL * D + KV_COLUMNS), BF16)),
        result(ROW, F32),
        result(TAIL, BF16),
        (
            pl.BlockSpec((SMAX, 1, 2, B, D), lambda g, i, m: (0, g, 0, 0, 0)),
            jax.ShapeDtypeStruct((SMAX, KV_LOCAL, 2, B, D), F32),
        ),
    ]
    return pl.pallas_call(
        attention_body,
        grid_spec=pltpu.PrefetchScalarGridSpec(
            num_scalar_prefetch=1,
            grid=(KV_LOCAL, ROW),
            in_specs=[wide, wide_go] + pair(ROW) + pair(TAIL) + one + one,
            out_specs=[r[0] for r in results],
            scratch_shapes=[
                pltpu.VMEM(((TAIL + ROW) * B, D), BF16),
                pltpu.VMEM(((TAIL + ROW) * B, D), BF16),
                pltpu.VMEM((SMAX * B, D), BF16),
                pltpu.VMEM((SMAX * B, D), BF16),
                pltpu.VMEM((D, (TAIL + ROW) * B), BF16),
                pltpu.VMEM((D, SMAX * B), BF16),
                pltpu.VMEM((2, (TAIL + ROW) * B, D), F32),
                pltpu.VMEM((2, SMAX * B, D), F32),
            ],
        ),
        out_shape=[r[1] for r in results],
        compiler_params=pltpu.CompilerParams(vmem_limit_bytes=48 * MIB),
        interpret=interpret,
    )(meta, qgo, qgo, kv, kv, tail, tail, sink, sink, other, other)


def line(y, z, core):
    return ((z % 4 * 8 + y) * 2 + z // 4) * 2 + core


def moved(moves):
    return [(line(*p, 0), line(*q, 0)) for p, q in moves] + [
        (line(*p[::-1], 1), line(*q[::-1], 1)) for p, q in moves
    ]


ROUNDS = (((4, 0), (2, 0), (6, 0)), ((0, 4), (1, 4), (1, 0)), ((0, 2), (0, 1), (0, 7)))


def spread():
    holders = [(0, 0)]
    rounds = []
    for offsets in ROUNDS:
        moves = [
            [((a, b), ((a + da) % 8, (b + db) % 8)) for a, b in holders] for da, db in offsets
        ]
        rounds.append([moved(m) for m in moves])
        holders = holders + [q for m in moves for _, q in m]
    return rounds


def gather():
    order = (1, 2, 4, 3, 5, 6, 7)
    cores = range(2)
    return [
        [[(line(o, z, c), line(0, z, c)) for z in range(8) for c in cores] for o in order],
        [[(line(0, o, c), line(0, 0, c)) for c in cores] for o in order],
    ]


def exchanged(value, axes):
    return lax.all_to_all(value, axes, split_axis=0, concat_axis=0, tiled=False)


def summed(total, permutes):
    send = total.astype(BF16)
    for got in [lax.ppermute(send, LINE, pairs) for pairs in permutes]:
        total = total + got.astype(F32)
    return total


def after(value, *others):
    return lax.optimization_barrier((value, others))[0]


def shards(queries, keys, values, output_gradient, windows, sinks):
    core = lax.axis_index("core")
    run = lax.axis_index(("y", "zh", "core")) * 4 + lax.axis_index("zl")
    x = lax.axis_index("x")
    meta = jnp.concatenate(
        [
            (run * ROW)[None].astype(jnp.int32),
            lax.dynamic_slice_in_dim(windows, x * Q_LOCAL, Q_LOCAL),
            lax.dynamic_slice_in_dim(sinks, x * Q_LOCAL, Q_LOCAL),
            core[None].astype(jnp.int32),
        ]
    )
    runs = [(run // 4 // 4, run // 4 // 2 % 2 * 4 + run % 4, run // 4 % 2) for run in range(128)]
    to_next = [(line(*a), line(*b)) for a, b in zip(runs[:-1], runs[1:])]
    swap = [(0, 1), (1, 0)]

    kv_split = split_pair(keys[0], values[0])
    qgo_split = split_pair(after(queries[0], kv_split), output_gradient[0])
    kv = after(exchanged(kv_split, "x"), qgo_split)
    qgo = exchanged(qgo_split, "x")
    tail = lax.ppermute(kv[ROW - TAIL :], LINE, to_next)
    sink = lax.ppermute(kv[1], LINE, [(line(0, 0, 0), line(0, 0, 1))])
    sink = jnp.where(run == 0, kv[0], sink)
    for step, permutes in enumerate(spread()):
        if step == 2:
            sink = after(sink, tail)
        got = [lax.ppermute(sink, LINE, pairs) for pairs in permutes]
        sink = sink + got[0] + got[1] + got[2]
    other = lax.ppermute(sink, "core", swap)
    dq, own, tail_grad, sink_grad = attention(meta, qgo, kv, tail, sink, other)

    tail_back = lax.ppermute(tail_grad, LINE, [(b, a) for a, b in to_next])
    total = lax.dynamic_index_in_dim(sink_grad, core, 0, False)
    away = lax.dynamic_index_in_dim(sink_grad, 1 - core, 0, False).astype(BF16)
    total = total + lax.ppermute(away, "core", swap).astype(F32)
    along_y, along_z = gather()
    total = summed(total, along_y)
    grads = with_key_grads(dq, own, after(tail_back, total))
    parts = exchanged(grads, "x")
    dq_tokens = join_columns(parts, Q_LOCAL * D)
    total = summed(after(total, grads), along_z)
    total = after(total, parts)
    total = total.astype(BF16)

    def at(x, core):
        return x * 32 + core

    pieces = [
        lax.ppermute(total, AXES, [(at(j, c), at(c, 0)) for c in range(SMAX)]) for j in range(ROW)
    ]
    dk, dv = join_pair(parts, pieces)
    return dq_tokens[None], dk[None], dv[None]


def solution(mesh):
    split = Mesh(mesh.devices.reshape(SIZES), AXES)
    tokens = P(("y", "zh", "core"), ("zl", "x"), None)
    return jax.shard_map(
        shards,
        mesh=split,
        in_specs=(tokens, tokens, tokens, tokens, P(), P()),
        out_specs=(tokens, tokens, tokens),
        check_vma=False,
    )
```

```python
import math

import jax
import jax.numpy as jnp
from jax import lax
from jax.experimental import pallas as pl
from jax.experimental.pallas import tpu as pltpu
from jax.sharding import Mesh, PartitionSpec as P

QUERY_HEADS = 32
KEY_VALUE_HEADS = 8
HEAD_DIMENSION = 128
BLOCK_TOKENS = 128
WMAX = 4
SMAX = 2
NEG_FILL = -1e30

AXES = ("zl", "x", "y", "zh", "core")
SIZES = (4, 4, 8, 2, 2)
LINE = ("zl", "y", "zh", "core")
ROW = 4
KV_LOCAL = KEY_VALUE_HEADS // ROW
GROUP = QUERY_HEADS // KEY_VALUE_HEADS
Q_LOCAL = KV_LOCAL * GROUP
TAIL = WMAX - 1
KV_COLUMNS = 2 * KV_LOCAL * HEAD_DIMENSION
PAIR = 2
D = HEAD_DIMENSION
B = BLOCK_TOKENS
SCALE = 1.0 / math.sqrt(HEAD_DIMENSION)
EXP2_SCALE = SCALE * math.log2(math.e)
META_CORE = 1 + 2 * Q_LOCAL
MIB = 1024 * 1024
F32 = jnp.float32
BF16 = jnp.bfloat16


ANY = pl.BlockSpec(memory_space=pl.ANY)
SMALL = pltpu.CompilerParams(vmem_limit_bytes=6 * MIB)


def split_pair(first, second):
    width = first.shape[1] // ROW

    def body(a, b, out, held, sem_in, sem_out):
        reads = []
        for i in range(ROW):
            columns = slice(i * width, (i + 1) * width)
            reads.append(
                pltpu.make_async_copy(a.at[:, columns], held.at[i, :, :width], sem_in.at[2 * i])
            )
            reads.append(
                pltpu.make_async_copy(b.at[:, columns], held.at[i, :, width:], sem_in.at[2 * i + 1])
            )
        for copy in reads:
            copy.start()
        writes = []
        for i in range(ROW):
            reads[2 * i].wait()
            reads[2 * i + 1].wait()
            writes.append(pltpu.make_async_copy(held.at[i], out.at[i], sem_out.at[i]))
            writes[-1].start()
        for copy in writes:
            copy.wait()

    shape = (ROW, B, 2 * width)
    return pl.pallas_call(
        body,
        in_specs=[ANY, ANY],
        out_specs=ANY,
        out_shape=jax.ShapeDtypeStruct(shape, first.dtype),
        scratch_shapes=[
            pltpu.VMEM(shape, first.dtype),
            pltpu.SemaphoreType.DMA((2 * ROW,)),
            pltpu.SemaphoreType.DMA((ROW,)),
        ],
    )(first, second)


def join_columns(parts, width):
    def body(src, out, held, sem_in, sem_out):
        reads = [
            pltpu.make_async_copy(src.at[i, :, :width], held.at[i], sem_in.at[i])
            for i in range(ROW)
        ]
        for copy in reads:
            copy.start()
        writes = []
        for i in range(ROW):
            reads[i].wait()
            columns = slice(i * width, (i + 1) * width)
            writes.append(pltpu.make_async_copy(held.at[i], out.at[:, columns], sem_out.at[i]))
            writes[-1].start()
        for copy in writes:
            copy.wait()

    return pl.pallas_call(
        body,
        in_specs=[ANY],
        out_specs=ANY,
        out_shape=jax.ShapeDtypeStruct((B, ROW * width), parts.dtype),
        scratch_shapes=[
            pltpu.VMEM((ROW, B, width), parts.dtype),
            pltpu.SemaphoreType.DMA((ROW,)),
            pltpu.SemaphoreType.DMA((ROW,)),
        ],
        compiler_params=SMALL,
    )(parts)


def with_key_grads(dq, own, tail):
    def body(_, own_ref, tail_ref, out):
        for b in range(ROW):
            for n in range(2 * KV_LOCAL):
                g, which = divmod(n, 2)
                total = own_ref[g, which, b * B : (b + 1) * B]
                if b >= ROW - TAIL:
                    start = (b - (ROW - TAIL)) * B
                    total = total + tail_ref[g, which, start : start + B].astype(F32)
                out[b, :, n * D : (n + 1) * D] = total.astype(BF16)

    return pl.pallas_call(
        body,
        grid=(1,),
        in_specs=[
            ANY,
            pl.BlockSpec(own.shape, lambda i: (0, 0, 0, 0)),
            pl.BlockSpec(tail.shape, lambda i: (0, 0, 0, 0)),
        ],
        out_specs=pl.BlockSpec((ROW, B, KV_COLUMNS), lambda i: (0, 0, Q_LOCAL * D // KV_COLUMNS)),
        out_shape=jax.ShapeDtypeStruct(dq.shape, dq.dtype),
        input_output_aliases={0: 0},
        compiler_params=SMALL,
    )(dq, own, tail)


def join_pair(parts, pieces):
    def body(src, *refs):
        extra = refs[:ROW]
        for i in range(ROW):
            for n in range(2 * KV_LOCAL):
                g, which = divmod(n, 2)
                out = refs[ROW + which]
                total = src[i, :, n * D : (n + 1) * D].astype(F32) + extra[i][g, which].astype(F32)
                h = i * KV_LOCAL + g
                out[:, h * D : (h + 1) * D] = total.astype(out.dtype)

    piece = pl.BlockSpec(pieces[0].shape, lambda i: (0, 0, 0, 0))
    width = KEY_VALUE_HEADS * D
    out = jax.ShapeDtypeStruct((B, width), parts.dtype)
    return pl.pallas_call(
        body,
        grid=(1,),
        in_specs=[
            pl.BlockSpec((ROW, B, KV_COLUMNS), lambda i: (0, 0, Q_LOCAL * D // KV_COLUMNS))
        ]
        + [piece] * ROW,
        out_specs=[pl.BlockSpec((B, width), lambda i: (0, 0))] * 2,
        out_shape=[out, out],
        compiler_params=SMALL,
    )(parts, *pieces)


def dot(a, b, ca, cb):
    return lax.dot_general(a, b, (((ca,), (cb,)), ((), ())), preferred_element_type=F32)


def attention_body(
    meta, q_ref, go_ref, k_ref, v_ref, tk_ref, tv_ref, sk_ref, sv_ref, ok_ref, ov_ref,
    dq_ref, own_ref, tail_ref, sink_ref, ks, vs, ssk, ssv, kst, sst, acc, sacc,
):
    g = pl.program_id(0)
    i = pl.program_id(1)

    @pl.when(i == 0)
    def _():
        ks[: TAIL * B] = tk_ref[...].reshape(TAIL * B, D)
        ks[TAIL * B :] = k_ref[...].reshape(ROW * B, D)
        vs[: TAIL * B] = tv_ref[...].reshape(TAIL * B, D)
        vs[TAIL * B :] = v_ref[...].reshape(ROW * B, D)
        near = pl.ds(pl.multiple_of(meta[META_CORE] * B, B), B)
        far = pl.ds(pl.multiple_of((1 - meta[META_CORE]) * B, B), B)
        ssk[near, :] = sk_ref[...]
        ssv[near, :] = sv_ref[...]
        ssk[far, :] = ok_ref[...]
        ssv[far, :] = ov_ref[...]
        kst[...] = ks[...].T
        sst[...] = ssk[...].T
        acc[...] = jnp.zeros_like(acc)
        sacc[...] = jnp.zeros_like(sacc)

    block = meta[0] + i
    rows = pl.ds(pl.multiple_of(i * B, B), WMAX * B)
    kw = ks[rows, :]
    vw = vs[rows, :]
    kwt = kst[:, rows]
    ksink = ssk[...]
    vsink = ssv[...]
    ksinkt = sst[...]
    key = lax.broadcasted_iota(jnp.int32, (B, PAIR * B), 0)
    query = lax.broadcasted_iota(jnp.int32, (B, PAIR * B), 1) % B
    causal = key <= query

    def bias(allowed):
        return jnp.concatenate(
            [jnp.full((1, B), jnp.where(ok, 0.0, NEG_FILL), F32) for ok in allowed], 1
        )

    pairs = [range(first, first + PAIR) for first in range(0, GROUP, PAIR)]
    first_products = []
    for heads in pairs:
        q2 = jnp.concatenate([q_ref[0, :, h * D : (h + 1) * D] for h in heads], 0)
        go2 = jnp.concatenate([go_ref[0, :, h * D : (h + 1) * D] for h in heads], 0)
        sw = dot(kw, q2, 1, 1)
        ss = dot(ksink, q2, 1, 1)
        pw = dot(vw, go2, 1, 1)
        ps = dot(vsink, go2, 1, 1)
        scores = [sw[j * B : (j + 1) * B] for j in range(WMAX)]
        scores[TAIL] = jnp.where(causal, scores[TAIL], NEG_FILL)
        scores += [ss[t * B : (t + 1) * B] for t in range(SMAX)]
        grads = [pw[j * B : (j + 1) * B] for j in range(WMAX)]
        grads += [ps[t * B : (t + 1) * B] for t in range(SMAX)]
        first_products.append((q2, go2, scores, grads))

    softmaxes = []
    for heads, (_, _, scores, grads) in zip(pairs, first_products):
        window = [meta[1 + g * GROUP + h] for h in heads]
        sink = [meta[1 + Q_LOCAL + g * GROUP + h] for h in heads]
        biases = [
            bias([(block >= TAIL - j) & (TAIL - j < w) for w in window]) for j in range(TAIL)
        ]
        biases += [jnp.zeros((1, PAIR * B), F32)]
        biases += [
            bias([(t < c) & (t <= block - w) for w, c in zip(window, sink)]) for t in range(SMAX)
        ]
        tops = [
            jnp.max(s, 0, keepdims=True) * EXP2_SCALE + extra for s, extra in zip(scores, biases)
        ]
        top = tops[0]
        for t in tops[1:]:
            top = jnp.maximum(top, t)
        exps = [jnp.exp2(s * EXP2_SCALE - (top - extra)) for s, extra in zip(scores, biases)]
        total = exps[0]
        product = exps[0] * grads[0]
        for e, p in zip(exps[1:], grads[1:]):
            total = total + e
            product = product + e * p
        inverse = 1.0 / jnp.sum(total, 0, keepdims=True)
        row_dot = jnp.sum(product, 0, keepdims=True) * inverse
        weights = [e * inverse for e in exps]
        rounded = [w.astype(BF16) for w in weights]
        dscores = [(w * (p - row_dot)).astype(BF16) for w, p in zip(weights, grads)]
        softmaxes.append(
            [
                jnp.concatenate(rows, 0)
                for rows in (rounded[:WMAX], rounded[WMAX:], dscores[:WMAX], dscores[WMAX:])
            ]
        )

    sums = []
    for heads, (q2, go2, _, _), (wb_window, wb_sink, ds_window, ds_sink) in zip(
        pairs, first_products, softmaxes
    ):
        sums.append(
            [
                dot(ds_window, q2, 1, 0),
                dot(wb_window, go2, 1, 0),
                dot(ds_sink, q2, 1, 0),
                dot(wb_sink, go2, 1, 0),
            ]
        )
        dqt = (dot(kwt, ds_window, 1, 0) + dot(ksinkt, ds_sink, 1, 0)) * SCALE
        for n, h in enumerate(heads):
            dq_ref[0, :, h * D : (h + 1) * D] = dqt[:, n * B : (n + 1) * B].T.astype(BF16)
    acc[0, rows, :] += sums[0][0] + sums[1][0]
    acc[1, rows, :] += sums[0][1] + sums[1][1]
    sacc[0] += sums[0][2] + sums[1][2]
    sacc[1] += sums[0][3] + sums[1][3]

    @pl.when(i == ROW - 1)
    def _():
        own_ref[0, 0] = acc[0, TAIL * B :] * SCALE
        own_ref[0, 1] = acc[1, TAIL * B :]
        tail_ref[0, 0] = (acc[0, : TAIL * B] * SCALE).astype(BF16)
        tail_ref[0, 1] = acc[1, : TAIL * B].astype(BF16)
        for t in range(SMAX):
            sink_ref[t, 0, 0] = sacc[0, t * B : (t + 1) * B] * SCALE
            sink_ref[t, 0, 1] = sacc[1, t * B : (t + 1) * B]


def attention(meta, qgo, kv, tail, sink, other, interpret=False):
    wide = pl.BlockSpec((1, B, GROUP * D), lambda g, i, m: (i, 0, g))
    wide_go = pl.BlockSpec((1, B, GROUP * D), lambda g, i, m: (i, 0, KV_LOCAL + g))

    def pair(count):
        return [
            pl.BlockSpec((count, B, D), lambda g, i, m: (0, 0, g)),
            pl.BlockSpec((count, B, D), lambda g, i, m: (0, 0, KV_LOCAL + g)),
        ]

    one = [
        pl.BlockSpec((B, D), lambda g, i, m: (0, g)),
        pl.BlockSpec((B, D), lambda g, i, m: (0, KV_LOCAL + g)),
    ]

    def result(rows, dtype):
        return (
            pl.BlockSpec((1, 2, rows * B, D), lambda g, i, m: (g, 0, 0, 0)),
            jax.ShapeDtypeStruct((KV_LOCAL, 2, rows * B, D), dtype),
        )

    results = [
        (wide, jax.ShapeDtypeStruct((ROW, B, Q_LOCAL * D + KV_COLUMNS), BF16)),
        result(ROW, F32),
        result(TAIL, BF16),
        (
            pl.BlockSpec((SMAX, 1, 2, B, D), lambda g, i, m: (0, g, 0, 0, 0)),
            jax.ShapeDtypeStruct((SMAX, KV_LOCAL, 2, B, D), F32),
        ),
    ]
    return pl.pallas_call(
        attention_body,
        grid_spec=pltpu.PrefetchScalarGridSpec(
            num_scalar_prefetch=1,
            grid=(KV_LOCAL, ROW),
            in_specs=[wide, wide_go] + pair(ROW) + pair(TAIL) + one + one,
            out_specs=[r[0] for r in results],
            scratch_shapes=[
                pltpu.VMEM(((TAIL + ROW) * B, D), BF16),
                pltpu.VMEM(((TAIL + ROW) * B, D), BF16),
                pltpu.VMEM((SMAX * B, D), BF16),
                pltpu.VMEM((SMAX * B, D), BF16),
                pltpu.VMEM((D, (TAIL + ROW) * B), BF16),
                pltpu.VMEM((D, SMAX * B), BF16),
                pltpu.VMEM((2, (TAIL + ROW) * B, D), F32),
                pltpu.VMEM((2, SMAX * B, D), F32),
            ],
        ),
        out_shape=[r[1] for r in results],
        compiler_params=pltpu.CompilerParams(vmem_limit_bytes=48 * MIB),
        interpret=interpret,
    )(meta, qgo, qgo, kv, kv, tail, tail, sink, sink, other, other)


def line(y, z, core):
    return ((z % 4 * 8 + y) * 2 + z // 4) * 2 + core


def moved(moves):
    return [(line(*p, 0), line(*q, 0)) for p, q in moves] + [
        (line(*p[::-1], 1), line(*q[::-1], 1)) for p, q in moves
    ]


def spread():
    def reached(end, step):
        return end + step if end == 0 else end - step

    ends = (0, 7)
    rounds = [
        [[((0, 0), corner)] for corner in ((7, 7), (7, 0), (0, 7))],
        [
            [((a, b), (reached(a, step), b)) for a in ends for b in ends]
            for step in (3, 2, 1)
        ],
        [
            [((a, b), (a, reached(b, step))) for a in range(8) for b in ends]
            for step in (3, 2, 1)
        ],
    ]
    return [[moved(moves) for moves in permutes] for permutes in rounds]


def gather():
    return [
        [[(b, a) for a, b in pairs] for pairs in permutes] for permutes in reversed(spread())
    ]


def exchanged(value, axes):
    return lax.all_to_all(value, axes, split_axis=0, concat_axis=0, tiled=False)


def summed(total, permutes):
    send = total.astype(BF16)
    for got in [lax.ppermute(send, LINE, pairs) for pairs in permutes]:
        total = total + got.astype(F32)
    return total


def after(value, *others):
    return lax.optimization_barrier((value, others))[0]


def shards(queries, keys, values, output_gradient, windows, sinks):
    core = lax.axis_index("core")
    run = lax.axis_index(("y", "zh", "core")) * 4 + lax.axis_index("zl")
    x = lax.axis_index("x")
    meta = jnp.concatenate(
        [
            (run * ROW)[None].astype(jnp.int32),
            lax.dynamic_slice_in_dim(windows, x * Q_LOCAL, Q_LOCAL),
            lax.dynamic_slice_in_dim(sinks, x * Q_LOCAL, Q_LOCAL),
            core[None].astype(jnp.int32),
        ]
    )
    runs = [(run // 4 // 4, run // 4 // 2 % 2 * 4 + run % 4, run // 4 % 2) for run in range(128)]
    to_next = [(line(*a), line(*b)) for a, b in zip(runs[:-1], runs[1:])]
    swap = [(0, 1), (1, 0)]

    kv_split = split_pair(keys[0], values[0])
    qgo_split = split_pair(after(queries[0], kv_split), output_gradient[0])
    kv = after(exchanged(kv_split, "x"), qgo_split)
    qgo = exchanged(qgo_split, "x")
    tail = lax.ppermute(kv[ROW - TAIL :], LINE, to_next)
    sink = lax.ppermute(kv[1], LINE, [(line(0, 0, 0), line(0, 0, 1))])
    sink = jnp.where(run == 0, kv[0], sink)
    for step, permutes in enumerate(spread()):
        if step == 2:
            sink = after(sink, tail)
        got = [lax.ppermute(sink, LINE, pairs) for pairs in permutes]
        sink = sink + got[0] + got[1] + got[2]
    other = lax.ppermute(sink, "core", swap)
    dq, own, tail_grad, sink_grad = attention(meta, qgo, kv, tail, sink, other)

    tail_back = lax.ppermute(tail_grad, LINE, [(b, a) for a, b in to_next])
    total = lax.dynamic_index_in_dim(sink_grad, core, 0, False)
    away = lax.dynamic_index_in_dim(sink_grad, 1 - core, 0, False).astype(BF16)
    total = total + lax.ppermute(away, "core", swap).astype(F32)
    rounds = gather()
    total = summed(total, rounds[0])
    grads = with_key_grads(dq, own, after(tail_back, total))
    parts = exchanged(grads, "x")
    dq_tokens = join_columns(parts, Q_LOCAL * D)
    total = summed(after(total, grads), rounds[1])
    total = summed(total, rounds[2])
    total = after(total, parts)
    total = total.astype(BF16)

    def at(x, core):
        return x * 32 + core

    pieces = [
        lax.ppermute(total, AXES, [(at(j, c), at(c, 0)) for c in range(SMAX)]) for j in range(ROW)
    ]
    dk, dv = join_pair(parts, pieces)
    return dq_tokens[None], dk[None], dv[None]


def solution(mesh):
    split = Mesh(mesh.devices.reshape(SIZES), AXES)
    tokens = P(("y", "zh", "core"), ("zl", "x"), None)
    return jax.shard_map(
        shards,
        mesh=split,
        in_specs=(tokens, tokens, tokens, tokens, P(), P()),
        out_specs=(tokens, tokens, tokens),
        check_vma=False,
    )
```

```python
import math

import jax
import jax.numpy as jnp
from jax import lax
from jax.experimental import pallas as pl
from jax.experimental.pallas import tpu as pltpu
from jax.sharding import Mesh, PartitionSpec as P

QUERY_HEADS = 32
KEY_VALUE_HEADS = 8
HEAD_DIMENSION = 128
BLOCK_TOKENS = 128
WMAX = 4
SMAX = 2
NEG_FILL = -1e30

AXES = ("zl", "x", "y", "zh", "core")
SIZES = (4, 4, 8, 2, 2)
LINE = ("zl", "y", "zh", "core")
ROW = 4
KV_LOCAL = KEY_VALUE_HEADS // ROW
GROUP = QUERY_HEADS // KEY_VALUE_HEADS
Q_LOCAL = KV_LOCAL * GROUP
TAIL = WMAX - 1
KV_COLUMNS = 2 * KV_LOCAL * HEAD_DIMENSION
PAIR = 2
D = HEAD_DIMENSION
B = BLOCK_TOKENS
SCALE = 1.0 / math.sqrt(HEAD_DIMENSION)
EXP2_SCALE = SCALE * math.log2(math.e)
META_CORE = 1 + 2 * Q_LOCAL
MIB = 1024 * 1024
F32 = jnp.float32
BF16 = jnp.bfloat16


ANY = pl.BlockSpec(memory_space=pl.ANY)
SMALL = pltpu.CompilerParams(vmem_limit_bytes=6 * MIB)


def split_pair(first, second):
    width = first.shape[1] // ROW

    def body(a, b, out, held, sem_in, sem_out):
        reads = []
        for i in range(ROW):
            columns = slice(i * width, (i + 1) * width)
            reads.append(
                pltpu.make_async_copy(a.at[:, columns], held.at[i, :, :width], sem_in.at[2 * i])
            )
            reads.append(
                pltpu.make_async_copy(b.at[:, columns], held.at[i, :, width:], sem_in.at[2 * i + 1])
            )
        for copy in reads:
            copy.start()
        writes = []
        for i in range(ROW):
            reads[2 * i].wait()
            reads[2 * i + 1].wait()
            writes.append(pltpu.make_async_copy(held.at[i], out.at[i], sem_out.at[i]))
            writes[-1].start()
        for copy in writes:
            copy.wait()

    shape = (ROW, B, 2 * width)
    return pl.pallas_call(
        body,
        in_specs=[ANY, ANY],
        out_specs=ANY,
        out_shape=jax.ShapeDtypeStruct(shape, first.dtype),
        scratch_shapes=[
            pltpu.VMEM(shape, first.dtype),
            pltpu.SemaphoreType.DMA((2 * ROW,)),
            pltpu.SemaphoreType.DMA((ROW,)),
        ],
    )(first, second)


def join_columns(parts, width):
    def body(src, out, held, sem_in, sem_out):
        reads = [
            pltpu.make_async_copy(src.at[i, :, :width], held.at[i], sem_in.at[i])
            for i in range(ROW)
        ]
        for copy in reads:
            copy.start()
        writes = []
        for i in range(ROW):
            reads[i].wait()
            columns = slice(i * width, (i + 1) * width)
            writes.append(pltpu.make_async_copy(held.at[i], out.at[:, columns], sem_out.at[i]))
            writes[-1].start()
        for copy in writes:
            copy.wait()

    return pl.pallas_call(
        body,
        in_specs=[ANY],
        out_specs=ANY,
        out_shape=jax.ShapeDtypeStruct((B, ROW * width), parts.dtype),
        scratch_shapes=[
            pltpu.VMEM((ROW, B, width), parts.dtype),
            pltpu.SemaphoreType.DMA((ROW,)),
            pltpu.SemaphoreType.DMA((ROW,)),
        ],
        compiler_params=SMALL,
    )(parts)


def with_key_grads(dq, own, tail):
    def body(_, own_ref, tail_ref, out):
        for b in range(ROW):
            for n in range(2 * KV_LOCAL):
                g, which = divmod(n, 2)
                total = own_ref[g, which, b * B : (b + 1) * B]
                if b >= ROW - TAIL:
                    start = (b - (ROW - TAIL)) * B
                    total = total + tail_ref[g, which, start : start + B].astype(F32)
                out[b, :, n * D : (n + 1) * D] = total.astype(BF16)

    return pl.pallas_call(
        body,
        grid=(1,),
        in_specs=[
            ANY,
            pl.BlockSpec(own.shape, lambda i: (0, 0, 0, 0)),
            pl.BlockSpec(tail.shape, lambda i: (0, 0, 0, 0)),
        ],
        out_specs=pl.BlockSpec((ROW, B, KV_COLUMNS), lambda i: (0, 0, Q_LOCAL * D // KV_COLUMNS)),
        out_shape=jax.ShapeDtypeStruct(dq.shape, dq.dtype),
        input_output_aliases={0: 0},
        compiler_params=SMALL,
    )(dq, own, tail)


def join_pair(parts, pieces):
    def body(src, *refs):
        extra = refs[:ROW]
        for i in range(ROW):
            for n in range(2 * KV_LOCAL):
                g, which = divmod(n, 2)
                out = refs[ROW + which]
                total = src[i, :, n * D : (n + 1) * D].astype(F32) + extra[i][g, which].astype(F32)
                h = i * KV_LOCAL + g
                out[:, h * D : (h + 1) * D] = total.astype(out.dtype)

    piece = pl.BlockSpec(pieces[0].shape, lambda i: (0, 0, 0, 0))
    width = KEY_VALUE_HEADS * D
    out = jax.ShapeDtypeStruct((B, width), parts.dtype)
    return pl.pallas_call(
        body,
        grid=(1,),
        in_specs=[
            pl.BlockSpec((ROW, B, KV_COLUMNS), lambda i: (0, 0, Q_LOCAL * D // KV_COLUMNS))
        ]
        + [piece] * ROW,
        out_specs=[pl.BlockSpec((B, width), lambda i: (0, 0))] * 2,
        out_shape=[out, out],
        compiler_params=SMALL,
    )(parts, *pieces)


def dot(a, b, ca, cb):
    return lax.dot_general(a, b, (((ca,), (cb,)), ((), ())), preferred_element_type=F32)


def attention_body(
    meta, q_ref, go_ref, k_ref, v_ref, tk_ref, tv_ref, sk_ref, sv_ref, ok_ref, ov_ref,
    dq_ref, own_ref, tail_ref, sink_ref, ks, vs, ssk, ssv, kst, sst, acc, sacc,
):
    g = pl.program_id(0)
    i = pl.program_id(1) * ROW

    @pl.when(i == 0)
    def _():
        ks[: TAIL * B] = tk_ref[...].reshape(TAIL * B, D)
        ks[TAIL * B :] = k_ref[...].reshape(ROW * B, D)
        vs[: TAIL * B] = tv_ref[...].reshape(TAIL * B, D)
        vs[TAIL * B :] = v_ref[...].reshape(ROW * B, D)
        near = pl.ds(pl.multiple_of(meta[META_CORE] * B, B), B)
        far = pl.ds(pl.multiple_of((1 - meta[META_CORE]) * B, B), B)
        ssk[near, :] = sk_ref[...]
        ssv[near, :] = sv_ref[...]
        ssk[far, :] = ok_ref[...]
        ssv[far, :] = ov_ref[...]
        kst[...] = ks[...].T
        sst[...] = ssk[...].T
        acc[...] = jnp.zeros_like(acc)
        sacc[...] = jnp.zeros_like(sacc)

    ksink = ssk[...]
    vsink = ssv[...]
    ksinkt = sst[...]
    key = lax.broadcasted_iota(jnp.int32, (B, PAIR * B), 0)
    query = lax.broadcasted_iota(jnp.int32, (B, PAIR * B), 1) % B
    causal = key <= query

    def bias(allowed):
        return jnp.concatenate(
            [jnp.full((1, B), jnp.where(ok, 0.0, NEG_FILL), F32) for ok in allowed], 1
        )

    for n in range(ROW):
        block = meta[0] + i + n
        rows = pl.ds(pl.multiple_of((i + n) * B, B), WMAX * B)
        kw = ks[rows, :]
        vw = vs[rows, :]
        kwt = kst[:, rows]
        pairs = [range(first, first + PAIR) for first in range(0, GROUP, PAIR)]
        first_products = []
        for heads in pairs:
            q2 = jnp.concatenate([q_ref[n, :, h * D : (h + 1) * D] for h in heads], 0)
            go2 = jnp.concatenate([go_ref[n, :, h * D : (h + 1) * D] for h in heads], 0)
            sw = dot(kw, q2, 1, 1)
            ss = dot(ksink, q2, 1, 1)
            pw = dot(vw, go2, 1, 1)
            ps = dot(vsink, go2, 1, 1)
            scores = [sw[j * B : (j + 1) * B] for j in range(WMAX)]
            scores[TAIL] = jnp.where(causal, scores[TAIL], NEG_FILL)
            scores += [ss[t * B : (t + 1) * B] for t in range(SMAX)]
            grads = [pw[j * B : (j + 1) * B] for j in range(WMAX)]
            grads += [ps[t * B : (t + 1) * B] for t in range(SMAX)]
            first_products.append((q2, go2, scores, grads))

        softmaxes = []
        for heads, (_, _, scores, grads) in zip(pairs, first_products):
            window = [meta[1 + g * GROUP + h] for h in heads]
            sink = [meta[1 + Q_LOCAL + g * GROUP + h] for h in heads]
            biases = [
                bias([(block >= TAIL - j) & (TAIL - j < w) for w in window]) for j in range(TAIL)
            ]
            biases += [jnp.zeros((1, PAIR * B), F32)]
            biases += [
                bias([(t < c) & (t <= block - w) for w, c in zip(window, sink)]) for t in range(SMAX)
            ]
            tops = [
                jnp.max(s, 0, keepdims=True) * EXP2_SCALE + extra for s, extra in zip(scores, biases)
            ]
            top = tops[0]
            for t in tops[1:]:
                top = jnp.maximum(top, t)
            exps = [jnp.exp2(s * EXP2_SCALE - (top - extra)) for s, extra in zip(scores, biases)]
            total = exps[0]
            product = exps[0] * grads[0]
            for e, p in zip(exps[1:], grads[1:]):
                total = total + e
                product = product + e * p
            inverse = 1.0 / jnp.sum(total, 0, keepdims=True)
            row_dot = jnp.sum(product, 0, keepdims=True) * inverse
            weights = [e * inverse for e in exps]
            rounded = [w.astype(BF16) for w in weights]
            dscores = [(w * (p - row_dot)).astype(BF16) for w, p in zip(weights, grads)]
            softmaxes.append(
                [
                    jnp.concatenate(rows, 0)
                    for rows in (rounded[:WMAX], rounded[WMAX:], dscores[:WMAX], dscores[WMAX:])
                ]
            )

        sums = []
        for heads, (q2, go2, _, _), (wb_window, wb_sink, ds_window, ds_sink) in zip(
            pairs, first_products, softmaxes
        ):
            sums.append(
                [
                    dot(ds_window, q2, 1, 0),
                    dot(wb_window, go2, 1, 0),
                    dot(ds_sink, q2, 1, 0),
                    dot(wb_sink, go2, 1, 0),
                ]
            )
            dqt = (dot(kwt, ds_window, 1, 0) + dot(ksinkt, ds_sink, 1, 0)) * SCALE
            for n2, h in enumerate(heads):
                dq_ref[n, :, h * D : (h + 1) * D] = dqt[:, n2 * B : (n2 + 1) * B].T.astype(BF16)
        acc[0, rows, :] += sums[0][0] + sums[1][0]
        acc[1, rows, :] += sums[0][1] + sums[1][1]
        sacc[0] += sums[0][2] + sums[1][2]
        sacc[1] += sums[0][3] + sums[1][3]


    @pl.when(i == 0)
    def _():
        own_ref[0, 0] = acc[0, TAIL * B :] * SCALE
        own_ref[0, 1] = acc[1, TAIL * B :]
        tail_ref[0, 0] = (acc[0, : TAIL * B] * SCALE).astype(BF16)
        tail_ref[0, 1] = acc[1, : TAIL * B].astype(BF16)
        for t in range(SMAX):
            sink_ref[t, 0, 0] = sacc[0, t * B : (t + 1) * B] * SCALE
            sink_ref[t, 0, 1] = sacc[1, t * B : (t + 1) * B]


def attention(meta, qgo, kv, tail, sink, other, interpret=False):
    wide = pl.BlockSpec((ROW, B, GROUP * D), lambda g, i, m: (i, 0, g))
    wide_go = pl.BlockSpec((ROW, B, GROUP * D), lambda g, i, m: (i, 0, KV_LOCAL + g))

    def pair(count):
        return [
            pl.BlockSpec((count, B, D), lambda g, i, m: (0, 0, g)),
            pl.BlockSpec((count, B, D), lambda g, i, m: (0, 0, KV_LOCAL + g)),
        ]

    one = [
        pl.BlockSpec((B, D), lambda g, i, m: (0, g)),
        pl.BlockSpec((B, D), lambda g, i, m: (0, KV_LOCAL + g)),
    ]

    def result(rows, dtype):
        return (
            pl.BlockSpec((1, 2, rows * B, D), lambda g, i, m: (g, 0, 0, 0)),
            jax.ShapeDtypeStruct((KV_LOCAL, 2, rows * B, D), dtype),
        )

    results = [
        (wide, jax.ShapeDtypeStruct((ROW, B, Q_LOCAL * D + KV_COLUMNS), BF16)),
        result(ROW, F32),
        result(TAIL, BF16),
        (
            pl.BlockSpec((SMAX, 1, 2, B, D), lambda g, i, m: (0, g, 0, 0, 0)),
            jax.ShapeDtypeStruct((SMAX, KV_LOCAL, 2, B, D), F32),
        ),
    ]
    return pl.pallas_call(
        attention_body,
        grid_spec=pltpu.PrefetchScalarGridSpec(
            num_scalar_prefetch=1,
            grid=(KV_LOCAL, 1),
            in_specs=[wide, wide_go] + pair(ROW) + pair(TAIL) + one + one,
            out_specs=[r[0] for r in results],
            scratch_shapes=[
                pltpu.VMEM(((TAIL + ROW) * B, D), BF16),
                pltpu.VMEM(((TAIL + ROW) * B, D), BF16),
                pltpu.VMEM((SMAX * B, D), BF16),
                pltpu.VMEM((SMAX * B, D), BF16),
                pltpu.VMEM((D, (TAIL + ROW) * B), BF16),
                pltpu.VMEM((D, SMAX * B), BF16),
                pltpu.VMEM((2, (TAIL + ROW) * B, D), F32),
                pltpu.VMEM((2, SMAX * B, D), F32),
            ],
        ),
        out_shape=[r[1] for r in results],
        compiler_params=pltpu.CompilerParams(vmem_limit_bytes=48 * MIB),
        interpret=interpret,
    )(meta, qgo, qgo, kv, kv, tail, tail, sink, sink, other, other)


def line(y, z, core):
    return ((z % 4 * 8 + y) * 2 + z // 4) * 2 + core


def at(x, core):
    return x * 32 + core


def moved(moves):
    return [(line(*p, 0), line(*q, 0)) for p, q in moves] + [
        (line(*p[::-1], 1), line(*q[::-1], 1)) for p, q in moves
    ]


ROUNDS = (((4, 0), (2, 0), (6, 0)), ((0, 4), (1, 4), (1, 0)), ((0, 2), (0, 1), (0, 7)))


def spread():
    holders = [(0, 0)]
    rounds = []
    for offsets in ROUNDS:
        moves = [
            [((a, b), ((a + da) % 8, (b + db) % 8)) for a, b in holders] for da, db in offsets
        ]
        rounds.append([moved(m) for m in moves])
        holders = holders + [q for m in moves for _, q in m]
    return rounds


def gather():
    def inner(end, step):
        return end + step if end == 0 else end - step

    ends = (0, 7)
    rounds = [
        [
            [((a, inner(b, step)), (a, b)) for a in range(8) for b in ends]
            for step in (1, 3, 2)
        ],
        [
            [((inner(a, step), b), (a, b)) for a in ends for b in ends]
            for step in (3, 2, 1)
        ],
        [[(corner, (0, 0))] for corner in ((7, 7), (7, 0), (0, 7))],
    ]
    return [[moved(moves) for moves in permutes] for permutes in rounds]


def exchanged(value, axes):
    return lax.all_to_all(value, axes, split_axis=0, concat_axis=0, tiled=False)


def summed(total, permutes):
    send = total.astype(BF16)
    for got in [lax.ppermute(send, LINE, pairs) for pairs in permutes]:
        total = total + got.astype(F32)
    return total


def after(value, *others):
    return lax.optimization_barrier((value, others))[0]


def shards(queries, keys, values, output_gradient, windows, sinks):
    core = lax.axis_index("core")
    run = lax.axis_index(("y", "zh", "core")) * 4 + lax.axis_index("zl")
    x = lax.axis_index("x")
    meta = jnp.concatenate(
        [
            (run * ROW)[None].astype(jnp.int32),
            lax.dynamic_slice_in_dim(windows, x * Q_LOCAL, Q_LOCAL),
            lax.dynamic_slice_in_dim(sinks, x * Q_LOCAL, Q_LOCAL),
            core[None].astype(jnp.int32),
        ]
    )
    runs = [(run // 4 // 4, run // 4 // 2 % 2 * 4 + run % 4, run // 4 % 2) for run in range(128)]
    to_next = [(line(*a), line(*b)) for a, b in zip(runs[:-1], runs[1:])]
    swap = [(0, 1), (1, 0)]

    kv_split = split_pair(keys[0], values[0])
    qgo_split = split_pair(after(queries[0], kv_split), output_gradient[0])
    kv = after(exchanged(kv_split, "x"), qgo_split)
    qgo = exchanged(qgo_split, "x")
    tail = lax.ppermute(kv[ROW - TAIL :], LINE, to_next)
    first = [
        lax.ppermute(
            kv_split[j],
            AXES,
            [(at(c, 0), at(j, c)) for c in range(SMAX) if at(c, 0) != at(j, c)],
        )
        for j in range(ROW)
    ]
    sink = jnp.where((run == 0) & (x == 0), kv_split[0], first[0] + first[1] + first[2] + first[3])
    for step, permutes in enumerate(spread()):
        if step == 2:
            sink = after(sink, tail)
        got = [lax.ppermute(sink, LINE, pairs) for pairs in permutes]
        sink = sink + got[0] + got[1] + got[2]
    other = lax.ppermute(sink, "core", swap)
    dq, own, tail_grad, sink_grad = attention(meta, qgo, kv, tail, sink, other)

    tail_back = lax.ppermute(tail_grad, LINE, [(b, a) for a, b in to_next])
    total = lax.dynamic_index_in_dim(sink_grad, core, 0, False)
    away = lax.dynamic_index_in_dim(sink_grad, 1 - core, 0, False).astype(BF16)
    total = total + lax.ppermute(away, "core", swap).astype(F32)
    rounds = gather()
    total = summed(total, rounds[0])
    grads = with_key_grads(dq, own, after(tail_back, total))
    parts = exchanged(grads, "x")
    dq_tokens = join_columns(parts, Q_LOCAL * D)
    total = after(total, grads)
    for permutes in rounds[1:]:
        total = summed(total, permutes)
    total = after(total, parts)
    total = total.astype(BF16)

    pieces = [
        lax.ppermute(total, AXES, [(at(j, c), at(c, 0)) for c in range(SMAX)]) for j in range(ROW)
    ]
    dk, dv = join_pair(parts, pieces)
    return dq_tokens[None], dk[None], dv[None]


def solution(mesh):
    split = Mesh(mesh.devices.reshape(SIZES), AXES)
    tokens = P(("y", "zh", "core"), ("zl", "x"), None)
    return jax.shard_map(
        shards,
        mesh=split,
        in_specs=(tokens, tokens, tokens, tokens, P(), P()),
        out_specs=(tokens, tokens, tokens),
        check_vma=False,
    )
```

```python
import math

import jax
import jax.numpy as jnp
from jax import lax
from jax.experimental import pallas as pl
from jax.experimental.pallas import tpu as pltpu
from jax.sharding import Mesh, PartitionSpec as P

QUERY_HEADS = 32
KEY_VALUE_HEADS = 8
HEAD_DIMENSION = 128
BLOCK_TOKENS = 128
WMAX = 4
SMAX = 2
NEG_FILL = -1e30

AXES = ("zl", "x", "y", "zh", "core")
SIZES = (4, 4, 8, 2, 2)
LINE = ("zl", "y", "zh", "core")
ROW = 4
KV_LOCAL = KEY_VALUE_HEADS // ROW
GROUP = QUERY_HEADS // KEY_VALUE_HEADS
Q_LOCAL = KV_LOCAL * GROUP
TAIL = WMAX - 1
KV_COLUMNS = 2 * KV_LOCAL * HEAD_DIMENSION
PAIR = 2
D = HEAD_DIMENSION
B = BLOCK_TOKENS
SCALE = 1.0 / math.sqrt(HEAD_DIMENSION)
EXP2_SCALE = SCALE * math.log2(math.e)
META_CORE = 1 + 2 * Q_LOCAL
MIB = 1024 * 1024
F32 = jnp.float32
BF16 = jnp.bfloat16


ANY = pl.BlockSpec(memory_space=pl.ANY)
SMALL = pltpu.CompilerParams(vmem_limit_bytes=6 * MIB)


def split_pair(first, second):
    width = first.shape[1] // ROW

    def body(a, b, out, held, sem_in, sem_out):
        reads = []
        for i in range(ROW):
            columns = slice(i * width, (i + 1) * width)
            reads.append(
                pltpu.make_async_copy(a.at[:, columns], held.at[i, :, :width], sem_in.at[2 * i])
            )
            reads.append(
                pltpu.make_async_copy(b.at[:, columns], held.at[i, :, width:], sem_in.at[2 * i + 1])
            )
        for copy in reads:
            copy.start()
        writes = []
        for i in range(ROW):
            reads[2 * i].wait()
            reads[2 * i + 1].wait()
            writes.append(pltpu.make_async_copy(held.at[i], out.at[i], sem_out.at[i]))
            writes[-1].start()
        for copy in writes:
            copy.wait()

    shape = (ROW, B, 2 * width)
    return pl.pallas_call(
        body,
        in_specs=[ANY, ANY],
        out_specs=ANY,
        out_shape=jax.ShapeDtypeStruct(shape, first.dtype),
        scratch_shapes=[
            pltpu.VMEM(shape, first.dtype),
            pltpu.SemaphoreType.DMA((2 * ROW,)),
            pltpu.SemaphoreType.DMA((ROW,)),
        ],
    )(first, second)


def join_columns(parts, width):
    def body(src, out, held, sem_in, sem_out):
        reads = [
            pltpu.make_async_copy(src.at[i, :, :width], held.at[i], sem_in.at[i])
            for i in range(ROW)
        ]
        for copy in reads:
            copy.start()
        writes = []
        for i in range(ROW):
            reads[i].wait()
            columns = slice(i * width, (i + 1) * width)
            writes.append(pltpu.make_async_copy(held.at[i], out.at[:, columns], sem_out.at[i]))
            writes[-1].start()
        for copy in writes:
            copy.wait()

    return pl.pallas_call(
        body,
        in_specs=[ANY],
        out_specs=ANY,
        out_shape=jax.ShapeDtypeStruct((B, ROW * width), parts.dtype),
        scratch_shapes=[
            pltpu.VMEM((ROW, B, width), parts.dtype),
            pltpu.SemaphoreType.DMA((ROW,)),
            pltpu.SemaphoreType.DMA((ROW,)),
        ],
        compiler_params=SMALL,
    )(parts)


def with_key_grads(dq, own, tail):
    def body(_, own_ref, tail_ref, out):
        for b in range(ROW):
            for n in range(2 * KV_LOCAL):
                g, which = divmod(n, 2)
                total = own_ref[g, which, b * B : (b + 1) * B]
                if b >= ROW - TAIL:
                    start = (b - (ROW - TAIL)) * B
                    total = total + tail_ref[g, which, start : start + B].astype(F32)
                out[b, :, n * D : (n + 1) * D] = total.astype(BF16)

    return pl.pallas_call(
        body,
        grid=(1,),
        in_specs=[
            ANY,
            pl.BlockSpec(own.shape, lambda i: (0, 0, 0, 0)),
            pl.BlockSpec(tail.shape, lambda i: (0, 0, 0, 0)),
        ],
        out_specs=pl.BlockSpec((ROW, B, KV_COLUMNS), lambda i: (0, 0, Q_LOCAL * D // KV_COLUMNS)),
        out_shape=jax.ShapeDtypeStruct(dq.shape, dq.dtype),
        input_output_aliases={0: 0},
        compiler_params=SMALL,
    )(dq, own, tail)


def join_pair(parts, pieces):
    def body(src, *refs):
        extra = refs[:ROW]
        for i in range(ROW):
            for n in range(2 * KV_LOCAL):
                g, which = divmod(n, 2)
                out = refs[ROW + which]
                total = src[i, :, n * D : (n + 1) * D].astype(F32) + extra[i][g, which].astype(F32)
                h = i * KV_LOCAL + g
                out[:, h * D : (h + 1) * D] = total.astype(out.dtype)

    piece = pl.BlockSpec(pieces[0].shape, lambda i: (0, 0, 0, 0))
    width = KEY_VALUE_HEADS * D
    out = jax.ShapeDtypeStruct((B, width), parts.dtype)
    return pl.pallas_call(
        body,
        grid=(1,),
        in_specs=[
            pl.BlockSpec((ROW, B, KV_COLUMNS), lambda i: (0, 0, Q_LOCAL * D // KV_COLUMNS))
        ]
        + [piece] * ROW,
        out_specs=[pl.BlockSpec((B, width), lambda i: (0, 0))] * 2,
        out_shape=[out, out],
        compiler_params=SMALL,
    )(parts, *pieces)


def dot(a, b, ca, cb):
    return lax.dot_general(a, b, (((ca,), (cb,)), ((), ())), preferred_element_type=F32)


def attention_body(
    meta, q_ref, go_ref, k_ref, v_ref, tk_ref, tv_ref, sk_ref, sv_ref, ok_ref, ov_ref,
    dq_ref, own_ref, tail_ref, sink_ref, ks, vs, ssk, ssv, kst, sst, acc, sacc,
):
    g = pl.program_id(0)

    ks[: TAIL * B] = tk_ref[...].reshape(TAIL * B, D)
    ks[TAIL * B :] = k_ref[...].reshape(ROW * B, D)
    vs[: TAIL * B] = tv_ref[...].reshape(TAIL * B, D)
    vs[TAIL * B :] = v_ref[...].reshape(ROW * B, D)
    near = pl.ds(pl.multiple_of(meta[META_CORE] * B, B), B)
    far = pl.ds(pl.multiple_of((1 - meta[META_CORE]) * B, B), B)
    ssk[near, :] = sk_ref[...]
    ssv[near, :] = sv_ref[...]
    ssk[far, :] = ok_ref[...]
    ssv[far, :] = ov_ref[...]
    kst[...] = ks[...].T
    sst[...] = ssk[...].T
    acc[...] = jnp.zeros_like(acc)
    sacc[...] = jnp.zeros_like(sacc)

    ksink = ssk[...]
    vsink = ssv[...]
    ksinkt = sst[...]
    key = lax.broadcasted_iota(jnp.int32, (B, PAIR * B), 0)
    query = lax.broadcasted_iota(jnp.int32, (B, PAIR * B), 1) % B
    causal = key <= query

    def bias(allowed):
        return jnp.concatenate(
            [jnp.full((1, B), jnp.where(ok, 0.0, NEG_FILL), F32) for ok in allowed], 1
        )

    for n in range(ROW):
        block = meta[0] + n
        rows = slice(n * B, (n + WMAX) * B)
        kw = ks[rows, :]
        vw = vs[rows, :]
        kwt = kst[:, rows]
        pairs = [range(first, first + PAIR) for first in range(0, GROUP, PAIR)]
        first_products = []
        for heads in pairs:
            q2 = jnp.concatenate([q_ref[n, :, h * D : (h + 1) * D] for h in heads], 0)
            go2 = jnp.concatenate([go_ref[n, :, h * D : (h + 1) * D] for h in heads], 0)
            sw = dot(kw, q2, 1, 1)
            ss = dot(ksink, q2, 1, 1)
            pw = dot(vw, go2, 1, 1)
            ps = dot(vsink, go2, 1, 1)
            scores = [sw[j * B : (j + 1) * B] for j in range(WMAX)]
            scores[TAIL] = jnp.where(causal, scores[TAIL], NEG_FILL)
            scores += [ss[t * B : (t + 1) * B] for t in range(SMAX)]
            grads = [pw[j * B : (j + 1) * B] for j in range(WMAX)]
            grads += [ps[t * B : (t + 1) * B] for t in range(SMAX)]
            first_products.append((q2, go2, scores, grads))

        softmaxes = []
        for heads, (_, _, scores, grads) in zip(pairs, first_products):
            window = [meta[1 + g * GROUP + h] for h in heads]
            sink = [meta[1 + Q_LOCAL + g * GROUP + h] for h in heads]
            biases = [
                bias([(block >= TAIL - j) & (TAIL - j < w) for w in window]) for j in range(TAIL)
            ]
            biases += [jnp.zeros((1, PAIR * B), F32)]
            biases += [
                bias([(t < c) & (t <= block - w) for w, c in zip(window, sink)]) for t in range(SMAX)
            ]
            tops = [
                jnp.max(s, 0, keepdims=True) * EXP2_SCALE + extra for s, extra in zip(scores, biases)
            ]
            top = tops[0]
            for t in tops[1:]:
                top = jnp.maximum(top, t)
            exps = [jnp.exp2(s * EXP2_SCALE - (top - extra)) for s, extra in zip(scores, biases)]
            total = exps[0]
            product = exps[0] * grads[0]
            for e, p in zip(exps[1:], grads[1:]):
                total = total + e
                product = product + e * p
            inverse = 1.0 / jnp.sum(total, 0, keepdims=True)
            row_dot = jnp.sum(product, 0, keepdims=True) * inverse
            weights = [e * inverse for e in exps]
            rounded = [w.astype(BF16) for w in weights]
            dscores = [(w * (p - row_dot)).astype(BF16) for w, p in zip(weights, grads)]
            softmaxes.append(
                [
                    jnp.concatenate(rows, 0)
                    for rows in (rounded[:WMAX], rounded[WMAX:], dscores[:WMAX], dscores[WMAX:])
                ]
            )

        sums = []
        for heads, (q2, go2, _, _), (wb_window, wb_sink, ds_window, ds_sink) in zip(
            pairs, first_products, softmaxes
        ):
            sums.append(
                [
                    dot(ds_window, q2, 1, 0),
                    dot(wb_window, go2, 1, 0),
                    dot(ds_sink, q2, 1, 0),
                    dot(wb_sink, go2, 1, 0),
                ]
            )
            dqt = (dot(kwt, ds_window, 1, 0) + dot(ksinkt, ds_sink, 1, 0)) * SCALE
            for n2, h in enumerate(heads):
                dq_ref[n, :, h * D : (h + 1) * D] = dqt[:, n2 * B : (n2 + 1) * B].T.astype(BF16)
        acc[0, rows, :] += sums[0][0] + sums[1][0]
        acc[1, rows, :] += sums[0][1] + sums[1][1]
        sacc[0] += sums[0][2] + sums[1][2]
        sacc[1] += sums[0][3] + sums[1][3]

    own_ref[0, 0] = acc[0, TAIL * B :] * SCALE
    own_ref[0, 1] = acc[1, TAIL * B :]
    tail_ref[0, 0] = (acc[0, : TAIL * B] * SCALE).astype(BF16)
    tail_ref[0, 1] = acc[1, : TAIL * B].astype(BF16)
    for t in range(SMAX):
        sink_ref[t, 0, 0] = sacc[0, t * B : (t + 1) * B] * SCALE
        sink_ref[t, 0, 1] = sacc[1, t * B : (t + 1) * B]


def attention(meta, qgo, kv, tail, sink, other, interpret=False):
    wide = pl.BlockSpec((ROW, B, GROUP * D), lambda g, m: (0, 0, g))
    wide_go = pl.BlockSpec((ROW, B, GROUP * D), lambda g, m: (0, 0, KV_LOCAL + g))

    def pair(count):
        return [
            pl.BlockSpec((count, B, D), lambda g, m: (0, 0, g)),
            pl.BlockSpec((count, B, D), lambda g, m: (0, 0, KV_LOCAL + g)),
        ]

    one = [
        pl.BlockSpec((B, D), lambda g, m: (0, g)),
        pl.BlockSpec((B, D), lambda g, m: (0, KV_LOCAL + g)),
    ]

    def result(rows, dtype):
        return (
            pl.BlockSpec((1, 2, rows * B, D), lambda g, m: (g, 0, 0, 0)),
            jax.ShapeDtypeStruct((KV_LOCAL, 2, rows * B, D), dtype),
        )

    results = [
        (wide, jax.ShapeDtypeStruct((ROW, B, Q_LOCAL * D + KV_COLUMNS), BF16)),
        result(ROW, F32),
        result(TAIL, BF16),
        (
            pl.BlockSpec((SMAX, 1, 2, B, D), lambda g, m: (0, g, 0, 0, 0)),
            jax.ShapeDtypeStruct((SMAX, KV_LOCAL, 2, B, D), F32),
        ),
    ]
    return pl.pallas_call(
        attention_body,
        grid_spec=pltpu.PrefetchScalarGridSpec(
            num_scalar_prefetch=1,
            grid=(KV_LOCAL,),
            in_specs=[wide, wide_go] + pair(ROW) + pair(TAIL) + one + one,
            out_specs=[r[0] for r in results],
            scratch_shapes=[
                pltpu.VMEM(((TAIL + ROW) * B, D), BF16),
                pltpu.VMEM(((TAIL + ROW) * B, D), BF16),
                pltpu.VMEM((SMAX * B, D), BF16),
                pltpu.VMEM((SMAX * B, D), BF16),
                pltpu.VMEM((D, (TAIL + ROW) * B), BF16),
                pltpu.VMEM((D, SMAX * B), BF16),
                pltpu.VMEM((2, (TAIL + ROW) * B, D), F32),
                pltpu.VMEM((2, SMAX * B, D), F32),
            ],
        ),
        out_shape=[r[1] for r in results],
        compiler_params=pltpu.CompilerParams(vmem_limit_bytes=48 * MIB),
        interpret=interpret,
    )(meta, qgo, qgo, kv, kv, tail, tail, sink, sink, other, other)


def line(y, z, core):
    return ((z % 4 * 8 + y) * 2 + z // 4) * 2 + core


def at(x, core):
    return x * 32 + core


def moved(moves):
    return [(line(*p, 0), line(*q, 0)) for p, q in moves] + [
        (line(*p[::-1], 1), line(*q[::-1], 1)) for p, q in moves
    ]


ROUNDS = (((4, 0), (2, 0), (6, 0)), ((0, 4), (1, 4), (1, 0)), ((0, 2), (0, 1), (0, 7)))


def spread():
    holders = [(0, 0)]
    rounds = []
    for offsets in ROUNDS:
        moves = [
            [((a, b), ((a + da) % 8, (b + db) % 8)) for a, b in holders] for da, db in offsets
        ]
        rounds.append([moved(m) for m in moves])
        holders = holders + [q for m in moves for _, q in m]
    return rounds


def gather():
    def inner(end, step):
        return end + step if end == 0 else end - step

    ends = (0, 7)
    rounds = [
        [[((inner(y, n), z), (y, z)) for y in ends for z in range(8)] for n in (3, 2, 1)],
        [[((y, inner(z, n)), (y, z)) for y in ends for z in ends] for n in (3, 2, 1)],
        [[(corner, (0, 0))] for corner in ((7, 7), (7, 0), (0, 7))],
    ]
    return [
        [[(line(*p, c), line(*q, c)) for p, q in moves for c in range(2)] for moves in permutes]
        for permutes in rounds
    ]


def exchanged(value, axes):
    return lax.all_to_all(value, axes, split_axis=0, concat_axis=0, tiled=False)


def summed(total, permutes):
    send = total.astype(BF16)
    for got in [lax.ppermute(send, LINE, pairs) for pairs in permutes]:
        total = total + got.astype(F32)
    return total


def after(value, *others):
    return lax.optimization_barrier((value, others))[0]


def shards(queries, keys, values, output_gradient, windows, sinks):
    core = lax.axis_index("core")
    run = lax.axis_index(("y", "zh", "core")) * 4 + lax.axis_index("zl")
    x = lax.axis_index("x")
    meta = jnp.concatenate(
        [
            (run * ROW)[None].astype(jnp.int32),
            lax.dynamic_slice_in_dim(windows, x * Q_LOCAL, Q_LOCAL),
            lax.dynamic_slice_in_dim(sinks, x * Q_LOCAL, Q_LOCAL),
            core[None].astype(jnp.int32),
        ]
    )
    runs = [(run // 4 // 4, run // 4 // 2 % 2 * 4 + run % 4, run // 4 % 2) for run in range(128)]
    to_next = [(line(*a), line(*b)) for a, b in zip(runs[:-1], runs[1:])]
    swap = [(0, 1), (1, 0)]

    kv_split = split_pair(keys[0], values[0])
    qgo_split = split_pair(after(queries[0], kv_split), output_gradient[0])
    kv = after(exchanged(kv_split, "x"), qgo_split)
    qgo = exchanged(qgo_split, "x")
    tail = lax.ppermute(kv[ROW - TAIL :], LINE, to_next)
    sink = lax.ppermute(kv[1], LINE, [(line(0, 0, 0), line(0, 0, 1))])
    sink = jnp.where(run == 0, kv[0], sink)
    for step, permutes in enumerate(spread()):
        if step == 2:
            sink = after(sink, tail)
        got = [lax.ppermute(sink, LINE, pairs) for pairs in permutes]
        sink = sink + got[0] + got[1] + got[2]
    other = lax.ppermute(sink, "core", swap)
    dq, own, tail_grad, sink_grad = attention(meta, qgo, kv, tail, sink, other)

    tail_back = lax.ppermute(tail_grad, LINE, [(b, a) for a, b in to_next])
    total = lax.dynamic_index_in_dim(sink_grad, core, 0, False)
    away = lax.dynamic_index_in_dim(sink_grad, 1 - core, 0, False).astype(BF16)
    total = total + lax.ppermute(away, "core", swap).astype(F32)
    rounds = gather()
    total = summed(total, rounds[0])
    grads = with_key_grads(dq, own, after(tail_back, total))
    parts = exchanged(grads, "x")
    dq_tokens = join_columns(parts, Q_LOCAL * D)
    total = after(total, grads)
    for permutes in rounds[1:]:
        total = summed(total, permutes)
    total = after(total, parts)
    total = total.astype(BF16)

    pieces = [
        lax.ppermute(total, AXES, [(at(j, c), at(c, 0)) for c in range(SMAX)]) for j in range(ROW)
    ]
    dk, dv = join_pair(parts, pieces)
    return dq_tokens[None], dk[None], dv[None]


def solution(mesh):
    split = Mesh(mesh.devices.reshape(SIZES), AXES)
    tokens = P(("y", "zh", "core"), ("zl", "x"), None)
    return jax.shard_map(
        shards,
        mesh=split,
        in_specs=(tokens, tokens, tokens, tokens, P(), P()),
        out_specs=(tokens, tokens, tokens),
        check_vma=False,
    )
```

```python
import math

import jax
import jax.numpy as jnp
from jax import lax
from jax.experimental import pallas as pl
from jax.experimental.pallas import tpu as pltpu
from jax.sharding import Mesh, PartitionSpec as P

QUERY_HEADS = 32
KEY_VALUE_HEADS = 8
HEAD_DIMENSION = 128
BLOCK_TOKENS = 128
WMAX = 4
SMAX = 2
NEG_FILL = -1e30

AXES = ("zl", "x", "y", "zh", "core")
SIZES = (4, 4, 8, 2, 2)
LINE = ("zl", "y", "zh", "core")
ROW = 4
KV_LOCAL = KEY_VALUE_HEADS // ROW
GROUP = QUERY_HEADS // KEY_VALUE_HEADS
Q_LOCAL = KV_LOCAL * GROUP
TAIL = WMAX - 1
KV_COLUMNS = 2 * KV_LOCAL * HEAD_DIMENSION
PAIR = 2
D = HEAD_DIMENSION
B = BLOCK_TOKENS
SCALE = 1.0 / math.sqrt(HEAD_DIMENSION)
EXP2_SCALE = SCALE * math.log2(math.e)
META_CORE = 1 + 2 * Q_LOCAL
MIB = 1024 * 1024
F32 = jnp.float32
BF16 = jnp.bfloat16


ANY = pl.BlockSpec(memory_space=pl.ANY)
SMALL = pltpu.CompilerParams(vmem_limit_bytes=6 * MIB)


def split_pair(first, second):
    width = first.shape[1] // ROW

    def body(a, b, out, held, sem_in, sem_out):
        reads = []
        for i in range(ROW):
            columns = slice(i * width, (i + 1) * width)
            reads.append(
                pltpu.make_async_copy(a.at[:, columns], held.at[i, :, :width], sem_in.at[2 * i])
            )
            reads.append(
                pltpu.make_async_copy(b.at[:, columns], held.at[i, :, width:], sem_in.at[2 * i + 1])
            )
        for copy in reads:
            copy.start()
        writes = []
        for i in range(ROW):
            reads[2 * i].wait()
            reads[2 * i + 1].wait()
            writes.append(pltpu.make_async_copy(held.at[i], out.at[i], sem_out.at[i]))
            writes[-1].start()
        for copy in writes:
            copy.wait()

    shape = (ROW, B, 2 * width)
    return pl.pallas_call(
        body,
        in_specs=[ANY, ANY],
        out_specs=ANY,
        out_shape=jax.ShapeDtypeStruct(shape, first.dtype),
        scratch_shapes=[
            pltpu.VMEM(shape, first.dtype),
            pltpu.SemaphoreType.DMA((2 * ROW,)),
            pltpu.SemaphoreType.DMA((ROW,)),
        ],
    )(first, second)


def join_columns(parts, width):
    def body(src, out, held, sem_in, sem_out):
        reads = [
            pltpu.make_async_copy(src.at[i, :, :width], held.at[i], sem_in.at[i])
            for i in range(ROW)
        ]
        for copy in reads:
            copy.start()
        writes = []
        for i in range(ROW):
            reads[i].wait()
            columns = slice(i * width, (i + 1) * width)
            writes.append(pltpu.make_async_copy(held.at[i], out.at[:, columns], sem_out.at[i]))
            writes[-1].start()
        for copy in writes:
            copy.wait()

    return pl.pallas_call(
        body,
        in_specs=[ANY],
        out_specs=ANY,
        out_shape=jax.ShapeDtypeStruct((B, ROW * width), parts.dtype),
        scratch_shapes=[
            pltpu.VMEM((ROW, B, width), parts.dtype),
            pltpu.SemaphoreType.DMA((ROW,)),
            pltpu.SemaphoreType.DMA((ROW,)),
        ],
        compiler_params=SMALL,
    )(parts)


def with_key_grads(dq, own, tail):
    def body(_, own_ref, tail_ref, out):
        for b in range(ROW):
            for n in range(2 * KV_LOCAL):
                g, which = divmod(n, 2)
                total = own_ref[g, which, b * B : (b + 1) * B]
                if b >= ROW - TAIL:
                    start = (b - (ROW - TAIL)) * B
                    total = total + tail_ref[g, which, start : start + B].astype(F32)
                out[b, :, n * D : (n + 1) * D] = total.astype(BF16)

    return pl.pallas_call(
        body,
        grid=(1,),
        in_specs=[
            ANY,
            pl.BlockSpec(own.shape, lambda i: (0, 0, 0, 0)),
            pl.BlockSpec(tail.shape, lambda i: (0, 0, 0, 0)),
        ],
        out_specs=pl.BlockSpec((ROW, B, KV_COLUMNS), lambda i: (0, 0, Q_LOCAL * D // KV_COLUMNS)),
        out_shape=jax.ShapeDtypeStruct(dq.shape, dq.dtype),
        input_output_aliases={0: 0},
        compiler_params=SMALL,
    )(dq, own, tail)


def join_pair(parts, pieces):
    def body(src, *refs):
        extra = refs[: 2 * KV_LOCAL]
        for i in range(ROW):
            for n in range(2 * KV_LOCAL):
                g, which = divmod(n, 2)
                out = refs[2 * KV_LOCAL + which]
                total = src[i, :, n * D : (n + 1) * D].astype(F32) + extra[n][i].astype(F32)
                h = i * KV_LOCAL + g
                out[:, h * D : (h + 1) * D] = total.astype(out.dtype)

    piece = pl.BlockSpec(pieces[0].shape, lambda i: (0, 0, 0))
    width = KEY_VALUE_HEADS * D
    out = jax.ShapeDtypeStruct((B, width), parts.dtype)
    return pl.pallas_call(
        body,
        grid=(1,),
        in_specs=[
            pl.BlockSpec((ROW, B, KV_COLUMNS), lambda i: (0, 0, Q_LOCAL * D // KV_COLUMNS))
        ]
        + [piece] * (2 * KV_LOCAL),
        out_specs=[pl.BlockSpec((B, width), lambda i: (0, 0))] * 2,
        out_shape=[out, out],
        compiler_params=SMALL,
    )(parts, *pieces)


def dot(a, b, ca, cb):
    return lax.dot_general(a, b, (((ca,), (cb,)), ((), ())), preferred_element_type=F32)


def attention_body(
    meta, q_ref, go_ref, k_ref, v_ref, tk_ref, tv_ref, sk_ref, sv_ref, ok_ref, ov_ref,
    dq_ref, own_ref, tail_ref, sink_ref, ks, vs, ssk, ssv, kst, sst, acc, sacc,
):
    g = pl.program_id(0)

    ks[: TAIL * B] = tk_ref[...].reshape(TAIL * B, D)
    ks[TAIL * B :] = k_ref[...].reshape(ROW * B, D)
    vs[: TAIL * B] = tv_ref[...].reshape(TAIL * B, D)
    vs[TAIL * B :] = v_ref[...].reshape(ROW * B, D)
    near = pl.ds(pl.multiple_of(meta[META_CORE] * B, B), B)
    far = pl.ds(pl.multiple_of((1 - meta[META_CORE]) * B, B), B)
    ssk[near, :] = sk_ref[...]
    ssv[near, :] = sv_ref[...]
    ssk[far, :] = ok_ref[...]
    ssv[far, :] = ov_ref[...]
    kst[...] = ks[...].T
    sst[...] = ssk[...].T
    acc[...] = jnp.zeros_like(acc)
    sacc[...] = jnp.zeros_like(sacc)

    ksink = ssk[...]
    vsink = ssv[...]
    ksinkt = sst[...]
    key = lax.broadcasted_iota(jnp.int32, (B, PAIR * B), 0)
    query = lax.broadcasted_iota(jnp.int32, (B, PAIR * B), 1) % B
    causal = key <= query

    def bias(allowed):
        return jnp.concatenate(
            [jnp.full((1, B), jnp.where(ok, 0.0, NEG_FILL), F32) for ok in allowed], 1
        )

    for n in range(ROW):
        block = meta[0] + n
        rows = slice(n * B, (n + WMAX) * B)
        kw = ks[rows, :]
        vw = vs[rows, :]
        kwt = kst[:, rows]
        pairs = [range(first, first + PAIR) for first in range(0, GROUP, PAIR)]
        first_products = []
        for heads in pairs:
            q2 = jnp.concatenate([q_ref[n, :, h * D : (h + 1) * D] for h in heads], 0)
            go2 = jnp.concatenate([go_ref[n, :, h * D : (h + 1) * D] for h in heads], 0)
            sw = dot(kw, q2, 1, 1)
            ss = dot(ksink, q2, 1, 1)
            pw = dot(vw, go2, 1, 1)
            ps = dot(vsink, go2, 1, 1)
            scores = [sw[j * B : (j + 1) * B] for j in range(WMAX)]
            scores[TAIL] = jnp.where(causal, scores[TAIL], NEG_FILL)
            scores += [ss[t * B : (t + 1) * B] for t in range(SMAX)]
            grads = [pw[j * B : (j + 1) * B] for j in range(WMAX)]
            grads += [ps[t * B : (t + 1) * B] for t in range(SMAX)]
            first_products.append((q2, go2, scores, grads))

        softmaxes = []
        for heads, (_, _, scores, grads) in zip(pairs, first_products):
            window = [meta[1 + g * GROUP + h] for h in heads]
            sink = [meta[1 + Q_LOCAL + g * GROUP + h] for h in heads]
            biases = [
                bias([(block >= TAIL - j) & (TAIL - j < w) for w in window]) for j in range(TAIL)
            ]
            biases += [jnp.zeros((1, PAIR * B), F32)]
            biases += [
                bias([(t < c) & (t <= block - w) for w, c in zip(window, sink)]) for t in range(SMAX)
            ]
            tops = [
                jnp.max(s, 0, keepdims=True) * EXP2_SCALE + extra for s, extra in zip(scores, biases)
            ]
            top = tops[0]
            for t in tops[1:]:
                top = jnp.maximum(top, t)
            exps = [jnp.exp2(s * EXP2_SCALE - (top - extra)) for s, extra in zip(scores, biases)]
            total = exps[0]
            product = exps[0] * grads[0]
            for e, p in zip(exps[1:], grads[1:]):
                total = total + e
                product = product + e * p
            inverse = 1.0 / jnp.sum(total, 0, keepdims=True)
            row_dot = jnp.sum(product, 0, keepdims=True) * inverse
            weights = [e * inverse for e in exps]
            rounded = [w.astype(BF16) for w in weights]
            dscores = [(w * (p - row_dot)).astype(BF16) for w, p in zip(weights, grads)]
            softmaxes.append(
                [
                    jnp.concatenate(rows, 0)
                    for rows in (rounded[:WMAX], rounded[WMAX:], dscores[:WMAX], dscores[WMAX:])
                ]
            )

        sums = []
        for heads, (q2, go2, _, _), (wb_window, wb_sink, ds_window, ds_sink) in zip(
            pairs, first_products, softmaxes
        ):
            sums.append(
                [
                    dot(ds_window, q2, 1, 0),
                    dot(wb_window, go2, 1, 0),
                    dot(ds_sink, q2, 1, 0),
                    dot(wb_sink, go2, 1, 0),
                ]
            )
            dqt = (dot(kwt, ds_window, 1, 0) + dot(ksinkt, ds_sink, 1, 0)) * SCALE
            for n2, h in enumerate(heads):
                dq_ref[n, :, h * D : (h + 1) * D] = dqt[:, n2 * B : (n2 + 1) * B].T.astype(BF16)
        acc[0, rows, :] += sums[0][0] + sums[1][0]
        acc[1, rows, :] += sums[0][1] + sums[1][1]
        sacc[0] += sums[0][2] + sums[1][2]
        sacc[1] += sums[0][3] + sums[1][3]

    own_ref[0, 0] = acc[0, TAIL * B :] * SCALE
    own_ref[0, 1] = acc[1, TAIL * B :]
    tail_ref[0, 0] = (acc[0, : TAIL * B] * SCALE).astype(BF16)
    tail_ref[0, 1] = acc[1, : TAIL * B].astype(BF16)
    for t in range(SMAX):
        sink_ref[t, 0, 0] = sacc[0, t * B : (t + 1) * B] * SCALE
        sink_ref[t, 0, 1] = sacc[1, t * B : (t + 1) * B]


def attention(meta, qgo, kv, tail, sink, other, interpret=False):
    wide = pl.BlockSpec((ROW, B, GROUP * D), lambda g, m: (0, 0, g))
    wide_go = pl.BlockSpec((ROW, B, GROUP * D), lambda g, m: (0, 0, KV_LOCAL + g))

    def pair(count):
        return [
            pl.BlockSpec((count, B, D), lambda g, m: (0, 0, g)),
            pl.BlockSpec((count, B, D), lambda g, m: (0, 0, KV_LOCAL + g)),
        ]

    one = [
        pl.BlockSpec((B, D), lambda g, m: (0, g)),
        pl.BlockSpec((B, D), lambda g, m: (0, KV_LOCAL + g)),
    ]

    def result(rows, dtype):
        return (
            pl.BlockSpec((1, 2, rows * B, D), lambda g, m: (g, 0, 0, 0)),
            jax.ShapeDtypeStruct((KV_LOCAL, 2, rows * B, D), dtype),
        )

    results = [
        (wide, jax.ShapeDtypeStruct((ROW, B, Q_LOCAL * D + KV_COLUMNS), BF16)),
        result(ROW, F32),
        result(TAIL, BF16),
        (
            pl.BlockSpec((SMAX, 1, 2, B, D), lambda g, m: (0, g, 0, 0, 0)),
            jax.ShapeDtypeStruct((SMAX, KV_LOCAL, 2, B, D), F32),
        ),
    ]
    return pl.pallas_call(
        attention_body,
        grid_spec=pltpu.PrefetchScalarGridSpec(
            num_scalar_prefetch=1,
            grid=(KV_LOCAL,),
            in_specs=[wide, wide_go] + pair(ROW) + pair(TAIL) + one + one,
            out_specs=[r[0] for r in results],
            scratch_shapes=[
                pltpu.VMEM(((TAIL + ROW) * B, D), BF16),
                pltpu.VMEM(((TAIL + ROW) * B, D), BF16),
                pltpu.VMEM((SMAX * B, D), BF16),
                pltpu.VMEM((SMAX * B, D), BF16),
                pltpu.VMEM((D, (TAIL + ROW) * B), BF16),
                pltpu.VMEM((D, SMAX * B), BF16),
                pltpu.VMEM((2, (TAIL + ROW) * B, D), F32),
                pltpu.VMEM((2, SMAX * B, D), F32),
            ],
        ),
        out_shape=[r[1] for r in results],
        compiler_params=pltpu.CompilerParams(vmem_limit_bytes=48 * MIB),
        interpret=interpret,
    )(meta, qgo, qgo, kv, kv, tail, tail, sink, sink, other, other)


def line(y, z, core):
    return ((z % 4 * 8 + y) * 2 + z // 4) * 2 + core


def at(zl, x, core):
    return zl * 128 + x * 32 + core


def moved(moves):
    return [(line(*p, 0), line(*q, 0)) for p, q in moves] + [
        (line(*p[::-1], 1), line(*q[::-1], 1)) for p, q in moves
    ]


ROUNDS = (((4, 0), (2, 0), (6, 0)), ((0, 4), (1, 4), (1, 0)), ((0, 2), (0, 1), (0, 7)))


def spread():
    holders = [(0, 0)]
    rounds = []
    for offsets in ROUNDS:
        moves = [
            [((a, b), ((a + da) % 8, (b + db) % 8)) for a, b in holders] for da, db in offsets
        ]
        rounds.append([moved(m) for m in moves])
        holders = holders + [q for m in moves for _, q in m]
    return rounds


def gather():
    cores = range(2)

    def inner(end, step):
        return end + step if end == 0 else end - step

    return [
        [
            [(line(inner(y, n), z, c), line(y, z, c)) for y in (0, 7) for z in range(8) for c in cores]
            for n in (3, 2, 1)
        ],
        [
            [(line(y, z + up, c), line(0, z, c)) for z in range(4) for c in cores]
            for y, up in ((7, 4), (0, 4), (7, 0))
        ],
    ]


def exchanged(value, axes):
    return lax.all_to_all(value, axes, split_axis=0, concat_axis=0, tiled=False)


def summed(total, permutes):
    send = total.astype(BF16)
    for got in [lax.ppermute(send, LINE, pairs) for pairs in permutes]:
        total = total + got.astype(F32)
    return total


def after(value, *others):
    return lax.optimization_barrier((value, others))[0]


def shards(queries, keys, values, output_gradient, windows, sinks):
    core = lax.axis_index("core")
    zl = lax.axis_index("zl")
    run = lax.axis_index(("y", "zh", "core")) * 4 + zl
    x = lax.axis_index("x")
    meta = jnp.concatenate(
        [
            (run * ROW)[None].astype(jnp.int32),
            lax.dynamic_slice_in_dim(windows, x * Q_LOCAL, Q_LOCAL),
            lax.dynamic_slice_in_dim(sinks, x * Q_LOCAL, Q_LOCAL),
            core[None].astype(jnp.int32),
        ]
    )
    runs = [(run // 4 // 4, run // 4 // 2 % 2 * 4 + run % 4, run // 4 % 2) for run in range(128)]
    to_next = [(line(*a), line(*b)) for a, b in zip(runs[:-1], runs[1:])]
    swap = [(0, 1), (1, 0)]

    kv_split = split_pair(keys[0], values[0])
    qgo_split = split_pair(after(queries[0], kv_split), output_gradient[0])
    kv = after(exchanged(kv_split, "x"), qgo_split)
    qgo = exchanged(qgo_split, "x")
    tail = lax.ppermute(kv[ROW - TAIL :], LINE, to_next)
    sink = lax.ppermute(kv[1], LINE, [(line(0, 0, 0), line(0, 0, 1))])
    sink = jnp.where(run == 0, kv[0], sink)
    for step, permutes in enumerate(spread()):
        if step == 2:
            sink = after(sink, tail)
        got = [lax.ppermute(sink, LINE, pairs) for pairs in permutes]
        sink = sink + got[0] + got[1] + got[2]
    other = lax.ppermute(sink, "core", swap)
    dq, own, tail_grad, sink_grad = attention(meta, qgo, kv, tail, sink, other)

    tail_back = lax.ppermute(tail_grad, LINE, [(b, a) for a, b in to_next])
    total = lax.dynamic_index_in_dim(sink_grad, core, 0, False)
    away = lax.dynamic_index_in_dim(sink_grad, 1 - core, 0, False).astype(BF16)
    total = total + lax.ppermute(away, "core", swap).astype(F32)
    shares = exchanged(total.astype(BF16).reshape(2 * KV_LOCAL, B, D), "zl")
    total = jnp.sum(shares.astype(F32), 0)
    grads = with_key_grads(dq, own, after(tail_back, total))
    parts = exchanged(grads, "x")
    dq_tokens = join_columns(parts, Q_LOCAL * D)
    total = after(total, grads)
    for permutes in gather():
        total = summed(total, permutes)
    total = total.astype(BF16)

    blocks = range(SMAX)
    rows = [
        lax.ppermute(total, AXES, [(at(z, j, c), at(z, c, 0)) for z in range(4) for c in blocks])
        for j in range(ROW)
    ]
    rows = after(jnp.stack(rows), parts)
    pieces = [jnp.where(zl == 0, rows, jnp.zeros_like(rows))]
    pieces += [
        lax.ppermute(rows, AXES, [(at(z, c, 0), at(0, c, 0)) for c in blocks]) for z in range(1, 4)
    ]
    dk, dv = join_pair(parts, pieces)
    return dq_tokens[None], dk[None], dv[None]


def solution(mesh):
    split = Mesh(mesh.devices.reshape(SIZES), AXES)
    tokens = P(("y", "zh", "core"), ("zl", "x"), None)
    return jax.shard_map(
        shards,
        mesh=split,
        in_specs=(tokens, tokens, tokens, tokens, P(), P()),
        out_specs=(tokens, tokens, tokens),
        check_vma=False,
    )
```

```python
import math

import jax
import jax.numpy as jnp
from jax import lax
from jax.experimental import pallas as pl
from jax.experimental.pallas import tpu as pltpu
from jax.sharding import Mesh, PartitionSpec as P

QUERY_HEADS = 32
KEY_VALUE_HEADS = 8
HEAD_DIMENSION = 128
BLOCK_TOKENS = 128
WMAX = 4
SMAX = 2
NEG_FILL = -1e30

AXES = ("zl", "x", "y", "zh", "core")
SIZES = (4, 4, 8, 2, 2)
LINE = ("zl", "y", "zh", "core")
ROW = 4
KV_LOCAL = KEY_VALUE_HEADS // ROW
GROUP = QUERY_HEADS // KEY_VALUE_HEADS
Q_LOCAL = KV_LOCAL * GROUP
TAIL = WMAX - 1
KV_COLUMNS = 2 * KV_LOCAL * HEAD_DIMENSION
PAIR = 2
D = HEAD_DIMENSION
B = BLOCK_TOKENS
SCALE = 1.0 / math.sqrt(HEAD_DIMENSION)
EXP2_SCALE = SCALE * math.log2(math.e)
META_CORE = 1 + 2 * Q_LOCAL
MIB = 1024 * 1024
F32 = jnp.float32
BF16 = jnp.bfloat16


ANY = pl.BlockSpec(memory_space=pl.ANY)
SMALL = pltpu.CompilerParams(vmem_limit_bytes=6 * MIB)


def split_pair(first, second):
    width = first.shape[1] // ROW

    def body(a, b, out, held, sem_in, sem_out):
        reads = []
        for i in range(ROW):
            columns = slice(i * width, (i + 1) * width)
            reads.append(
                pltpu.make_async_copy(a.at[:, columns], held.at[i, :, :width], sem_in.at[2 * i])
            )
            reads.append(
                pltpu.make_async_copy(b.at[:, columns], held.at[i, :, width:], sem_in.at[2 * i + 1])
            )
        for copy in reads:
            copy.start()
        writes = []
        for i in range(ROW):
            reads[2 * i].wait()
            reads[2 * i + 1].wait()
            writes.append(pltpu.make_async_copy(held.at[i], out.at[i], sem_out.at[i]))
            writes[-1].start()
        for copy in writes:
            copy.wait()

    shape = (ROW, B, 2 * width)
    return pl.pallas_call(
        body,
        in_specs=[ANY, ANY],
        out_specs=ANY,
        out_shape=jax.ShapeDtypeStruct(shape, first.dtype),
        scratch_shapes=[
            pltpu.VMEM(shape, first.dtype),
            pltpu.SemaphoreType.DMA((2 * ROW,)),
            pltpu.SemaphoreType.DMA((ROW,)),
        ],
    )(first, second)


def join_columns(parts, width):
    def body(src, out, held, sem_in, sem_out):
        reads = [
            pltpu.make_async_copy(src.at[i, :, :width], held.at[i], sem_in.at[i])
            for i in range(ROW)
        ]
        for copy in reads:
            copy.start()
        writes = []
        for i in range(ROW):
            reads[i].wait()
            columns = slice(i * width, (i + 1) * width)
            writes.append(pltpu.make_async_copy(held.at[i], out.at[:, columns], sem_out.at[i]))
            writes[-1].start()
        for copy in writes:
            copy.wait()

    return pl.pallas_call(
        body,
        in_specs=[ANY],
        out_specs=ANY,
        out_shape=jax.ShapeDtypeStruct((B, ROW * width), parts.dtype),
        scratch_shapes=[
            pltpu.VMEM((ROW, B, width), parts.dtype),
            pltpu.SemaphoreType.DMA((ROW,)),
            pltpu.SemaphoreType.DMA((ROW,)),
        ],
        compiler_params=SMALL,
    )(parts)


def with_key_grads(dq, own, tail):
    def body(_, own_ref, tail_ref, out):
        for b in range(ROW):
            for n in range(2 * KV_LOCAL):
                g, which = divmod(n, 2)
                total = own_ref[g, which, b * B : (b + 1) * B]
                if b >= ROW - TAIL:
                    start = (b - (ROW - TAIL)) * B
                    total = total + tail_ref[g, which, start : start + B].astype(F32)
                out[b, :, n * D : (n + 1) * D] = total.astype(BF16)

    return pl.pallas_call(
        body,
        grid=(1,),
        in_specs=[
            ANY,
            pl.BlockSpec(own.shape, lambda i: (0, 0, 0, 0)),
            pl.BlockSpec(tail.shape, lambda i: (0, 0, 0, 0)),
        ],
        out_specs=pl.BlockSpec((ROW, B, KV_COLUMNS), lambda i: (0, 0, Q_LOCAL * D // KV_COLUMNS)),
        out_shape=jax.ShapeDtypeStruct(dq.shape, dq.dtype),
        input_output_aliases={0: 0},
        compiler_params=SMALL,
    )(dq, own, tail)


def join_pair(parts, pieces):
    def body(src, *refs):
        extra = refs[:ROW]
        for i in range(ROW):
            for n in range(2 * KV_LOCAL):
                g, which = divmod(n, 2)
                out = refs[ROW + which]
                total = src[i, :, n * D : (n + 1) * D].astype(F32) + extra[i][g, which].astype(F32)
                h = i * KV_LOCAL + g
                out[:, h * D : (h + 1) * D] = total.astype(out.dtype)

    piece = pl.BlockSpec(pieces[0].shape, lambda i: (0, 0, 0, 0))
    width = KEY_VALUE_HEADS * D
    out = jax.ShapeDtypeStruct((B, width), parts.dtype)
    return pl.pallas_call(
        body,
        grid=(1,),
        in_specs=[
            pl.BlockSpec((ROW, B, KV_COLUMNS), lambda i: (0, 0, Q_LOCAL * D // KV_COLUMNS))
        ]
        + [piece] * ROW,
        out_specs=[pl.BlockSpec((B, width), lambda i: (0, 0))] * 2,
        out_shape=[out, out],
        compiler_params=SMALL,
    )(parts, *pieces)


def dot(a, b, ca, cb):
    return lax.dot_general(a, b, (((ca,), (cb,)), ((), ())), preferred_element_type=F32)


def attention_body(
    meta, q_ref, go_ref, k_ref, v_ref, tk_ref, tv_ref, sk_ref, sv_ref, ok_ref, ov_ref,
    dq_ref, own_ref, tail_ref, sink_ref, ks, vs, ssk, ssv, kst, sst, acc, sacc,
):
    g = pl.program_id(0)

    ks[: TAIL * B] = tk_ref[...].reshape(TAIL * B, D)
    ks[TAIL * B :] = k_ref[...].reshape(ROW * B, D)
    vs[: TAIL * B] = tv_ref[...].reshape(TAIL * B, D)
    vs[TAIL * B :] = v_ref[...].reshape(ROW * B, D)
    near = pl.ds(pl.multiple_of(meta[META_CORE] * B, B), B)
    far = pl.ds(pl.multiple_of((1 - meta[META_CORE]) * B, B), B)
    ssk[near, :] = sk_ref[...]
    ssv[near, :] = sv_ref[...]
    ssk[far, :] = ok_ref[...]
    ssv[far, :] = ov_ref[...]
    kst[...] = ks[...].T
    sst[...] = ssk[...].T
    acc[...] = jnp.zeros_like(acc)
    sacc[...] = jnp.zeros_like(sacc)

    ksink = ssk[...]
    vsink = ssv[...]
    ksinkt = sst[...]
    key = lax.broadcasted_iota(jnp.int32, (B, PAIR * B), 0)
    query = lax.broadcasted_iota(jnp.int32, (B, PAIR * B), 1) % B
    causal = key <= query

    def bias(allowed):
        return jnp.concatenate(
            [jnp.full((1, B), jnp.where(ok, 0.0, NEG_FILL), F32) for ok in allowed], 1
        )

    for n in range(ROW):
        block = meta[0] + n
        rows = slice(n * B, (n + WMAX) * B)
        kw = ks[rows, :]
        vw = vs[rows, :]
        kwt = kst[:, rows]
        pairs = [range(first, first + PAIR) for first in range(0, GROUP, PAIR)]
        first_products = []
        for heads in pairs:
            q2 = jnp.concatenate([q_ref[n, :, h * D : (h + 1) * D] for h in heads], 0)
            go2 = jnp.concatenate([go_ref[n, :, h * D : (h + 1) * D] for h in heads], 0)
            sw = dot(kw, q2, 1, 1)
            ss = dot(ksink, q2, 1, 1)
            pw = dot(vw, go2, 1, 1)
            ps = dot(vsink, go2, 1, 1)
            scores = [sw[j * B : (j + 1) * B] for j in range(WMAX)]
            scores[TAIL] = jnp.where(causal, scores[TAIL], NEG_FILL)
            scores += [ss[t * B : (t + 1) * B] for t in range(SMAX)]
            grads = [pw[j * B : (j + 1) * B] for j in range(WMAX)]
            grads += [ps[t * B : (t + 1) * B] for t in range(SMAX)]
            first_products.append((q2, go2, scores, grads))

        softmaxes = []
        for heads, (_, _, scores, grads) in zip(pairs, first_products):
            window = [meta[1 + g * GROUP + h] for h in heads]
            sink = [meta[1 + Q_LOCAL + g * GROUP + h] for h in heads]
            biases = [
                bias([(block >= TAIL - j) & (TAIL - j < w) for w in window]) for j in range(TAIL)
            ]
            biases += [jnp.zeros((1, PAIR * B), F32)]
            biases += [
                bias([(t < c) & (t <= block - w) for w, c in zip(window, sink)]) for t in range(SMAX)
            ]
            tops = [
                jnp.max(s, 0, keepdims=True) * EXP2_SCALE + extra for s, extra in zip(scores, biases)
            ]
            top = tops[0]
            for t in tops[1:]:
                top = jnp.maximum(top, t)
            exps = [jnp.exp2(s * EXP2_SCALE - (top - extra)) for s, extra in zip(scores, biases)]
            total = exps[0]
            product = exps[0] * grads[0]
            for e, p in zip(exps[1:], grads[1:]):
                total = total + e
                product = product + e * p
            inverse = 1.0 / jnp.sum(total, 0, keepdims=True)
            row_dot = jnp.sum(product, 0, keepdims=True) * inverse
            weights = [e * inverse for e in exps]
            rounded = [w.astype(BF16) for w in weights]
            dscores = [(w * (p - row_dot)).astype(BF16) for w, p in zip(weights, grads)]
            softmaxes.append(
                [
                    jnp.concatenate(rows, 0)
                    for rows in (rounded[:WMAX], rounded[WMAX:], dscores[:WMAX], dscores[WMAX:])
                ]
            )

        sums = []
        for heads, (q2, go2, _, _), (wb_window, wb_sink, ds_window, ds_sink) in zip(
            pairs, first_products, softmaxes
        ):
            sums.append(
                [
                    dot(ds_window, q2, 1, 0),
                    dot(wb_window, go2, 1, 0),
                    dot(ds_sink, q2, 1, 0),
                    dot(wb_sink, go2, 1, 0),
                ]
            )
            dqt = (dot(kwt, ds_window, 1, 0) + dot(ksinkt, ds_sink, 1, 0)) * SCALE
            for n2, h in enumerate(heads):
                dq_ref[n, :, h * D : (h + 1) * D] = dqt[:, n2 * B : (n2 + 1) * B].T.astype(BF16)
        acc[0, rows, :] += sums[0][0] + sums[1][0]
        acc[1, rows, :] += sums[0][1] + sums[1][1]
        sacc[0] += sums[0][2] + sums[1][2]
        sacc[1] += sums[0][3] + sums[1][3]

    own_ref[0, 0] = acc[0, TAIL * B :] * SCALE
    own_ref[0, 1] = acc[1, TAIL * B :]
    tail_ref[0, 0] = (acc[0, : TAIL * B] * SCALE).astype(BF16)
    tail_ref[0, 1] = acc[1, : TAIL * B].astype(BF16)
    for t in range(SMAX):
        sink_ref[t, 0, 0] = sacc[0, t * B : (t + 1) * B] * SCALE
        sink_ref[t, 0, 1] = sacc[1, t * B : (t + 1) * B]


def attention(meta, qgo, kv, tail, sink, other, interpret=False):
    wide = pl.BlockSpec((ROW, B, GROUP * D), lambda g, m: (0, 0, g))
    wide_go = pl.BlockSpec((ROW, B, GROUP * D), lambda g, m: (0, 0, KV_LOCAL + g))

    def pair(count):
        return [
            pl.BlockSpec((count, B, D), lambda g, m: (0, 0, g)),
            pl.BlockSpec((count, B, D), lambda g, m: (0, 0, KV_LOCAL + g)),
        ]

    one = [
        pl.BlockSpec((B, D), lambda g, m: (0, g)),
        pl.BlockSpec((B, D), lambda g, m: (0, KV_LOCAL + g)),
    ]

    def result(rows, dtype):
        return (
            pl.BlockSpec((1, 2, rows * B, D), lambda g, m: (g, 0, 0, 0)),
            jax.ShapeDtypeStruct((KV_LOCAL, 2, rows * B, D), dtype),
        )

    results = [
        (wide, jax.ShapeDtypeStruct((ROW, B, Q_LOCAL * D + KV_COLUMNS), BF16)),
        result(ROW, F32),
        result(TAIL, BF16),
        (
            pl.BlockSpec((SMAX, 1, 2, B, D), lambda g, m: (0, g, 0, 0, 0)),
            jax.ShapeDtypeStruct((SMAX, KV_LOCAL, 2, B, D), F32),
        ),
    ]
    return pl.pallas_call(
        attention_body,
        grid_spec=pltpu.PrefetchScalarGridSpec(
            num_scalar_prefetch=1,
            grid=(KV_LOCAL,),
            in_specs=[wide, wide_go] + pair(ROW) + pair(TAIL) + one + one,
            out_specs=[r[0] for r in results],
            scratch_shapes=[
                pltpu.VMEM(((TAIL + ROW) * B, D), BF16),
                pltpu.VMEM(((TAIL + ROW) * B, D), BF16),
                pltpu.VMEM((SMAX * B, D), BF16),
                pltpu.VMEM((SMAX * B, D), BF16),
                pltpu.VMEM((D, (TAIL + ROW) * B), BF16),
                pltpu.VMEM((D, SMAX * B), BF16),
                pltpu.VMEM((2, (TAIL + ROW) * B, D), F32),
                pltpu.VMEM((2, SMAX * B, D), F32),
            ],
        ),
        out_shape=[r[1] for r in results],
        compiler_params=pltpu.CompilerParams(vmem_limit_bytes=48 * MIB),
        interpret=interpret,
    )(meta, qgo, qgo, kv, kv, tail, tail, sink, sink, other, other)


def line(y, z, core):
    return ((z % 4 * 8 + y) * 2 + z // 4) * 2 + core


def at(x, core):
    return x * 32 + core


def moved(moves):
    return [(line(*p, 0), line(*q, 0)) for p, q in moves] + [
        (line(*p[::-1], 1), line(*q[::-1], 1)) for p, q in moves
    ]


ROUNDS = (((4, 0), (2, 0), (6, 0)), ((0, 4), (1, 4), (1, 0)), ((0, 2), (0, 1), (0, 7)))


def spread():
    holders = [(0, 0)]
    rounds = []
    for offsets in ROUNDS:
        moves = [
            [((a, b), ((a + da) % 8, (b + db) % 8)) for a, b in holders] for da, db in offsets
        ]
        rounds.append([moved(m) for m in moves])
        holders = holders + [q for m in moves for _, q in m]
    return rounds


def gather():
    def inner(end, step):
        return end + step if end == 0 else end - step

    ends = (0, 7)
    rounds = [
        [[((a, inner(b, n)), (a, b)) for a in range(8) for b in ends] for n in (3, 2, 1)],
        [[((inner(a, n), b), (a, b)) for a in ends for b in ends] for n in (3, 2, 1)],
        [[(corner, (0, 0))] for corner in ((7, 7), (7, 0), (0, 7))],
    ]
    return [[moved(moves) for moves in permutes] for permutes in rounds]


def exchanged(value, axes):
    return lax.all_to_all(value, axes, split_axis=0, concat_axis=0, tiled=False)


def summed(total, permutes):
    send = total.astype(BF16)
    for got in [lax.ppermute(send, LINE, pairs) for pairs in permutes]:
        total = total + got.astype(F32)
    return total


def after(value, *others):
    return lax.optimization_barrier((value, others))[0]


def shards(queries, keys, values, output_gradient, windows, sinks):
    core = lax.axis_index("core")
    run = lax.axis_index(("y", "zh", "core")) * 4 + lax.axis_index("zl")
    x = lax.axis_index("x")
    meta = jnp.concatenate(
        [
            (run * ROW)[None].astype(jnp.int32),
            lax.dynamic_slice_in_dim(windows, x * Q_LOCAL, Q_LOCAL),
            lax.dynamic_slice_in_dim(sinks, x * Q_LOCAL, Q_LOCAL),
            core[None].astype(jnp.int32),
        ]
    )
    runs = [(run // 4 // 4, run // 4 // 2 % 2 * 4 + run % 4, run // 4 % 2) for run in range(128)]
    to_next = [(line(*a), line(*b)) for a, b in zip(runs[:-1], runs[1:])]
    swap = [(0, 1), (1, 0)]

    kv_split = split_pair(keys[0], values[0])
    qgo_split = split_pair(after(queries[0], kv_split), output_gradient[0])
    kv = after(exchanged(kv_split, "x"), qgo_split)
    qgo = exchanged(qgo_split, "x")
    tail = lax.ppermute(kv[ROW - TAIL :], LINE, to_next)
    sink = lax.ppermute(kv[1], LINE, [(line(0, 0, 0), line(0, 0, 1))])
    sink = jnp.where(run == 0, kv[0], sink)
    for step, permutes in enumerate(spread()):
        if step == 2:
            sink = after(sink, tail)
        got = [lax.ppermute(sink, LINE, pairs) for pairs in permutes]
        sink = sink + got[0] + got[1] + got[2]
    other = lax.ppermute(sink, "core", swap)
    dq, own, tail_grad, sink_grad = attention(meta, qgo, kv, tail, sink, other)

    total = lax.dynamic_index_in_dim(sink_grad, core, 0, False)
    away = lax.dynamic_index_in_dim(sink_grad, 1 - core, 0, False).astype(BF16)
    total = total + lax.ppermute(away, "core", swap).astype(F32)
    rounds = gather()
    total = summed(total, rounds[0])
    tail_back = lax.ppermute(after(tail_grad, total), LINE, [(b, a) for a, b in to_next])
    total = summed(total, rounds[1])
    grads = with_key_grads(dq, own, after(tail_back, total))
    parts = exchanged(grads, "x")
    dq_tokens = join_columns(parts, Q_LOCAL * D)
    total = summed(after(total, grads), rounds[2])
    total = total.astype(BF16)

    pieces = [
        lax.ppermute(total, AXES, [(at(j, c), at(c, 0)) for c in range(SMAX)]) for j in range(ROW)
    ]
    dk, dv = join_pair(parts, pieces)
    return dq_tokens[None], dk[None], dv[None]


def solution(mesh):
    split = Mesh(mesh.devices.reshape(SIZES), AXES)
    tokens = P(("y", "zh", "core"), ("zl", "x"), None)
    return jax.shard_map(
        shards,
        mesh=split,
        in_specs=(tokens, tokens, tokens, tokens, P(), P()),
        out_specs=(tokens, tokens, tokens),
        check_vma=False,
    )
```

```python
import math

import jax
import jax.numpy as jnp
from jax import lax
from jax.experimental import pallas as pl
from jax.experimental.pallas import tpu as pltpu
from jax.sharding import Mesh, PartitionSpec as P

QUERY_HEADS = 32
KEY_VALUE_HEADS = 8
HEAD_DIMENSION = 128
BLOCK_TOKENS = 128
WMAX = 4
SMAX = 2
NEG_FILL = -1e30

AXES = ("zl", "x", "y", "zh", "core")
SIZES = (4, 4, 8, 2, 2)
LINE = ("zl", "y", "zh", "core")
ROW = 4
KV_LOCAL = KEY_VALUE_HEADS // ROW
GROUP = QUERY_HEADS // KEY_VALUE_HEADS
Q_LOCAL = KV_LOCAL * GROUP
TAIL = WMAX - 1
KV_COLUMNS = 2 * KV_LOCAL * HEAD_DIMENSION
PAIR = 2
D = HEAD_DIMENSION
B = BLOCK_TOKENS
SCALE = 1.0 / math.sqrt(HEAD_DIMENSION)
EXP2_SCALE = SCALE * math.log2(math.e)
META_CORE = 1 + 2 * Q_LOCAL
MIB = 1024 * 1024
F32 = jnp.float32
BF16 = jnp.bfloat16


ANY = pl.BlockSpec(memory_space=pl.ANY)
SMALL = pltpu.CompilerParams(vmem_limit_bytes=6 * MIB)


def split_pair(first, second):
    width = first.shape[1] // ROW

    def body(a, b, out, held, sem_in, sem_out):
        reads = []
        for i in range(ROW):
            columns = slice(i * width, (i + 1) * width)
            reads.append(
                pltpu.make_async_copy(a.at[:, columns], held.at[i, :, :width], sem_in.at[2 * i])
            )
            reads.append(
                pltpu.make_async_copy(b.at[:, columns], held.at[i, :, width:], sem_in.at[2 * i + 1])
            )
        for copy in reads:
            copy.start()
        writes = []
        for i in range(ROW):
            reads[2 * i].wait()
            reads[2 * i + 1].wait()
            writes.append(pltpu.make_async_copy(held.at[i], out.at[i], sem_out.at[i]))
            writes[-1].start()
        for copy in writes:
            copy.wait()

    shape = (ROW, B, 2 * width)
    return pl.pallas_call(
        body,
        in_specs=[ANY, ANY],
        out_specs=ANY,
        out_shape=jax.ShapeDtypeStruct(shape, first.dtype),
        scratch_shapes=[
            pltpu.VMEM(shape, first.dtype),
            pltpu.SemaphoreType.DMA((2 * ROW,)),
            pltpu.SemaphoreType.DMA((ROW,)),
        ],
    )(first, second)


def join_columns(parts, width):
    def body(src, out, held, sem_in, sem_out):
        reads = [
            pltpu.make_async_copy(src.at[i, :, :width], held.at[i], sem_in.at[i])
            for i in range(ROW)
        ]
        for copy in reads:
            copy.start()
        writes = []
        for i in range(ROW):
            reads[i].wait()
            columns = slice(i * width, (i + 1) * width)
            writes.append(pltpu.make_async_copy(held.at[i], out.at[:, columns], sem_out.at[i]))
            writes[-1].start()
        for copy in writes:
            copy.wait()

    return pl.pallas_call(
        body,
        in_specs=[ANY],
        out_specs=ANY,
        out_shape=jax.ShapeDtypeStruct((B, ROW * width), parts.dtype),
        scratch_shapes=[
            pltpu.VMEM((ROW, B, width), parts.dtype),
            pltpu.SemaphoreType.DMA((ROW,)),
            pltpu.SemaphoreType.DMA((ROW,)),
        ],
        compiler_params=SMALL,
    )(parts)


def with_key_grads(dq, own, tail):
    def body(_, own_ref, tail_ref, out):
        for b in range(ROW):
            for n in range(2 * KV_LOCAL):
                g, which = divmod(n, 2)
                total = own_ref[g, which, b * B : (b + 1) * B]
                if b >= ROW - TAIL:
                    start = (b - (ROW - TAIL)) * B
                    total = total + tail_ref[g, which, start : start + B].astype(F32)
                out[b, :, n * D : (n + 1) * D] = total.astype(BF16)

    return pl.pallas_call(
        body,
        grid=(1,),
        in_specs=[
            ANY,
            pl.BlockSpec(own.shape, lambda i: (0, 0, 0, 0)),
            pl.BlockSpec(tail.shape, lambda i: (0, 0, 0, 0)),
        ],
        out_specs=pl.BlockSpec((ROW, B, KV_COLUMNS), lambda i: (0, 0, Q_LOCAL * D // KV_COLUMNS)),
        out_shape=jax.ShapeDtypeStruct(dq.shape, dq.dtype),
        input_output_aliases={0: 0},
        compiler_params=SMALL,
    )(dq, own, tail)


def join_pair(parts, pieces):
    def body(src, *refs):
        extra = refs[:ROW]
        for i in range(ROW):
            for n in range(2 * KV_LOCAL):
                g, which = divmod(n, 2)
                out = refs[ROW + which]
                total = src[i, :, n * D : (n + 1) * D].astype(F32) + extra[i][g, which].astype(F32)
                h = i * KV_LOCAL + g
                out[:, h * D : (h + 1) * D] = total.astype(out.dtype)

    piece = pl.BlockSpec(pieces[0].shape, lambda i: (0, 0, 0, 0))
    width = KEY_VALUE_HEADS * D
    out = jax.ShapeDtypeStruct((B, width), parts.dtype)
    return pl.pallas_call(
        body,
        grid=(1,),
        in_specs=[
            pl.BlockSpec((ROW, B, KV_COLUMNS), lambda i: (0, 0, Q_LOCAL * D // KV_COLUMNS))
        ]
        + [piece] * ROW,
        out_specs=[pl.BlockSpec((B, width), lambda i: (0, 0))] * 2,
        out_shape=[out, out],
        compiler_params=SMALL,
    )(parts, *pieces)


def dot(a, b, ca, cb):
    return lax.dot_general(a, b, (((ca,), (cb,)), ((), ())), preferred_element_type=F32)


def attention_body(
    meta, q_ref, go_ref, k_ref, v_ref, tk_ref, tv_ref, sk_ref, sv_ref, ok_ref, ov_ref,
    dq_ref, own_ref, tail_ref, sink_ref, ks, vs, ssk, ssv, kst, sst, acc, sacc,
):
    g = pl.program_id(0)

    ks[: TAIL * B] = tk_ref[...].reshape(TAIL * B, D)
    ks[TAIL * B :] = k_ref[...].reshape(ROW * B, D)
    vs[: TAIL * B] = tv_ref[...].reshape(TAIL * B, D)
    vs[TAIL * B :] = v_ref[...].reshape(ROW * B, D)
    near = pl.ds(pl.multiple_of(meta[META_CORE] * B, B), B)
    far = pl.ds(pl.multiple_of((1 - meta[META_CORE]) * B, B), B)
    ssk[near, :] = sk_ref[...]
    ssv[near, :] = sv_ref[...]
    ssk[far, :] = ok_ref[...]
    ssv[far, :] = ov_ref[...]
    kst[...] = ks[...].T
    sst[...] = ssk[...].T
    acc[...] = jnp.zeros_like(acc)
    sacc[...] = jnp.zeros_like(sacc)

    ksink = ssk[...]
    vsink = ssv[...]
    ksinkt = sst[...]
    key = lax.broadcasted_iota(jnp.int32, (B, PAIR * B), 0)
    query = lax.broadcasted_iota(jnp.int32, (B, PAIR * B), 1) % B
    causal = key <= query

    def bias(allowed):
        return jnp.concatenate(
            [jnp.full((1, B), jnp.where(ok, 0.0, NEG_FILL), F32) for ok in allowed], 1
        )

    for n in range(ROW):
        block = meta[0] + n
        rows = slice(n * B, (n + WMAX) * B)
        kw = ks[rows, :]
        vw = vs[rows, :]
        kwt = kst[:, rows]
        pairs = [range(first, first + PAIR) for first in range(0, GROUP, PAIR)]
        first_products = []
        for heads in pairs:
            q2 = jnp.concatenate([q_ref[n, :, h * D : (h + 1) * D] for h in heads], 0)
            go2 = jnp.concatenate([go_ref[n, :, h * D : (h + 1) * D] for h in heads], 0)
            sw = dot(kw, q2, 1, 1)
            ss = dot(ksink, q2, 1, 1)
            pw = dot(vw, go2, 1, 1)
            ps = dot(vsink, go2, 1, 1)
            scores = [sw[j * B : (j + 1) * B] for j in range(WMAX)]
            scores[TAIL] = jnp.where(causal, scores[TAIL], NEG_FILL)
            scores += [ss[t * B : (t + 1) * B] for t in range(SMAX)]
            grads = [pw[j * B : (j + 1) * B] for j in range(WMAX)]
            grads += [ps[t * B : (t + 1) * B] for t in range(SMAX)]
            first_products.append((q2, go2, scores, grads))

        softmaxes = []
        for heads, (_, _, scores, grads) in zip(pairs, first_products):
            window = [meta[1 + g * GROUP + h] for h in heads]
            sink = [meta[1 + Q_LOCAL + g * GROUP + h] for h in heads]
            biases = [
                bias([(block >= TAIL - j) & (TAIL - j < w) for w in window]) for j in range(TAIL)
            ]
            biases += [jnp.zeros((1, PAIR * B), F32)]
            biases += [
                bias([(t < c) & (t <= block - w) for w, c in zip(window, sink)]) for t in range(SMAX)
            ]
            tops = [
                jnp.max(s, 0, keepdims=True) * EXP2_SCALE + extra for s, extra in zip(scores, biases)
            ]
            top = tops[0]
            for t in tops[1:]:
                top = jnp.maximum(top, t)
            exps = [jnp.exp2(s * EXP2_SCALE - (top - extra)) for s, extra in zip(scores, biases)]
            total = exps[0]
            product = exps[0] * grads[0]
            for e, p in zip(exps[1:], grads[1:]):
                total = total + e
                product = product + e * p
            inverse = 1.0 / jnp.sum(total, 0, keepdims=True)
            row_dot = jnp.sum(product, 0, keepdims=True) * inverse
            weights = [e * inverse for e in exps]
            rounded = [w.astype(BF16) for w in weights]
            dscores = [(w * (p - row_dot)).astype(BF16) for w, p in zip(weights, grads)]
            softmaxes.append(
                [
                    jnp.concatenate(rows, 0)
                    for rows in (rounded[:WMAX], rounded[WMAX:], dscores[:WMAX], dscores[WMAX:])
                ]
            )

        sums = []
        for heads, (q2, go2, _, _), (wb_window, wb_sink, ds_window, ds_sink) in zip(
            pairs, first_products, softmaxes
        ):
            sums.append(
                [
                    dot(ds_window, q2, 1, 0),
                    dot(wb_window, go2, 1, 0),
                    dot(ds_sink, q2, 1, 0),
                    dot(wb_sink, go2, 1, 0),
                ]
            )
            dqt = (dot(kwt, ds_window, 1, 0) + dot(ksinkt, ds_sink, 1, 0)) * SCALE
            for n2, h in enumerate(heads):
                dq_ref[n, :, h * D : (h + 1) * D] = dqt[:, n2 * B : (n2 + 1) * B].T.astype(BF16)
        acc[0, rows, :] += sums[0][0] + sums[1][0]
        acc[1, rows, :] += sums[0][1] + sums[1][1]
        sacc[0] += sums[0][2] + sums[1][2]
        sacc[1] += sums[0][3] + sums[1][3]

    own_ref[0, 0] = acc[0, TAIL * B :] * SCALE
    own_ref[0, 1] = acc[1, TAIL * B :]
    tail_ref[0, 0] = (acc[0, : TAIL * B] * SCALE).astype(BF16)
    tail_ref[0, 1] = acc[1, : TAIL * B].astype(BF16)
    for t in range(SMAX):
        sink_ref[t, 0, 0] = sacc[0, t * B : (t + 1) * B] * SCALE
        sink_ref[t, 0, 1] = sacc[1, t * B : (t + 1) * B]


def attention(meta, qgo, kv, tail, sink, other, interpret=False):
    wide = pl.BlockSpec((ROW, B, GROUP * D), lambda g, m: (0, 0, g))
    wide_go = pl.BlockSpec((ROW, B, GROUP * D), lambda g, m: (0, 0, KV_LOCAL + g))

    def pair(count):
        return [
            pl.BlockSpec((count, B, D), lambda g, m: (0, 0, g)),
            pl.BlockSpec((count, B, D), lambda g, m: (0, 0, KV_LOCAL + g)),
        ]

    one = [
        pl.BlockSpec((B, D), lambda g, m: (0, g)),
        pl.BlockSpec((B, D), lambda g, m: (0, KV_LOCAL + g)),
    ]

    def result(rows, dtype):
        return (
            pl.BlockSpec((1, 2, rows * B, D), lambda g, m: (g, 0, 0, 0)),
            jax.ShapeDtypeStruct((KV_LOCAL, 2, rows * B, D), dtype),
        )

    results = [
        (wide, jax.ShapeDtypeStruct((ROW, B, Q_LOCAL * D + KV_COLUMNS), BF16)),
        result(ROW, F32),
        result(TAIL, BF16),
        (
            pl.BlockSpec((SMAX, 1, 2, B, D), lambda g, m: (0, g, 0, 0, 0)),
            jax.ShapeDtypeStruct((SMAX, KV_LOCAL, 2, B, D), F32),
        ),
    ]
    return pl.pallas_call(
        attention_body,
        grid_spec=pltpu.PrefetchScalarGridSpec(
            num_scalar_prefetch=1,
            grid=(KV_LOCAL,),
            in_specs=[wide, wide_go] + pair(ROW) + pair(TAIL) + one + one,
            out_specs=[r[0] for r in results],
            scratch_shapes=[
                pltpu.VMEM(((TAIL + ROW) * B, D), BF16),
                pltpu.VMEM(((TAIL + ROW) * B, D), BF16),
                pltpu.VMEM((SMAX * B, D), BF16),
                pltpu.VMEM((SMAX * B, D), BF16),
                pltpu.VMEM((D, (TAIL + ROW) * B), BF16),
                pltpu.VMEM((D, SMAX * B), BF16),
                pltpu.VMEM((2, (TAIL + ROW) * B, D), F32),
                pltpu.VMEM((2, SMAX * B, D), F32),
            ],
        ),
        out_shape=[r[1] for r in results],
        compiler_params=pltpu.CompilerParams(vmem_limit_bytes=48 * MIB),
        interpret=interpret,
    )(meta, qgo, qgo, kv, kv, tail, tail, sink, sink, other, other)


def line(y, z, core):
    return ((z % 4 * 8 + y) * 2 + z // 4) * 2 + core


def at(x, core):
    return x * 32 + core


def moved(moves):
    return [(line(*p, 0), line(*q, 0)) for p, q in moves] + [
        (line(*p[::-1], 1), line(*q[::-1], 1)) for p, q in moves
    ]


ROUNDS = (((4, 0), (2, 0), (6, 0)), ((0, 4), (1, 4), (1, 0)), ((0, 2), (0, 1), (0, 7)))


def spread():
    holders = [(0, 0)]
    rounds = []
    for offsets in ROUNDS:
        moves = [
            [((a, b), ((a + da) % 8, (b + db) % 8)) for a, b in holders] for da, db in offsets
        ]
        rounds.append([moved(m) for m in moves])
        holders = holders + [q for m in moves for _, q in m]
    return rounds


def gather():
    def inner(end, step):
        return end + step if end == 0 else end - step

    ends = (0, 7)
    rounds = [
        [[((a, inner(b, n)), (a, b)) for a in range(8) for b in ends] for n in (1, 3, 2)],
        [[((inner(a, n), b), (a, b)) for a in ends for b in ends] for n in (3, 2, 1)],
        [[(corner, (0, 0))] for corner in ((7, 7), (7, 0), (0, 7))],
    ]
    return [[moved(moves) for moves in permutes] for permutes in rounds]


def exchanged(value, axes):
    return lax.all_to_all(value, axes, split_axis=0, concat_axis=0, tiled=False)


def summed(total, permutes):
    send = total.astype(BF16)
    for got in [lax.ppermute(send, LINE, pairs) for pairs in permutes]:
        total = total + got.astype(F32)
    return total


def after(value, *others):
    return lax.optimization_barrier((value, others))[0]


def shards(queries, keys, values, output_gradient, windows, sinks):
    core = lax.axis_index("core")
    run = lax.axis_index(("y", "zh", "core")) * 4 + lax.axis_index("zl")
    x = lax.axis_index("x")
    meta = jnp.concatenate(
        [
            (run * ROW)[None].astype(jnp.int32),
            lax.dynamic_slice_in_dim(windows, x * Q_LOCAL, Q_LOCAL),
            lax.dynamic_slice_in_dim(sinks, x * Q_LOCAL, Q_LOCAL),
            core[None].astype(jnp.int32),
        ]
    )
    runs = [(run // 4 // 4, run // 4 // 2 % 2 * 4 + run % 4, run // 4 % 2) for run in range(128)]
    to_next = [(line(*a), line(*b)) for a, b in zip(runs[:-1], runs[1:])]
    swap = [(0, 1), (1, 0)]

    kv_split = split_pair(keys[0], values[0])
    qgo_split = split_pair(after(queries[0], kv_split), output_gradient[0])
    kv = after(exchanged(kv_split, "x"), qgo_split)
    qgo = exchanged(qgo_split, "x")
    tail = lax.ppermute(kv[ROW - TAIL :], LINE, to_next)
    sink = lax.ppermute(kv[1], LINE, [(line(0, 0, 0), line(0, 0, 1))])
    sink = jnp.where(run == 0, kv[0], sink)
    for step, permutes in enumerate(spread()):
        if step == 2:
            sink = after(sink, tail)
        got = [lax.ppermute(sink, LINE, pairs) for pairs in permutes]
        sink = sink + got[0] + got[1] + got[2]
    other = lax.ppermute(sink, "core", swap)
    dq, own, tail_grad, sink_grad = attention(meta, qgo, kv, tail, sink, other)

    total = lax.dynamic_index_in_dim(sink_grad, core, 0, False)
    away = lax.dynamic_index_in_dim(sink_grad, 1 - core, 0, False).astype(BF16)
    total = total + lax.ppermute(away, "core", swap).astype(F32)
    rounds = gather()
    send = total.astype(BF16)
    got = [lax.ppermute(send, LINE, pairs) for pairs in rounds[0]]
    tail_back = lax.ppermute(after(tail_grad, got[0]), LINE, [(b, a) for a, b in to_next])
    for piece in got:
        total = total + piece.astype(F32)
    total = summed(total, rounds[1])
    grads = with_key_grads(dq, own, after(tail_back, total))
    parts = exchanged(grads, "x")
    dq_tokens = join_columns(parts, Q_LOCAL * D)
    total = summed(after(total, grads), rounds[2])
    total = total.astype(BF16)

    pieces = [
        lax.ppermute(total, AXES, [(at(j, c), at(c, 0)) for c in range(SMAX)]) for j in range(ROW)
    ]
    dk, dv = join_pair(parts, pieces)
    return dq_tokens[None], dk[None], dv[None]


def solution(mesh):
    split = Mesh(mesh.devices.reshape(SIZES), AXES)
    tokens = P(("y", "zh", "core"), ("zl", "x"), None)
    return jax.shard_map(
        shards,
        mesh=split,
        in_specs=(tokens, tokens, tokens, tokens, P(), P()),
        out_specs=(tokens, tokens, tokens),
        check_vma=False,
    )
```
